32 devices in a mesh: ctx: 4 (over y, core), fsdp: 8 (over z, x).
Axes of the slice: x: 2, y: 2, z: 4, core: 2. Of those that a mesh axis runs over, the one named last changes fastest.
Arguments:
- tokens: bfloat16 [8, 2048, 1024], P('fsdp', 'ctx'), may hold values from -6 to 6
- memory: bfloat16 [8, 2048, 1024], P('fsdp', 'ctx'), may hold values from -6 to 6
- cotangent: bfloat16 [8, 2048, 1024], P('fsdp', 'ctx'), may hold values from -6 to 6
- block_map: int32 [8, 8, 8], P('fsdp'), may hold values from 0 to 1, as said below
- block_order: int32 [8, 4], P('fsdp'), may hold values from 0 to 3, each once within a row
- self_projection: bfloat16 [1024, 3072], P('fsdp'), may hold values from -0.1875 to 0.1875
- self_output: bfloat16 [1024, 1024], P('fsdp'), may hold values from -0.375 to 0.375
- self_query_bias: bfloat16 [1024], P('fsdp'), may hold values from -2.5 to 2.5
- self_value_bias: bfloat16 [1024], P('fsdp'), may hold values from -2.5 to 2.5
- self_output_bias: bfloat16 [1024], P('fsdp'), may hold values from -2.5 to 2.5
- first_gain: bfloat16 [1024], P('fsdp'), may hold values from 0.5 to 1.5
- first_shift: bfloat16 [1024], P('fsdp'), may hold values from -2.5 to 2.5
- cross_query: bfloat16 [1024, 1024], P('fsdp'), may hold values from -0.1875 to 0.1875
- cross_memory: bfloat16 [1024, 2048], P('fsdp'), may hold values from -0.1875 to 0.1875
- cross_output: bfloat16 [1024, 1024], P('fsdp'), may hold values from -0.375 to 0.375
- cross_query_bias: bfloat16 [1024], P('fsdp'), may hold values from -2.5 to 2.5
- cross_value_bias: bfloat16 [1024], P('fsdp'), may hold values from -2.5 to 2.5
- cross_output_bias: bfloat16 [1024], P('fsdp'), may hold values from -2.5 to 2.5
- second_gain: bfloat16 [1024], P('fsdp'), may hold values from 0.5 to 1.5
- second_shift: bfloat16 [1024], P('fsdp'), may hold values from -2.5 to 2.5
- expand_weight: bfloat16 [1024, 4096], P('fsdp'), may hold values from -0.1875 to 0.1875
- reduce_weight: bfloat16 [4096, 1024], P('fsdp'), may hold values from -0.09375 to 0.09375
- expand_bias: bfloat16 [4096], P('fsdp'), may hold values from -2.5 to 2.5
- reduce_bias: bfloat16 [1024], P('fsdp'), may hold values from -2.5 to 2.5
- third_gain: bfloat16 [1024], P('fsdp'), may hold values from 0.5 to 1.5
- third_shift: bfloat16 [1024], P('fsdp'), may hold values from -2.5 to 2.5
Outputs:
- output: bfloat16 [8, 2048, 1024], P('fsdp', 'ctx')
- token_grad: float32 [8, 2048, 1024], P('fsdp', 'ctx')
- memory_grad: float32 [8, 2048, 1024], P('fsdp', 'ctx')
- grad_self_projection: float32 [1024, 3072], P('fsdp')
- grad_self_output: float32 [1024, 1024], P('fsdp')
- grad_self_query_bias: float32 [1024], P('fsdp')
- grad_self_value_bias: float32 [1024], P('fsdp')
- grad_self_output_bias: float32 [1024], P('fsdp')
- grad_first_gain: float32 [1024], P('fsdp')
- grad_first_shift: float32 [1024], P('fsdp')
- grad_cross_query: float32 [1024, 1024], P('fsdp')
- grad_cross_memory: float32 [1024, 2048], P('fsdp')
- grad_cross_output: float32 [1024, 1024], P('fsdp')
- grad_cross_query_bias: float32 [1024], P('fsdp')
- grad_cross_value_bias: float32 [1024], P('fsdp')
- grad_cross_output_bias: float32 [1024], P('fsdp')
- grad_second_gain: float32 [1024], P('fsdp')
- grad_second_shift: float32 [1024], P('fsdp')
- grad_expand_weight: float32 [1024, 4096], P('fsdp')
- grad_reduce_weight: float32 [4096, 1024], P('fsdp')
- grad_expand_bias: float32 [4096], P('fsdp')
- grad_reduce_bias: float32 [1024], P('fsdp')
- grad_third_gain: float32 [1024], P('fsdp')
- grad_third_shift: float32 [1024], P('fsdp')
The draws below stay inside these ranges and needn't reach their ends.
Inputs may be any that keep to these rules, and one draw needn't show every extreme that they name: block_map[s, i, j] is 1 exactly when j <= i and j is not before the first block of the document holding block i; each sequence holds one or two documents of whole blocks, so every block sees itself. Each row lists every group number once: index c of ctx holds group block_order[s, c] of sequence s, of 512 tokens.
All inputs are finite; a program needn't handle non-finite values.
Results may differ from the reference program's by a relative error of at most 0.022.
Values may be sent and summed in bfloat16 or wider, within the bound.
No kernel may reach another device: no remote copies, remote signals or barrier semaphores. Data moves between devices by JAX's collectives and lax.ppermute only.
A program may use at most 320 MiB of HBM per device.

```python
import math
import jax
import jax.numpy as jnp
from jax import lax

D = 1024
HEADS = 16
HEAD_DIM = 64
FF = 4096
BLK = 256
SEQ_LEN = 2048
MEM_LEN = 2048
SEQS = 8
TOK_DEV = 512
N_CTX = 4


def draw_block_map(key, part):
    count = SEQ_LEN // BLK
    boundary = jax.random.randint(key, (SEQS, 1, 1), 0, count, dtype=jnp.int32)
    row_index = lax.broadcasted_iota(jnp.int32, (SEQS, count, count), 1)
    column_index = lax.broadcasted_iota(jnp.int32, (SEQS, count, count), 2)
    start = jnp.where(row_index >= boundary, boundary, 0)
    return ((column_index <= row_index) & (column_index >= start)).astype(jnp.int32)


def level_of(key, shape, pieces, least, largest):
    def one(axis_at, shards_of):
        heights = jax.random.uniform(jax.random.fold_in(jax.random.fold_in(key, 6), axis_at), (shards_of,), jnp.float32, least / len(pieces), largest / len(pieces))
        return jnp.repeat(jnp.exp(heights), shape[axis_at] // shards_of).reshape((-1,) + (1,) * (len(shape) - axis_at - 1))

    factor_of = one(*pieces[0])
    for cut in pieces[1:]:
        factor_of = factor_of * one(*cut)
    return factor_of


def normal_values(own_key, shape, scale, limit, shards=(), held_as=jnp.bfloat16):
    drawn = scale * jax.random.normal(own_key, shape, jnp.float32)
    if shards:
        drawn = drawn * level_of(own_key, shape, shards, -0.22, 0.18)
    return jnp.clip(drawn, -limit, limit).astype(held_as)


def setup_inputs(seed: int = 0) -> dict:
    seeds = jax.random.split(jax.random.key(seed), 27)
    tokens = normal_values(seeds[0], (SEQS, SEQ_LEN, D), 1.0, 6.0, ((0, 8), (1, 4)))
    memory = normal_values(seeds[1], (SEQS, MEM_LEN, D), 1.0, 6.0, ((0, 8), (1, 4)))
    cotangent = normal_values(seeds[2], (SEQS, SEQ_LEN, D), 1.0, 6.0, ((0, 8), (1, 4)))
    block_map = draw_block_map(jax.random.fold_in(seeds[26], 71), 0)
    block_order = jax.vmap(lambda own: jax.random.permutation(own, N_CTX))(jax.random.split(seeds[4], SEQS)).reshape((SEQS, N_CTX)).astype(jnp.int32)
    self_projection = normal_values(seeds[5], (D, 3 * D), D ** -0.5, 0.1875, ((0, 8),))
    self_output = normal_values(seeds[6], (D, D), (D // 4) ** -0.5, 0.375, ((0, 8),))
    self_query_bias = normal_values(seeds[7], (D,), 0.3, 2.5, ((0, 8),))
    self_value_bias = normal_values(seeds[8], (D,), 0.3, 2.5, ((0, 8),))
    self_output_bias = normal_values(seeds[9], (D,), 0.3, 2.5, ((0, 8),))
    first_gain = jnp.clip(1.0 + 0.1 * jax.random.normal(seeds[10], (D,), jnp.float32), 0.5, 1.5).astype(jnp.bfloat16)
    first_shift = normal_values(seeds[11], (D,), 0.3, 2.5, ((0, 8),))
    cross_query = normal_values(seeds[12], (D, D), D ** -0.5, 0.1875, ((0, 8),))
    cross_memory = normal_values(seeds[13], (D, 2 * D), D ** -0.5, 0.1875, ((0, 8),))
    cross_output = normal_values(seeds[14], (D, D), (D // 4) ** -0.5, 0.375, ((0, 8),))
    cross_query_bias = normal_values(seeds[15], (D,), 0.3, 2.5, ((0, 8),))
    cross_value_bias = normal_values(seeds[16], (D,), 0.3, 2.5, ((0, 8),))
    cross_output_bias = normal_values(seeds[17], (D,), 0.3, 2.5, ((0, 8),))
    second_gain = jnp.clip(1.0 + 0.1 * jax.random.normal(seeds[18], (D,), jnp.float32), 0.5, 1.5).astype(jnp.bfloat16)
    second_shift = normal_values(seeds[19], (D,), 0.3, 2.5, ((0, 8),))
    expand_weight = normal_values(seeds[20], (D, FF), D ** -0.5, 0.1875, ((0, 8),))
    reduce_weight = normal_values(seeds[21], (FF, D), FF ** -0.5, 0.09375, ((0, 8),))
    expand_bias = normal_values(seeds[22], (FF,), 0.3, 2.5, ((0, 8),))
    reduce_bias = normal_values(seeds[23], (D,), 0.3, 2.5, ((0, 8),))
    third_gain = jnp.clip(1.0 + 0.1 * jax.random.normal(seeds[24], (D,), jnp.float32), 0.5, 1.5).astype(jnp.bfloat16)
    third_shift = normal_values(seeds[25], (D,), 0.3, 2.5, ((0, 8),))
    return {"tokens": tokens, "memory": memory, "cotangent": cotangent, "block_map": block_map, "block_order": block_order, "self_projection": self_projection, "self_output": self_output, "self_query_bias": self_query_bias, "self_value_bias": self_value_bias, "self_output_bias": self_output_bias, "first_gain": first_gain, "first_shift": first_shift, "cross_query": cross_query, "cross_memory": cross_memory, "cross_output": cross_output, "cross_query_bias": cross_query_bias, "cross_value_bias": cross_value_bias, "cross_output_bias": cross_output_bias, "second_gain": second_gain, "second_shift": second_shift, "expand_weight": expand_weight, "reduce_weight": reduce_weight, "expand_bias": expand_bias, "reduce_bias": reduce_bias, "third_gain": third_gain, "third_shift": third_shift}


epsilon = 1e-05
residual_scale = 18.0 ** 0.25
score_scale = 0.125
masked_score = -1e+30
highest = lax.Precision.HIGHEST
gelu_coeff = math.sqrt(2.0 / math.pi)

@jax.custom_vjp
def low(v):
    return lax.optimization_barrier(v.astype(jnp.bfloat16)).astype(jnp.float32)

@jax.custom_vjp
def low_back(v):
    return v

def low_keep(v):
    return (low(v), None)

def low_pass(kept, grad):
    return (grad,)

def back_keep(v):
    return (v, None)

def back_low(kept, grad):
    return (low(grad),)
low.defvjp(low_keep, low_pass)
low_back.defvjp(back_keep, back_low)

def rounded(value):
    return low_back(low(value))

def matmul(left, right):
    return jnp.dot(left, right, precision=highest)

def gelu_tanh(value):
    return 0.5 * value * (1.0 + jnp.tanh(gelu_coeff * (value + 0.044715 * value * value * value)))

def layer_norm(summed, gain, shift):
    centred = summed - lax.optimization_barrier(jnp.mean(summed, axis=-1, keepdims=True))
    inverse = lax.rsqrt(lax.optimization_barrier(jnp.mean(centred * centred, axis=-1, keepdims=True)) + epsilon)
    return centred * inverse * gain + shift

def attend(queries, keys, values, visible):
    length = queries.shape[0]
    rows = min(512, length)
    count = length // rows
    query_blocks = queries.reshape(count, rows, HEADS, HEAD_DIM)
    key_heads = keys.reshape(keys.shape[0], HEADS, HEAD_DIM)
    value_heads = values.reshape(values.shape[0], HEADS, HEAD_DIM)

    def block_scores(query_block):
        scores = jnp.einsum('qhd,khd->hqk', query_block, key_heads, precision=highest) * score_scale
        return low_back(scores)

    def finish(scores):
        top = lax.optimization_barrier(jnp.max(scores, axis=-1, keepdims=True))
        weights = jnp.exp(scores - top)
        probs = weights / lax.optimization_barrier(jnp.sum(weights, axis=-1, keepdims=True))
        return jnp.einsum('hqk,khd->qhd', low(probs), value_heads, precision=highest)
    if visible is None:

        def plain_block(query_block):
            return finish(block_scores(query_block))
        result = lax.map(jax.checkpoint(plain_block), query_blocks)
    else:

        def masked_block(inputs):
            query_block, mask_block = inputs
            scores = jnp.where(mask_block[None], block_scores(query_block), masked_score)
            return finish(scores)
        result = lax.map(jax.checkpoint(masked_block), (query_blocks, visible.reshape(count, rows, -1)))
    return result.reshape(length, HEADS * HEAD_DIM)

def layer(parameters, token_rows, memory_rows, visible):
    self_projection, self_output, self_query_bias, self_value_bias, self_output_bias, first_gain, first_shift, cross_query, cross_memory, cross_output, cross_query_bias, cross_value_bias, cross_output_bias, second_gain, second_shift, expand_weight, reduce_weight, expand_bias, reduce_bias, third_gain, third_shift = parameters
    width = token_rows.shape[1]
    projected = matmul(token_rows, self_projection)
    queries = rounded(projected[:, :width] + self_query_bias)
    keys = rounded(projected[:, width:2 * width])
    values = rounded(projected[:, 2 * width:] + self_value_bias)
    attended = rounded(attend(queries, keys, values, visible))
    branch = low_back(matmul(attended, self_output) + self_output_bias)
    hidden_one = layer_norm(residual_scale * token_rows + branch, first_gain, first_shift)
    cross_queries = rounded(matmul(low(hidden_one), cross_query) + cross_query_bias)
    memory_proj = matmul(memory_rows, cross_memory)
    memory_keys = rounded(memory_proj[:, :width])
    memory_values = rounded(memory_proj[:, width:] + cross_value_bias)
    cross_attended = rounded(attend(cross_queries, memory_keys, memory_values, None))
    cross_branch = low_back(matmul(cross_attended, cross_output) + cross_output_bias)
    hidden_two = layer_norm(residual_scale * hidden_one + cross_branch, second_gain, second_shift)
    expanded = low_back(matmul(low(hidden_two), expand_weight) + expand_bias)
    activated = low(gelu_tanh(expanded))
    reduced = low_back(matmul(activated, reduce_weight) + reduce_bias)
    return layer_norm(residual_scale * hidden_two + reduced, third_gain, third_shift)

def token_blocks(order):
    positions = jnp.arange(SEQ_LEN, dtype=jnp.int32)
    group_index = positions // TOK_DEV
    return ((order[group_index] * TOK_DEV + positions % TOK_DEV) // BLK).astype(jnp.int32)

def reference(tokens, memory, cotangent, block_map, block_order, self_projection, self_output, self_query_bias, self_value_bias, self_output_bias, first_gain, first_shift, cross_query, cross_memory, cross_output, cross_query_bias, cross_value_bias, cross_output_bias, second_gain, second_shift, expand_weight, reduce_weight, expand_bias, reduce_bias, third_gain, third_shift):
    parameters = tuple((weight.astype(jnp.float32) for weight in (self_projection, self_output, self_query_bias, self_value_bias, self_output_bias, first_gain, first_shift, cross_query, cross_memory, cross_output, cross_query_bias, cross_value_bias, cross_output_bias, second_gain, second_shift, expand_weight, reduce_weight, expand_bias, reduce_bias, third_gain, third_shift)))

    def one_sequence(totals, inputs):
        seq_tokens, seq_memory, seq_cotangent, seq_map, seq_order = inputs
        blocks = token_blocks(seq_order)
        visible = seq_map[blocks[:, None], blocks[None, :]] > 0

        def forward(parameter_set, token_rows, memory_rows):
            return layer(parameter_set, token_rows, memory_rows, visible)
        result, pullback = jax.vjp(forward, parameters, seq_tokens.astype(jnp.float32), seq_memory.astype(jnp.float32))
        grad_parameters, grad_tokens, grad_memory = pullback(seq_cotangent.astype(jnp.float32))
        totals = jax.tree.map(lambda first, second: first + second, totals, grad_parameters)
        return (totals, (result.astype(jnp.bfloat16), grad_tokens, grad_memory))
    zeros = tuple((jnp.zeros(weight.shape, jnp.float32) for weight in parameters))
    totals, (outputs, token_grads, memory_grads) = lax.scan(one_sequence, zeros, (tokens, memory, cotangent, block_map, block_order))
    return (outputs, token_grads, memory_grads, totals[0], totals[1], totals[2], totals[3], totals[4], totals[5], totals[6], totals[7], totals[8], totals[9], totals[10], totals[11], totals[12], totals[13], totals[14], totals[15], totals[16], totals[17], totals[18], totals[19], totals[20])
```

```python
import functools
import math

import jax
import jax.numpy as jnp
from jax import lax
from jax.experimental import pallas as pl
from jax.experimental.pallas import tpu as pltpu
from jax.sharding import PartitionSpec as P

HEADS = 16
HEAD_DIM = 64
BLK = 256


epsilon = 1e-05
residual_scale = 18.0**0.25
score_scale = 0.125
masked_score = -1e30
gelu_coeff = math.sqrt(2.0 / math.pi)


def gelu_tanh(value):
    return 0.5 * value * (1.0 + jnp.tanh(gelu_coeff * (value + 0.044715 * value * value * value)))


def gelu_slope(value):
    inner = jnp.tanh(gelu_coeff * (value + 0.044715 * value * value * value))
    return 0.5 * (1.0 + inner) + 0.5 * value * (1.0 - inner * inner) * gelu_coeff * (
        1.0 + 3.0 * 0.044715 * value * value
    )


def layer_norm(summed, gain, shift):
    centred = summed - jnp.mean(summed, axis=-1, keepdims=True)
    inverse = lax.rsqrt(jnp.mean(centred * centred, axis=-1, keepdims=True) + epsilon)
    normed = centred * inverse
    return (normed * gain + shift, normed, inverse)


def layer_norm_back(upstream, gain, normed, inverse):
    scaled = upstream * gain
    inner = (
        scaled
        - jnp.mean(scaled, axis=-1, keepdims=True)
        - normed * jnp.mean(scaled * normed, axis=-1, keepdims=True)
    )
    return (inner * inverse, jnp.sum(upstream * normed, axis=0), jnp.sum(upstream, axis=0))


score_log2 = 0.125 * math.log2(math.e)
NT = (((1,), (1,)), ((), ()))
NN = (((1,), (0,)), ((), ()))
TN = (((0,), (0,)), ((), ()))


def mxu(left, right, dims):
    return lax.dot_general(left, right, dims, preferred_element_type=jnp.float32)


def two_heads(pair):
    low = lax.broadcasted_iota(jnp.int32, pair.shape, 1) < 64
    zero = jnp.zeros_like(pair)
    return jnp.concatenate([jnp.where(low, pair, zero), jnp.where(low, zero, pair)], axis=0)


def one_pair(stacked):
    rows = stacked.shape[0] // 2
    top = stacked[:rows]
    low = lax.broadcasted_iota(jnp.int32, top.shape, 1) < 64
    return jnp.where(low, top, stacked[rows:])


def place_of(order_ref, slot_ref, index, per_group):
    return order_ref[slot_ref[0] ^ (index // per_group)] * per_group + index % per_group


def seen(scalars, query_index, key_index, per_group, count):
    if scalars is None:
        return None
    order_ref, map_ref, slot_ref = scalars
    row = place_of(order_ref, slot_ref, query_index, per_group)
    column = place_of(order_ref, slot_ref, key_index, per_group)
    return map_ref[row * count + column] > 0


def guarded(flag, work):
    if flag is None:
        work()
    else:
        pl.when(flag)(work)


def pair_lanes(unit):
    return slice(unit * 128, (unit + 1) * 128)


def forward_body(masked, units, chunks, key_rows, pieces, per_group, *refs):
    scalars = None
    if masked:
        scalars, refs = refs[:3], refs[3:]
    q_ref, refs = refs[0], refs[1:]
    k_refs, v_refs, refs = refs[:pieces], refs[pieces:2 * pieces], refs[2 * pieces:]
    o_ref, lse_ref, stacked, scores, top, shift, total, acc = refs
    rows = stacked.shape[1]
    query_index = pl.program_id(1)

    def part(ref_list, chunk, unit):
        if pieces > 1:
            return ref_list[chunk][:, pair_lanes(unit)]
        return ref_list[0][chunk * key_rows:(chunk + 1) * key_rows, pair_lanes(unit)]

    for unit in range(units):
        stacked[unit] = two_heads(q_ref[:, pair_lanes(unit)])
        top[unit] = jnp.full((rows, 128), -1e30, jnp.float32)
        total[unit] = jnp.zeros((rows, 128), jnp.float32)
        acc[unit] = jnp.zeros((rows, 128), jnp.float32)
    for chunk in range(chunks):
        flag = seen(scalars, query_index, chunk, per_group, chunks)

        def scan_max(chunk=chunk):
            for unit in range(units):
                found = mxu(stacked[unit], part(k_refs, chunk, unit), NT)
                scores[unit, chunk] = found
                best = top[unit]
                for lane in range(0, key_rows, 128):
                    best = jnp.maximum(best, found[:, lane:lane + 128])
                top[unit] = best

        guarded(flag, scan_max)
    for unit in range(units):
        peak = jnp.max(top[unit], axis=1, keepdims=True) * score_log2
        shift[unit] = jnp.broadcast_to(peak, (rows, 128))
    for chunk in range(chunks):
        flag = seen(scalars, query_index, chunk, per_group, chunks)

        def weigh(chunk=chunk):
            for unit in range(units):
                found = scores[unit, chunk]
                offset = shift[unit]
                summed = total[unit]
                parts = []
                for lane in range(0, key_rows, 128):
                    weight = jnp.exp2(found[:, lane:lane + 128] * score_log2 - offset)
                    summed = summed + weight
                    parts.append(weight.astype(jnp.bfloat16))
                total[unit] = summed
                acc[unit] = acc[unit] + mxu(jnp.concatenate(parts, axis=1), part(v_refs, chunk, unit), NN)

        guarded(flag, weigh)
    for unit in range(units):
        row_sum = jnp.sum(total[unit], axis=1, keepdims=True)
        o_ref[:, pair_lanes(unit)] = one_pair(acc[unit] / row_sum).astype(o_ref.dtype)
        lse = shift[unit] + jnp.log2(row_sum)
        lse_ref[unit] = lse.T[:8]


def backward_body(masked, units, chunks, key_rows, pieces, per_group, *refs):
    scalars = None
    if masked:
        scalars, refs = refs[:3], refs[3:]
    q_ref, do_ref, o_ref, lse_ref, refs = refs[0], refs[1], refs[2], refs[3], refs[4:]
    k_refs, v_refs, refs = refs[:pieces], refs[pieces:2 * pieces], refs[2 * pieces:]
    dq_ref, dk_refs, dv_refs, refs = refs[0], refs[1:1 + pieces], refs[1 + pieces:1 + 2 * pieces], refs[1 + 2 * pieces:]
    stacked, grads, delta, dq_acc, dk_acc, dv_acc = refs
    query_index = pl.program_id(1)

    def part(ref_list, chunk, unit):
        if pieces > 1:
            return ref_list[chunk][:, pair_lanes(unit)]
        return ref_list[0][chunk * key_rows:(chunk + 1) * key_rows, pair_lanes(unit)]

    @pl.when(query_index == 0)
    def clear():
        dk_acc[...] = jnp.zeros_like(dk_acc)
        dv_acc[...] = jnp.zeros_like(dv_acc)

    for unit in range(units):
        lanes = pair_lanes(unit)
        stacked[unit] = two_heads(q_ref[:, lanes])
        upstream = do_ref[:, lanes]
        grads[unit] = two_heads(upstream)
        product = (upstream.astype(jnp.float32) * o_ref[:, lanes].astype(jnp.float32)).T
        first = jnp.sum(product[:64], axis=0, keepdims=True)
        second = jnp.sum(product[64:], axis=0, keepdims=True)
        delta[unit] = jnp.broadcast_to(jnp.concatenate([first, second], axis=1), delta.shape[1:])
        dq_acc[unit] = jnp.zeros(dq_acc.shape[1:], jnp.float32)
    for chunk in range(chunks):
        flag = seen(scalars, query_index, chunk, per_group, chunks)

        def step(chunk=chunk):
            for unit in range(units):
                queries, upstream = stacked[unit], grads[unit]
                keys, values = part(k_refs, chunk, unit), part(v_refs, chunk, unit)
                found = mxu(keys, queries, NT)
                probs = jnp.exp2(found * score_log2 - lse_ref[unit, 0:1])
                grad_probs = mxu(values, upstream, NT)
                grad_scores = (probs * (grad_probs - delta[unit, 0:1])).astype(jnp.bfloat16)
                dv_acc[unit, chunk] += mxu(probs.astype(jnp.bfloat16), upstream, NN)
                dk_acc[unit, chunk] += mxu(grad_scores, queries, NN)
                dq_acc[unit] += mxu(grad_scores, keys, TN)

        guarded(flag, step)
    for unit in range(units):
        dq_ref[:, pair_lanes(unit)] = (one_pair(dq_acc[unit]) * 0.125).astype(dq_ref.dtype)

    @pl.when(query_index == pl.num_programs(1) - 1)
    def finish():
        for unit in range(units):
            for chunk in range(chunks):
                if pieces > 1:
                    rows = slice(None)
                    dk_ref, dv_ref = dk_refs[chunk], dv_refs[chunk]
                else:
                    rows = slice(chunk * key_rows, (chunk + 1) * key_rows)
                    dk_ref, dv_ref = dk_refs[0], dv_refs[0]
                dk_ref[rows, pair_lanes(unit)] = (dk_acc[unit, chunk] * 0.125).astype(dk_ref.dtype)
                dv_ref[rows, pair_lanes(unit)] = dv_acc[unit, chunk].astype(dv_ref.dtype)


def attention_forward(q, q_col, k_list, k_col, v_list, v_col, width, scalars, key_rows, units=2, per_group=2):
    pieces = len(k_list)
    lanes = units * 128
    rows = q.shape[0]
    keys = sum(k.shape[0] for k in k_list)
    chunks = keys // key_rows
    groups, blocks = width // lanes, rows // BLK
    masked = scalars is not None
    spec_q = pl.BlockSpec((BLK, lanes), lambda h, i, *_: (i, q_col + h))
    specs_k = [pl.BlockSpec((k.shape[0], lanes), lambda h, i, *_: (0, k_col + h)) for k in k_list]
    specs_v = [pl.BlockSpec((v.shape[0], lanes), lambda h, i, *_: (0, v_col + h)) for v in v_list]
    body = functools.partial(forward_body, masked, units, chunks, key_rows, pieces, per_group)
    pairs = rows * keys * (width // 64)
    return pl.pallas_call(
        body,
        grid_spec=pltpu.PrefetchScalarGridSpec(
            num_scalar_prefetch=3 if masked else 0,
            grid=(groups, blocks),
            in_specs=[spec_q] + specs_k + specs_v,
            out_specs=[
                pl.BlockSpec((BLK, lanes), lambda h, i, *_: (i, h)),
                pl.BlockSpec((units, 8, 2 * BLK), lambda h, i, *_: (h, 0, i)),
            ],
            scratch_shapes=[
                pltpu.VMEM((units, 2 * BLK, 128), jnp.bfloat16),
                pltpu.VMEM((units, chunks, 2 * BLK, key_rows), jnp.float32),
                pltpu.VMEM((units, 2 * BLK, 128), jnp.float32),
                pltpu.VMEM((units, 2 * BLK, 128), jnp.float32),
                pltpu.VMEM((units, 2 * BLK, 128), jnp.float32),
                pltpu.VMEM((units, 2 * BLK, 128), jnp.float32),
            ],
        ),
        out_shape=[
            jax.ShapeDtypeStruct((rows, width), jnp.bfloat16),
            jax.ShapeDtypeStruct((width // 128, 8, blocks * 2 * BLK), jnp.float32),
        ],
        compiler_params=pltpu.CompilerParams(vmem_limit_bytes=48 << 20),
        cost_estimate=pl.CostEstimate(flops=pairs * 512, transcendentals=pairs, bytes_accessed=4 * (rows + keys) * width),
    )(*(scalars or ()), q, *k_list, *v_list)


def attention_backward(q, q_col, do, o, lse, k_list, k_col, v_list, v_col, width, scalars, key_rows, units=2, per_group=2):
    pieces = len(k_list)
    lanes = units * 128
    rows = q.shape[0]
    keys = sum(k.shape[0] for k in k_list)
    chunks = keys // key_rows
    groups, blocks = width // lanes, rows // BLK
    masked = scalars is not None
    spec_q = pl.BlockSpec((BLK, lanes), lambda h, i, *_: (i, q_col + h))
    spec_o = pl.BlockSpec((BLK, lanes), lambda h, i, *_: (i, h))
    spec_lse = pl.BlockSpec((units, 8, 2 * BLK), lambda h, i, *_: (h, 0, i))
    specs_k = [pl.BlockSpec((k.shape[0], lanes), lambda h, i, *_: (0, k_col + h)) for k in k_list]
    specs_v = [pl.BlockSpec((v.shape[0], lanes), lambda h, i, *_: (0, v_col + h)) for v in v_list]
    outs_k = [pl.BlockSpec((k.shape[0], lanes), lambda h, i, *_: (0, h)) for k in k_list]
    body = functools.partial(backward_body, masked, units, chunks, key_rows, pieces, per_group)
    pairs = rows * keys * (width // 64)
    shape_k = [jax.ShapeDtypeStruct((k.shape[0], width), jnp.bfloat16) for k in k_list]
    return pl.pallas_call(
        body,
        grid_spec=pltpu.PrefetchScalarGridSpec(
            num_scalar_prefetch=3 if masked else 0,
            grid=(groups, blocks),
            in_specs=[spec_q, spec_o, spec_o, spec_lse] + specs_k + specs_v,
            out_specs=[spec_o] + outs_k + outs_k,
            scratch_shapes=[
                pltpu.VMEM((units, 2 * BLK, 128), jnp.bfloat16),
                pltpu.VMEM((units, 2 * BLK, 128), jnp.bfloat16),
                pltpu.VMEM((units, 8, 2 * BLK), jnp.float32),
                pltpu.VMEM((units, 2 * BLK, 128), jnp.float32),
                pltpu.VMEM((units, chunks, key_rows, 128), jnp.float32),
                pltpu.VMEM((units, chunks, key_rows, 128), jnp.float32),
            ],
        ),
        out_shape=[jax.ShapeDtypeStruct((rows, width), jnp.bfloat16)] + shape_k + shape_k,
        compiler_params=pltpu.CompilerParams(vmem_limit_bytes=48 << 20),
        cost_estimate=pl.CostEstimate(flops=pairs * 1280, transcendentals=pairs, bytes_accessed=8 * (rows + keys) * width),
    )(*(scalars or ()), q, do, o, lse, *k_list, *v_list)


def core_perm():
    return [(c, c ^ 1) for c in range(4)]


def y_perm():
    return [(c, c ^ 2) for c in range(4)]


def diagonal_perm():
    return [(c, c ^ 3) for c in range(4)]


def x_perm():
    return [(f, f ^ 1) for f in range(8)]


def z_perm(k):
    return [(f, f ^ (2 * k)) for f in range(8)]


def to_core(v):
    return lax.ppermute(v, "ctx", core_perm())


def to_y(v):
    return lax.ppermute(v, "ctx", y_perm())


def to_diagonal(v):
    return lax.ppermute(v, "ctx", diagonal_perm())


def to_x(v):
    return lax.ppermute(v, "fsdp", x_perm())


def to_z(v, k):
    return lax.ppermute(v, "fsdp", z_perm(k))


def fsdp_pieces(own):
    along = [own] + [to_z(own, k) for k in (1, 2, 3)]
    return along + [to_x(piece) for piece in along]


def fsdp_sources(me):
    return [me ^ (2 * k + d) for d in (0, 1) for k in range(4)]


def place_body(count, stacks, rows, *refs):
    offsets, refs = refs[0], refs[1:]
    pieces, outs, sems = refs[:count], refs[count:count + stacks], refs[-1]
    copies = []
    for i in range(count):
        start = pl.multiple_of(offsets[i], rows)
        for s in range(stacks):
            source = pieces[i].at[s] if len(pieces[i].shape) == 3 else pieces[i]
            copy = pltpu.make_async_copy(source, outs[s].at[pl.ds(start, rows)], sems.at[i, s])
            copy.start()
            copies.append(copy)
    for copy in copies:
        copy.wait()


def place(pieces, offsets):
    shape = pieces[0].shape
    stacks = shape[0] if len(shape) == 3 else 1
    rows, columns = shape[-2:]
    count = len(pieces)
    out = [jax.ShapeDtypeStruct((count * rows, columns), pieces[0].dtype)] * stacks
    anywhere = pl.BlockSpec(memory_space=pl.ANY)
    return pl.pallas_call(
        functools.partial(place_body, count, stacks, rows),
        in_specs=[pl.BlockSpec(memory_space=pltpu.SMEM)] + [anywhere] * count,
        out_specs=[anywhere] * stacks,
        out_shape=out,
        scratch_shapes=[pltpu.SemaphoreType.DMA((count, stacks))],
        cost_estimate=pl.CostEstimate(flops=0, transcendentals=0, bytes_accessed=4 * count * stacks * rows * columns),
    )(jnp.stack(offsets).astype(jnp.int32), *pieces)


def xor_take(stack, me):
    return jnp.concatenate([lax.dynamic_index_in_dim(stack, n ^ me, 0) for n in range(stack.shape[0])])


def sum_over_fsdp(grads, z, x, core):
    f32, bf16 = jnp.float32, jnp.bfloat16
    width = grads[0].shape[1]
    halves = [g.reshape(8, 2, 64, width) for g in grads]
    send = jnp.stack([lax.dynamic_index_in_dim(h, core ^ 1, 1, keepdims=False) for h in halves])
    keep = jnp.stack([lax.dynamic_index_in_dim(h, core, 1, keepdims=False) for h in halves])
    part = (keep.astype(f32) + to_core(send).astype(f32)).astype(bf16)
    part = part.reshape(len(grads), 4, 2, 64, width)
    send = lax.dynamic_index_in_dim(part, x ^ 1, 2, keepdims=False)
    keep = lax.dynamic_index_in_dim(part, x, 2, keepdims=False)
    part = (keep.astype(f32) + to_x(send).astype(f32)).astype(bf16)
    got = [to_z(lax.dynamic_index_in_dim(part, z ^ k, 1, keepdims=False), k) for k in (1, 2, 3)]
    total = lax.dynamic_index_in_dim(part, z, 1, keepdims=False).astype(f32)
    for piece in got:
        total = total + piece.astype(f32)
    low = total.astype(bf16)
    low = (low.astype(f32) + to_y(low).astype(f32)).astype(bf16)
    other = to_core(low)
    first = jnp.where(core == 0, low, other)
    second = jnp.where(core == 0, other, low)
    return jnp.concatenate([first, second], axis=1).astype(f32)


def sum_everywhere(value):
    value = value + to_core(value)
    value = value + to_y(value)
    value = value + to_x(value)
    got = [to_z(value, k) for k in (1, 2, 3)]
    return value + got[0] + got[1] + got[2]


def tiled_shards(
    tokens,
    memory,
    cotangent,
    block_map,
    block_order,
    self_projection,
    self_output,
    self_query_bias,
    self_value_bias,
    self_output_bias,
    first_gain,
    first_shift,
    cross_query,
    cross_memory,
    cross_output,
    cross_query_bias,
    cross_value_bias,
    cross_output_bias,
    second_gain,
    second_shift,
    expand_weight,
    reduce_weight,
    expand_bias,
    reduce_bias,
    third_gain,
    third_shift,
):
    bf16 = jnp.bfloat16
    f32 = jnp.float32
    own_rows = tokens[0]
    rows, width = own_rows.shape
    me_c, me_f = lax.axis_index("ctx"), lax.axis_index("fsdp")
    core, z, x = me_c % 2, me_f // 2, me_f % 2
    share = width // 4

    def dot(left, right):
        return jnp.dot(left, right, preferred_element_type=f32)

    rows_y = to_y(own_rows)
    columns = [lax.dynamic_slice(self_projection, (0, part * width + me_c * share), (128, share)) for part in range(3)]
    projection_pieces = fsdp_pieces(jnp.concatenate(columns, axis=1))
    rows_core = to_core(own_rows)
    rows_diagonal = to_core(rows_y)
    sequence = jnp.concatenate([own_rows, rows_core, rows_y, rows_diagonal])
    sources = fsdp_sources(me_f)
    (projection,) = place(projection_pieces, [s * 128 for s in sources])

    vectors = (self_query_bias, self_value_bias, self_output_bias, first_gain, first_shift, cross_query_bias,
               cross_value_bias, cross_output_bias, second_gain, second_shift, reduce_bias, third_gain, third_shift)
    packed = jnp.concatenate([jnp.stack(vectors), expand_bias.reshape(4, 128)])
    gathered = lax.all_gather(packed, "fsdp", axis=0).astype(f32)
    (query_bias, value_bias, out_bias, gain_one, shift_one, cross_qbias, cross_vbias, cross_obias,
     gain_two, shift_two, reduce_bias_full, gain_three, shift_three) = [gathered[:, i].reshape(width) for i in range(13)]
    expand_bias_full = gathered[:, 13:].reshape(4 * width)

    expand_full = lax.all_gather(lax.dynamic_slice_in_dim(expand_weight, me_c * 32, 32), ("fsdp", "ctx"), axis=0, tiled=True)
    reduce_full = lax.all_gather(lax.dynamic_slice_in_dim(reduce_weight, me_c * 128, 128), ("fsdp", "ctx"), axis=0, tiled=True)

    middle = jnp.stack([cross_memory[:, :width], cross_memory[:, width:], self_output, cross_query, cross_output])
    half_pieces = fsdp_pieces(lax.dynamic_slice_in_dim(middle, core * 64, 64, axis=1))
    other_pieces = [to_core(piece) for piece in half_pieces]
    offsets = [s * 128 + core * 64 for s in sources] + [s * 128 + (core ^ 1) * 64 for s in sources]
    memory_key_full, memory_value_full, self_out_full, cross_query_full, cross_out_full = place(half_pieces + other_pieces, offsets)

    projected = dot(sequence, projection)
    bias = jnp.concatenate([
        lax.dynamic_slice_in_dim(query_bias, me_c * share, share),
        jnp.zeros((share,), f32),
        lax.dynamic_slice_in_dim(value_bias, me_c * share, share),
    ])
    qkv = (projected + bias).astype(bf16)
    scalars = (block_order[0], block_map[0].reshape(-1), me_c.reshape(1).astype(jnp.int32))
    heads_out, self_lse = attention_forward(qkv, 0, [qkv], 1, [qkv], 2, share, scalars, BLK)

    memory_rows = memory[0]
    memory_keys = dot(memory_rows, memory_key_full).astype(bf16)
    memory_values = (dot(memory_rows, memory_value_full) + cross_vbias).astype(bf16)
    keys_y, values_y = to_y(memory_keys), to_y(memory_values)
    key_list = [memory_keys, to_core(memory_keys), keys_y, to_core(keys_y)]
    value_list = [memory_values, to_core(memory_values), values_y, to_core(values_y)]

    pieces = [heads_out[i * rows:(i + 1) * rows] for i in range(4)]
    attended = jnp.concatenate([pieces[0], to_core(pieces[1]), to_y(pieces[2]), to_diagonal(pieces[3])], axis=1)
    self_out_rel = xor_take(self_out_full.reshape(4, share, width), me_c).reshape(width, width)
    branch = dot(attended, self_out_rel) + out_bias
    hidden_one, normed_one, inverse_one = layer_norm(residual_scale * own_rows.astype(f32) + branch, gain_one, shift_one)

    hidden_low = hidden_one.astype(bf16)
    cross_queries = (dot(hidden_low, cross_query_full) + cross_qbias).astype(bf16)
    cross_low, cross_lse = attention_forward(cross_queries, 0, key_list, 0, value_list, 0, width, None, rows)
    cross_branch = dot(cross_low, cross_out_full) + cross_obias
    hidden_two, normed_two, inverse_two = layer_norm(residual_scale * hidden_one + cross_branch, gain_two, shift_two)

    hidden_two_low = hidden_two.astype(bf16)
    expanded = dot(hidden_two_low, expand_full) + expand_bias_full
    activated = gelu_tanh(expanded).astype(bf16)
    reduced = dot(activated, reduce_full) + reduce_bias_full
    result, normed_three, inverse_three = layer_norm(residual_scale * hidden_two + reduced, gain_three, shift_three)
    output = result.astype(bf16)[None]

    upstream = cotangent[0].astype(f32)
    grad_third, grad_third_gain, grad_third_shift = layer_norm_back(upstream, gain_three, normed_three, inverse_three)
    grad_reduced = grad_third.astype(bf16)
    grad_reduce_bias = jnp.sum(grad_reduced.astype(f32), axis=0)
    grad_reduce_weight = dot(activated.T, grad_reduced).astype(bf16)
    grad_expanded = (dot(grad_reduced, reduce_full.T) * gelu_slope(expanded)).astype(bf16)
    grad_expand_bias = jnp.sum(grad_expanded.astype(f32), axis=0)
    expand_parts = [
        dot(hidden_two_low.T, grad_expanded[:, i * width:(i + 1) * width]).astype(bf16).reshape(8, 128, width)
        for i in range(4)
    ]
    feed = jnp.concatenate([jnp.stack(expand_parts, axis=1), grad_reduce_weight.reshape(8, 4, 128, width)], axis=2)
    feed_share = lax.psum_scatter(feed.reshape(32 * 256, width), ("fsdp", "ctx"), scatter_dimension=0, tiled=True)
    grad_hidden_two = residual_scale * grad_third + dot(grad_expanded, expand_full.T)

    grad_second, grad_second_gain, grad_second_shift = layer_norm_back(grad_hidden_two, gain_two, normed_two, inverse_two)
    grad_cross_branch = grad_second.astype(bf16)
    grad_cross_output_bias = jnp.sum(grad_cross_branch.astype(f32), axis=0)
    grad_cross_output = dot(cross_low.T, grad_cross_branch).astype(bf16)
    grad_cross_low = dot(grad_cross_branch, cross_out_full.T).astype(bf16)
    cross_back = attention_backward(
        cross_queries, 0, grad_cross_low, cross_low, cross_lse, key_list, 0, value_list, 0, width, None, rows
    )
    grad_cross_queries = cross_back[0]

    def to_owner(terms):
        near = terms[0].astype(f32) + to_core(terms[1]).astype(f32)
        far = (terms[2].astype(f32) + to_core(terms[3]).astype(f32)).astype(bf16)
        return (near + to_y(far).astype(f32)).astype(bf16)

    grad_memory_keys, grad_memory_values = to_owner(cross_back[1:5]), to_owner(cross_back[5:9])

    grad_cross_query_bias = jnp.sum(grad_cross_queries.astype(f32), axis=0)
    grad_cross_query = dot(hidden_low.T, grad_cross_queries).astype(bf16)
    grad_hidden_one = residual_scale * grad_second + dot(grad_cross_queries, cross_query_full.T)
    grad_first, grad_first_gain, grad_first_shift = layer_norm_back(grad_hidden_one, gain_one, normed_one, inverse_one)
    grad_branch = grad_first.astype(bf16)
    grad_self_output_bias = jnp.sum(grad_branch.astype(f32), axis=0)
    grad_attended = dot(grad_branch, self_out_rel.T).astype(bf16)
    sends = [grad_attended[:, i * share:(i + 1) * share] for i in range(4)]
    heads_grad = jnp.concatenate([sends[0], to_core(sends[1]), to_y(sends[2]), to_diagonal(sends[3])])
    grad_self_output = xor_take(dot(attended.T, grad_branch).astype(bf16).reshape(4, share, width), me_c).reshape(width, width)

    grad_cross_value_bias = jnp.sum(grad_memory_values.astype(f32), axis=0)
    grad_memory_key_weight = dot(memory_rows.T, grad_memory_keys).astype(bf16)
    grad_memory_value_weight = dot(memory_rows.T, grad_memory_values).astype(bf16)
    memory_grad = (dot(grad_memory_keys, memory_key_full.T) + dot(grad_memory_values, memory_value_full.T))[None]
    middle_sum = sum_over_fsdp(
        [grad_cross_output, grad_cross_query, grad_memory_key_weight, grad_memory_value_weight, grad_self_output], z, x, core
    )

    grad_q, grad_k, grad_v = attention_backward(
        qkv, 0, heads_grad, heads_out, self_lse, [qkv], 1, [qkv], 2, share, scalars, BLK
    )
    grad_qkv = jnp.concatenate([grad_q, grad_k, grad_v], axis=1)
    partial = dot(grad_qkv, projection.T).astype(bf16)
    near = partial[:rows].astype(f32) + to_core(partial[rows:2 * rows]).astype(f32)
    far = (partial[2 * rows:3 * rows].astype(f32) + to_core(partial[3 * rows:]).astype(f32)).astype(bf16)
    token_grad = (residual_scale * grad_first + near + to_y(far).astype(f32))[None]

    own_grad = dot(sequence.T, grad_qkv).astype(bf16).reshape(4, 2, 128, 3 * share)
    keep = lax.dynamic_index_in_dim(own_grad, x, 1, keepdims=False).astype(f32)
    part = (keep + to_x(lax.dynamic_index_in_dim(own_grad, x ^ 1, 1, keepdims=False)).astype(f32)).astype(bf16)
    got = [to_z(lax.dynamic_index_in_dim(part, z ^ k, 0, keepdims=False), k) for k in (1, 2, 3)]
    total = lax.dynamic_index_in_dim(part, z, 0, keepdims=False).astype(f32)
    total = (total + got[0].astype(f32) + got[1].astype(f32) + got[2].astype(f32)).astype(bf16)
    shares = xor_take(jnp.stack([total, to_core(total), to_y(total), to_diagonal(total)]), me_c)
    grad_self_projection = shares.reshape(4, 128, 3, share).transpose(1, 2, 0, 3).reshape(128, 3 * width).astype(f32)

    value_sums = jnp.stack([jnp.sum(grad_q.astype(f32), axis=0), jnp.sum(grad_v.astype(f32), axis=0)])
    own_sums = lax.dynamic_update_slice(jnp.zeros((2, width), f32), value_sums, (0, me_c * share))
    vector_grads = jnp.concatenate([
        jnp.stack([
            grad_self_output_bias, grad_first_gain, grad_first_shift, grad_cross_query_bias, grad_cross_value_bias,
            grad_cross_output_bias, grad_second_gain, grad_second_shift, grad_reduce_bias, grad_third_gain, grad_third_shift,
        ]),
        grad_expand_bias.reshape(8, 4, 128).transpose(1, 0, 2).reshape(4, width),
    ])
    early = lax.dynamic_slice_in_dim(sum_everywhere(vector_grads), me_f * 128, 128, axis=1)
    late = lax.dynamic_slice_in_dim(sum_everywhere(own_sums), me_f * 128, 128, axis=1)

    feed_all = xor_take(jnp.stack([feed_share, to_core(feed_share), to_y(feed_share), to_diagonal(feed_share)]), me_c)
    grad_expand = feed_all[:, :128].transpose(1, 0, 2).reshape(128, 4 * width).astype(f32)
    grad_reduce = feed_all[:, 128:].reshape(512, width).astype(f32)

    grad_cross_memory = jnp.concatenate([middle_sum[2], middle_sum[3]], axis=1)
    return (
        output,
        token_grad,
        memory_grad,
        grad_self_projection,
        middle_sum[4],
        late[0],
        late[1],
        early[0],
        early[1],
        early[2],
        middle_sum[1],
        grad_cross_memory,
        middle_sum[0],
        early[3],
        early[4],
        early[5],
        early[6],
        early[7],
        grad_expand,
        grad_reduce,
        early[11:15].reshape(512),
        early[8],
        early[9],
        early[10],
    )


def head_split(matrix):
    return matrix.reshape(matrix.shape[0], HEADS, HEAD_DIM)


def piece_size(length):
    return min(512, length)


def piece_masks(key_blocks, allowed_rows):
    length = key_blocks.shape[0]
    piece = piece_size(length)
    count = length // piece
    if allowed_rows is None:
        return jnp.ones((count, 1, 1), jnp.bool_)
    nblocks = allowed_rows.shape[1]
    onehot = (key_blocks[:, None] == jnp.arange(nblocks, dtype=jnp.int32)[None, :]).astype(
        jnp.float32
    )
    live = jnp.dot(allowed_rows, onehot.T) > 0.5
    return jnp.moveaxis(live.reshape(live.shape[0], count, piece), 1, 0)


def masked_scores(query_heads, key_piece, live):
    scores = (
        jnp.einsum("qhd,khd->hqk", query_heads, key_piece, preferred_element_type=jnp.float32)
        * score_scale
    )
    return jnp.where(live[None], scores, masked_score)


def run_guarded(guarded, live, work, fallback):
    if guarded:
        return lax.cond(jnp.any(live), work, lambda unused: fallback, live)
    return work(live)


def attend_forward(query_heads, key_heads, value_heads, live_pieces, guarded):
    count = live_pieces.shape[0]
    piece = key_heads.shape[0] // count
    key_pieces = key_heads.reshape((count, piece) + key_heads.shape[1:])
    value_pieces = value_heads.reshape((count, piece) + value_heads.shape[1:])
    rows = query_heads.shape[0]

    def first_step(carry, inputs):
        run_max, run_sum = carry
        key_piece, live = inputs

        def work(live_now):
            scores = masked_scores(query_heads, key_piece, live_now)
            new_max = jnp.maximum(run_max, jnp.max(scores, axis=-1))
            shifted = jnp.where(live_now[None], jnp.exp(scores - new_max[:, :, None]), 0.0)
            return (new_max, run_sum * jnp.exp(run_max - new_max) + jnp.sum(shifted, axis=-1))

        return (run_guarded(guarded, live, work, (run_max, run_sum)), None)

    start = (
        jnp.full((HEADS, rows), masked_score, jnp.float32),
        jnp.zeros((HEADS, rows), jnp.float32),
    )
    (final_max, final_sum), unused = lax.scan(first_step, start, (key_pieces, live_pieces))
    log_total = final_max + jnp.log(final_sum)

    def second_step(total, inputs):
        key_piece, value_piece, live = inputs

        def work(live_now):
            scores = masked_scores(query_heads, key_piece, live_now)
            probs = jnp.exp(scores - log_total[:, :, None]).astype(jnp.bfloat16)
            return total + jnp.einsum(
                "hqk,khd->qhd", probs, value_piece, preferred_element_type=jnp.float32
            )

        return (run_guarded(guarded, live, work, total), None)

    empty = jnp.zeros((rows, HEADS, HEAD_DIM), jnp.float32)
    attended, unused = lax.scan(second_step, empty, (key_pieces, value_pieces, live_pieces))
    return (attended, log_total)


def attend_backward(
    query_heads, key_heads, value_heads, log_total, grad_heads, delta, live_pieces, guarded
):
    count = live_pieces.shape[0]
    piece = key_heads.shape[0] // count
    key_pieces = key_heads.reshape((count, piece) + key_heads.shape[1:])
    value_pieces = value_heads.reshape((count, piece) + value_heads.shape[1:])
    rows = query_heads.shape[0]
    blank = jnp.zeros((piece, HEADS, HEAD_DIM), jnp.float32)

    def back_step(grad_query, inputs):
        key_piece, value_piece, live = inputs

        def work(live_now):
            scores = masked_scores(query_heads, key_piece, live_now)
            probs = jnp.exp(scores - log_total[:, :, None])
            grad_probs = jnp.einsum(
                "qhd,khd->hqk", grad_heads, value_piece, preferred_element_type=jnp.float32
            )
            grad_scores = (probs * (grad_probs - delta[:, :, None])).astype(jnp.bfloat16)
            new_query = (
                grad_query
                + jnp.einsum(
                    "hqk,khd->qhd", grad_scores, key_piece, preferred_element_type=jnp.float32
                )
                * score_scale
            )
            grad_key = (
                jnp.einsum(
                    "hqk,qhd->khd", grad_scores, query_heads, preferred_element_type=jnp.float32
                )
                * score_scale
            )
            grad_value = jnp.einsum(
                "hqk,qhd->khd",
                probs.astype(jnp.bfloat16),
                grad_heads,
                preferred_element_type=jnp.float32,
            )
            return (new_query, (grad_key, grad_value))

        return run_guarded(guarded, live, work, (grad_query, (blank, blank)))

    empty = jnp.zeros((rows, HEADS, HEAD_DIM), jnp.float32)
    grad_query, (key_grads, value_grads) = lax.scan(
        back_step, empty, (key_pieces, value_pieces, live_pieces)
    )
    width = HEADS * HEAD_DIM
    return (
        grad_query.reshape(rows, width),
        key_grads.reshape(-1, width),
        value_grads.reshape(-1, width),
    )


def plain_shards(
    tokens,
    memory,
    cotangent,
    block_map,
    block_order,
    self_projection,
    self_output,
    self_query_bias,
    self_value_bias,
    self_output_bias,
    first_gain,
    first_shift,
    cross_query,
    cross_memory,
    cross_output,
    cross_query_bias,
    cross_value_bias,
    cross_output_bias,
    second_gain,
    second_shift,
    expand_weight,
    reduce_weight,
    expand_bias,
    reduce_bias,
    third_gain,
    third_shift,
):
    bf16 = jnp.bfloat16
    f32 = jnp.float32
    rows_in = tokens[0]
    rows = rows_in.shape[0]
    width = rows_in.shape[1]
    ctx_count = lax.axis_size("ctx")
    slot = lax.axis_index("ctx")
    positions = jnp.arange(rows * ctx_count, dtype=jnp.int32)
    group_index = positions // rows
    group_match = group_index[:, None] == jnp.arange(ctx_count, dtype=jnp.int32)[None, :]
    group_place = jnp.sum(jnp.where(group_match, block_order[0][None, :], 0), axis=1)
    key_blocks = (group_place * rows + positions % rows) // BLK
    own_blocks = lax.dynamic_slice_in_dim(key_blocks, slot * rows, rows)
    nblocks = block_map.shape[1]
    own_onehot = (own_blocks[:, None] == jnp.arange(nblocks, dtype=jnp.int32)[None, :]).astype(f32)
    allowed_rows = jnp.dot(own_onehot, block_map[0].astype(f32))
    self_live = piece_masks(key_blocks, allowed_rows)
    (
        projection_full,
        self_out_full,
        query_bias_full,
        value_bias_full,
        out_bias_full,
        gain_one,
        shift_one,
    ) = (
        lax.all_gather(self_projection, "fsdp", axis=0, tiled=True),
        lax.all_gather(self_output, "fsdp", axis=0, tiled=True),
        lax.all_gather(self_query_bias, "fsdp", axis=0, tiled=True),
        lax.all_gather(self_value_bias, "fsdp", axis=0, tiled=True),
        lax.all_gather(self_output_bias, "fsdp", axis=0, tiled=True),
        lax.all_gather(first_gain, "fsdp", axis=0, tiled=True),
        lax.all_gather(first_shift, "fsdp", axis=0, tiled=True),
    )
    projected = jnp.dot(rows_in, projection_full, preferred_element_type=f32)
    queries = (projected[:, :width] + query_bias_full).astype(bf16)
    keys_own = projected[:, width : 2 * width].astype(bf16)
    values_own = (projected[:, 2 * width :] + value_bias_full).astype(bf16)
    keys_all, values_all = (
        lax.all_gather(keys_own, "ctx", axis=0, tiled=True),
        lax.all_gather(values_own, "ctx", axis=0, tiled=True),
    )
    query_heads = head_split(queries)
    key_heads = head_split(keys_all)
    value_heads = head_split(values_all)
    attended, self_total = attend_forward(query_heads, key_heads, value_heads, self_live, True)
    attended_low = attended.reshape(rows, width).astype(bf16)
    branch = jnp.dot(attended_low, self_out_full, preferred_element_type=f32) + out_bias_full
    hidden_one, normed_one, inverse_one = layer_norm(
        residual_scale * rows_in.astype(f32) + branch, gain_one, shift_one
    )
    (
        cross_query_full,
        cross_memory_full,
        cross_out_full,
        cross_qbias_full,
        cross_vbias_full,
        cross_obias_full,
        gain_two,
        shift_two,
    ) = (
        lax.all_gather(cross_query, "fsdp", axis=0, tiled=True),
        lax.all_gather(cross_memory, "fsdp", axis=0, tiled=True),
        lax.all_gather(cross_output, "fsdp", axis=0, tiled=True),
        lax.all_gather(cross_query_bias, "fsdp", axis=0, tiled=True),
        lax.all_gather(cross_value_bias, "fsdp", axis=0, tiled=True),
        lax.all_gather(cross_output_bias, "fsdp", axis=0, tiled=True),
        lax.all_gather(second_gain, "fsdp", axis=0, tiled=True),
        lax.all_gather(second_shift, "fsdp", axis=0, tiled=True),
    )
    hidden_low = hidden_one.astype(bf16)
    cross_queries = (
        jnp.dot(hidden_low, cross_query_full, preferred_element_type=f32) + cross_qbias_full
    ).astype(bf16)
    memory_rows = memory[0]
    memory_proj = jnp.dot(memory_rows, cross_memory_full, preferred_element_type=f32)
    memory_keys = memory_proj[:, :width].astype(bf16)
    memory_values = (memory_proj[:, width:] + cross_vbias_full).astype(bf16)
    memory_keys_all, memory_values_all = (
        lax.all_gather(memory_keys, "ctx", axis=0, tiled=True),
        lax.all_gather(memory_values, "ctx", axis=0, tiled=True),
    )
    cross_heads = head_split(cross_queries)
    memory_key_heads = head_split(memory_keys_all)
    memory_value_heads = head_split(memory_values_all)
    cross_live = piece_masks(jnp.zeros((memory_keys_all.shape[0],), jnp.int32), None)
    cross_attended, cross_total = attend_forward(
        cross_heads, memory_key_heads, memory_value_heads, cross_live, False
    )
    cross_low = cross_attended.reshape(rows, width).astype(bf16)
    cross_branch = jnp.dot(cross_low, cross_out_full, preferred_element_type=f32) + cross_obias_full
    hidden_two, normed_two, inverse_two = layer_norm(
        residual_scale * hidden_one + cross_branch, gain_two, shift_two
    )
    expand_full, reduce_full, expand_bias_full, reduce_bias_full, gain_three, shift_three = (
        lax.all_gather(expand_weight, "fsdp", axis=0, tiled=True),
        lax.all_gather(reduce_weight, "fsdp", axis=0, tiled=True),
        lax.all_gather(expand_bias, "fsdp", axis=0, tiled=True),
        lax.all_gather(reduce_bias, "fsdp", axis=0, tiled=True),
        lax.all_gather(third_gain, "fsdp", axis=0, tiled=True),
        lax.all_gather(third_shift, "fsdp", axis=0, tiled=True),
    )
    hidden_two_low = hidden_two.astype(bf16)
    expanded = jnp.dot(hidden_two_low, expand_full, preferred_element_type=f32) + expand_bias_full
    activated = gelu_tanh(expanded).astype(bf16)
    reduced = jnp.dot(activated, reduce_full, preferred_element_type=f32) + reduce_bias_full
    result, normed_three, inverse_three = layer_norm(
        residual_scale * hidden_two + reduced, gain_three, shift_three
    )
    output = result.astype(bf16)[None]
    upstream = cotangent[0].astype(f32)
    grad_third, grad_third_gain, grad_third_shift = layer_norm_back(
        upstream, gain_three, normed_three, inverse_three
    )
    grad_reduced = grad_third.astype(bf16)
    grad_reduce_bias = jnp.sum(grad_reduced.astype(f32), axis=0)
    grad_reduce_weight = jnp.dot(activated.T, grad_reduced, preferred_element_type=f32)
    grad_activated = jnp.dot(grad_reduced, reduce_full.T, preferred_element_type=f32)
    grad_expanded = (grad_activated * gelu_slope(expanded)).astype(bf16)
    grad_expand_bias = jnp.sum(grad_expanded.astype(f32), axis=0)
    grad_expand_weight = jnp.dot(hidden_two_low.T, grad_expanded, preferred_element_type=f32)
    grad_hidden_two = residual_scale * grad_third + jnp.dot(
        grad_expanded, expand_full.T, preferred_element_type=f32
    )
    grad_second, grad_second_gain, grad_second_shift = layer_norm_back(
        grad_hidden_two, gain_two, normed_two, inverse_two
    )
    grad_cross_branch = grad_second.astype(bf16)
    grad_cross_output_bias = jnp.sum(grad_cross_branch.astype(f32), axis=0)
    grad_cross_output = jnp.dot(cross_low.T, grad_cross_branch, preferred_element_type=f32)
    grad_cross_low = jnp.dot(
        grad_cross_branch, cross_out_full.T, preferred_element_type=f32
    ).astype(bf16)
    grad_cross_heads = head_split(grad_cross_low)
    cross_delta = jnp.sum(grad_cross_heads.astype(f32) * cross_attended, axis=-1).T
    grad_cross_queries, memory_key_terms, memory_value_terms = attend_backward(
        cross_heads,
        memory_key_heads,
        memory_value_heads,
        cross_total,
        grad_cross_heads,
        cross_delta,
        cross_live,
        False,
    )
    grad_memory_keys, grad_memory_values = (
        lax.psum_scatter(
            memory_key_terms.astype(jnp.bfloat16), "ctx", scatter_dimension=0, tiled=True
        ).astype(jnp.float32),
        lax.psum_scatter(
            memory_value_terms.astype(jnp.bfloat16), "ctx", scatter_dimension=0, tiled=True
        ).astype(jnp.float32),
    )
    grad_memory_pair = jnp.concatenate(
        [grad_memory_keys.astype(bf16), grad_memory_values.astype(bf16)], axis=1
    )
    grad_cross_value_bias = jnp.sum(grad_memory_pair[:, width:].astype(f32), axis=0)
    grad_cross_memory = jnp.dot(memory_rows.T, grad_memory_pair, preferred_element_type=f32)
    memory_grad = jnp.dot(grad_memory_pair, cross_memory_full.T, preferred_element_type=f32)[None]
    grad_cross_low_queries = grad_cross_queries.astype(bf16)
    grad_cross_query_bias = jnp.sum(grad_cross_low_queries.astype(f32), axis=0)
    grad_cross_query = jnp.dot(hidden_low.T, grad_cross_low_queries, preferred_element_type=f32)
    grad_hidden_one = residual_scale * grad_second + jnp.dot(
        grad_cross_low_queries, cross_query_full.T, preferred_element_type=f32
    )
    grad_first, grad_first_gain, grad_first_shift = layer_norm_back(
        grad_hidden_one, gain_one, normed_one, inverse_one
    )
    grad_branch = grad_first.astype(bf16)
    grad_self_output_bias = jnp.sum(grad_branch.astype(f32), axis=0)
    grad_self_output = jnp.dot(attended_low.T, grad_branch, preferred_element_type=f32)
    grad_attended = jnp.dot(grad_branch, self_out_full.T, preferred_element_type=f32).astype(bf16)
    grad_attended_heads = head_split(grad_attended)
    self_delta = jnp.sum(grad_attended_heads.astype(f32) * attended, axis=-1).T
    grad_queries, key_terms, value_terms = attend_backward(
        query_heads,
        key_heads,
        value_heads,
        self_total,
        grad_attended_heads,
        self_delta,
        self_live,
        True,
    )
    grad_keys, grad_values = (
        lax.psum_scatter(
            key_terms.astype(jnp.bfloat16), "ctx", scatter_dimension=0, tiled=True
        ).astype(jnp.float32),
        lax.psum_scatter(
            value_terms.astype(jnp.bfloat16), "ctx", scatter_dimension=0, tiled=True
        ).astype(jnp.float32),
    )
    grad_projected = jnp.concatenate(
        [grad_queries.astype(bf16), grad_keys.astype(bf16), grad_values.astype(bf16)], axis=1
    )
    grad_self_query_bias = jnp.sum(grad_projected[:, :width].astype(f32), axis=0)
    grad_self_value_bias = jnp.sum(grad_projected[:, 2 * width :].astype(f32), axis=0)
    grad_self_projection = jnp.dot(rows_in.T, grad_projected, preferred_element_type=f32)
    token_grad = (
        residual_scale * grad_first
        + jnp.dot(grad_projected, projection_full.T, preferred_element_type=f32)
    )[None]
    shares = (
        lax.psum_scatter(
            grad_self_projection.astype(jnp.bfloat16), "fsdp", scatter_dimension=0, tiled=True
        ).astype(jnp.float32),
        lax.psum_scatter(
            grad_self_output.astype(jnp.bfloat16), "fsdp", scatter_dimension=0, tiled=True
        ).astype(jnp.float32),
        lax.psum_scatter(
            grad_self_query_bias.astype(jnp.bfloat16), "fsdp", scatter_dimension=0, tiled=True
        ).astype(jnp.float32),
        lax.psum_scatter(
            grad_self_value_bias.astype(jnp.bfloat16), "fsdp", scatter_dimension=0, tiled=True
        ).astype(jnp.float32),
        lax.psum_scatter(
            grad_self_output_bias.astype(jnp.bfloat16), "fsdp", scatter_dimension=0, tiled=True
        ).astype(jnp.float32),
        lax.psum_scatter(
            grad_first_gain.astype(jnp.bfloat16), "fsdp", scatter_dimension=0, tiled=True
        ).astype(jnp.float32),
        lax.psum_scatter(
            grad_first_shift.astype(jnp.bfloat16), "fsdp", scatter_dimension=0, tiled=True
        ).astype(jnp.float32),
        lax.psum_scatter(
            grad_cross_query.astype(jnp.bfloat16), "fsdp", scatter_dimension=0, tiled=True
        ).astype(jnp.float32),
        lax.psum_scatter(
            grad_cross_memory.astype(jnp.bfloat16), "fsdp", scatter_dimension=0, tiled=True
        ).astype(jnp.float32),
        lax.psum_scatter(
            grad_cross_output.astype(jnp.bfloat16), "fsdp", scatter_dimension=0, tiled=True
        ).astype(jnp.float32),
        lax.psum_scatter(
            grad_cross_query_bias.astype(jnp.bfloat16), "fsdp", scatter_dimension=0, tiled=True
        ).astype(jnp.float32),
        lax.psum_scatter(
            grad_cross_value_bias.astype(jnp.bfloat16), "fsdp", scatter_dimension=0, tiled=True
        ).astype(jnp.float32),
        lax.psum_scatter(
            grad_cross_output_bias.astype(jnp.bfloat16), "fsdp", scatter_dimension=0, tiled=True
        ).astype(jnp.float32),
        lax.psum_scatter(
            grad_second_gain.astype(jnp.bfloat16), "fsdp", scatter_dimension=0, tiled=True
        ).astype(jnp.float32),
        lax.psum_scatter(
            grad_second_shift.astype(jnp.bfloat16), "fsdp", scatter_dimension=0, tiled=True
        ).astype(jnp.float32),
        lax.psum_scatter(
            grad_expand_weight.astype(jnp.bfloat16), "fsdp", scatter_dimension=0, tiled=True
        ).astype(jnp.float32),
        lax.psum_scatter(
            grad_reduce_weight.astype(jnp.bfloat16), "fsdp", scatter_dimension=0, tiled=True
        ).astype(jnp.float32),
        lax.psum_scatter(
            grad_expand_bias.astype(jnp.bfloat16), "fsdp", scatter_dimension=0, tiled=True
        ).astype(jnp.float32),
        lax.psum_scatter(
            grad_reduce_bias.astype(jnp.bfloat16), "fsdp", scatter_dimension=0, tiled=True
        ).astype(jnp.float32),
        lax.psum_scatter(
            grad_third_gain.astype(jnp.bfloat16), "fsdp", scatter_dimension=0, tiled=True
        ).astype(jnp.float32),
        lax.psum_scatter(
            grad_third_shift.astype(jnp.bfloat16), "fsdp", scatter_dimension=0, tiled=True
        ).astype(jnp.float32),
    )
    summed = (
        lax.psum(shares[0].astype(jnp.bfloat16), "ctx").astype(jnp.float32),
        lax.psum(shares[1].astype(jnp.bfloat16), "ctx").astype(jnp.float32),
        lax.psum(shares[2].astype(jnp.bfloat16), "ctx").astype(jnp.float32),
        lax.psum(shares[3].astype(jnp.bfloat16), "ctx").astype(jnp.float32),
        lax.psum(shares[4].astype(jnp.bfloat16), "ctx").astype(jnp.float32),
        lax.psum(shares[5].astype(jnp.bfloat16), "ctx").astype(jnp.float32),
        lax.psum(shares[6].astype(jnp.bfloat16), "ctx").astype(jnp.float32),
        lax.psum(shares[7].astype(jnp.bfloat16), "ctx").astype(jnp.float32),
        lax.psum(shares[8].astype(jnp.bfloat16), "ctx").astype(jnp.float32),
        lax.psum(shares[9].astype(jnp.bfloat16), "ctx").astype(jnp.float32),
        lax.psum(shares[10].astype(jnp.bfloat16), "ctx").astype(jnp.float32),
        lax.psum(shares[11].astype(jnp.bfloat16), "ctx").astype(jnp.float32),
        lax.psum(shares[12].astype(jnp.bfloat16), "ctx").astype(jnp.float32),
        lax.psum(shares[13].astype(jnp.bfloat16), "ctx").astype(jnp.float32),
        lax.psum(shares[14].astype(jnp.bfloat16), "ctx").astype(jnp.float32),
        lax.psum(shares[15].astype(jnp.bfloat16), "ctx").astype(jnp.float32),
        lax.psum(shares[16].astype(jnp.bfloat16), "ctx").astype(jnp.float32),
        lax.psum(shares[17].astype(jnp.bfloat16), "ctx").astype(jnp.float32),
        lax.psum(shares[18].astype(jnp.bfloat16), "ctx").astype(jnp.float32),
        lax.psum(shares[19].astype(jnp.bfloat16), "ctx").astype(jnp.float32),
        lax.psum(shares[20].astype(jnp.bfloat16), "ctx").astype(jnp.float32),
    )
    return (
        output,
        token_grad,
        memory_grad,
        summed[0],
        summed[1],
        summed[2],
        summed[3],
        summed[4],
        summed[5],
        summed[6],
        summed[7],
        summed[8],
        summed[9],
        summed[10],
        summed[11],
        summed[12],
        summed[13],
        summed[14],
        summed[15],
        summed[16],
        summed[17],
        summed[18],
        summed[19],
        summed[20],
    )


def solution(mesh):
    placed = (
        P("fsdp", "ctx", None),
        P("fsdp", "ctx", None),
        P("fsdp", "ctx", None),
        P("fsdp", None, None),
        P("fsdp", None),
        P("fsdp", None),
        P("fsdp", None),
        P("fsdp"),
        P("fsdp"),
        P("fsdp"),
        P("fsdp"),
        P("fsdp"),
        P("fsdp", None),
        P("fsdp", None),
        P("fsdp", None),
        P("fsdp"),
        P("fsdp"),
        P("fsdp"),
        P("fsdp"),
        P("fsdp"),
        P("fsdp", None),
        P("fsdp", None),
        P("fsdp"),
        P("fsdp"),
        P("fsdp"),
        P("fsdp"),
    )
    sizes = (mesh.shape["ctx"], mesh.shape["fsdp"])
    return jax.shard_map(
        tiled_shards if sizes == (4, 8) else plain_shards,
        mesh=mesh,
        in_specs=placed,
        out_specs=(
            P("fsdp", "ctx", None),
            P("fsdp", "ctx", None),
            P("fsdp", "ctx", None),
            P("fsdp", None),
            P("fsdp", None),
            P("fsdp"),
            P("fsdp"),
            P("fsdp"),
            P("fsdp"),
            P("fsdp"),
            P("fsdp", None),
            P("fsdp", None),
            P("fsdp", None),
            P("fsdp"),
            P("fsdp"),
            P("fsdp"),
            P("fsdp"),
            P("fsdp"),
            P("fsdp", None),
            P("fsdp", None),
            P("fsdp"),
            P("fsdp"),
            P("fsdp"),
            P("fsdp"),
        ),
        check_vma=False,
    )
```

```python
import functools
import math

import jax
import jax.numpy as jnp
from jax import lax
from jax.experimental import pallas as pl
from jax.experimental.layout import Layout, with_layout_constraint
from jax.experimental.pallas import tpu as pltpu
from jax.sharding import PartitionSpec as P

HEADS = 16
HEAD_DIM = 64
BLK = 256


epsilon = 1e-05
residual_scale = 18.0**0.25
score_scale = 0.125
masked_score = -1e30
gelu_coeff = math.sqrt(2.0 / math.pi)


def gelu_tanh(value):
    return 0.5 * value * (1.0 + jnp.tanh(gelu_coeff * (value + 0.044715 * value * value * value)))


def gelu_slope(value):
    inner = jnp.tanh(gelu_coeff * (value + 0.044715 * value * value * value))
    return 0.5 * (1.0 + inner) + 0.5 * value * (1.0 - inner * inner) * gelu_coeff * (
        1.0 + 3.0 * 0.044715 * value * value
    )


def layer_norm(summed, gain, shift):
    centred = summed - jnp.mean(summed, axis=-1, keepdims=True)
    inverse = lax.rsqrt(jnp.mean(centred * centred, axis=-1, keepdims=True) + epsilon)
    normed = centred * inverse
    return (normed * gain + shift, normed, inverse)


def layer_norm_back(upstream, gain, normed, inverse):
    scaled = upstream * gain
    inner = (
        scaled
        - jnp.mean(scaled, axis=-1, keepdims=True)
        - normed * jnp.mean(scaled * normed, axis=-1, keepdims=True)
    )
    return (inner * inverse, jnp.sum(upstream * normed, axis=0), jnp.sum(upstream, axis=0))


score_log2 = 0.125 * math.log2(math.e)
NT = (((1,), (1,)), ((), ()))
NN = (((1,), (0,)), ((), ()))
TN = (((0,), (0,)), ((), ()))


def mxu(left, right, dims):
    return lax.dot_general(left, right, dims, preferred_element_type=jnp.float32)


def two_heads(pair):
    low = lax.broadcasted_iota(jnp.int32, pair.shape, 1) < 64
    zero = jnp.zeros_like(pair)
    return jnp.concatenate([jnp.where(low, pair, zero), jnp.where(low, zero, pair)], axis=0)


def one_pair(stacked):
    rows = stacked.shape[0] // 2
    top = stacked[:rows]
    low = lax.broadcasted_iota(jnp.int32, top.shape, 1) < 64
    return jnp.where(low, top, stacked[rows:])


def place_of(order_ref, slot_ref, index, per_group):
    return order_ref[slot_ref[0] ^ (index // per_group)] * per_group + index % per_group


def seen(scalars, query_index, key_index, per_group, count):
    if scalars is None:
        return None
    order_ref, map_ref, slot_ref = scalars
    row = place_of(order_ref, slot_ref, query_index, per_group)
    column = place_of(order_ref, slot_ref, key_index, per_group)
    return map_ref[row * count + column] > 0


def guarded(flag, work):
    if flag is None:
        work()
    else:
        pl.when(flag)(work)


def pair_lanes(unit):
    return slice(unit * 128, (unit + 1) * 128)


def forward_body(masked, units, chunks, key_rows, pieces, per_group, *refs):
    scalars = None
    if masked:
        scalars, refs = refs[:3], refs[3:]
    q_ref, refs = refs[0], refs[1:]
    k_refs, v_refs, refs = refs[:pieces], refs[pieces:2 * pieces], refs[2 * pieces:]
    o_ref, lse_ref, stacked, scores, top, shift, total, acc = refs
    rows = stacked.shape[1]
    query_index = pl.program_id(1)

    def part(ref_list, chunk, unit):
        if pieces > 1:
            return ref_list[chunk][:, pair_lanes(unit)]
        return ref_list[0][chunk * key_rows:(chunk + 1) * key_rows, pair_lanes(unit)]

    for unit in range(units):
        stacked[unit] = two_heads(q_ref[:, pair_lanes(unit)])
        top[unit] = jnp.full((rows, 128), -1e30, jnp.float32)
        total[unit] = jnp.zeros((rows, 128), jnp.float32)
        acc[unit] = jnp.zeros((rows, 128), jnp.float32)
    for chunk in range(chunks):
        flag = seen(scalars, query_index, chunk, per_group, chunks)

        def scan_max(chunk=chunk):
            for unit in range(units):
                found = mxu(stacked[unit], part(k_refs, chunk, unit), NT)
                scores[unit, chunk] = found
                best = top[unit]
                for lane in range(0, key_rows, 128):
                    best = jnp.maximum(best, found[:, lane:lane + 128])
                top[unit] = best

        guarded(flag, scan_max)
    for unit in range(units):
        peak = jnp.max(top[unit], axis=1, keepdims=True) * score_log2
        shift[unit] = jnp.broadcast_to(peak, (rows, 128))
    for chunk in range(chunks):
        flag = seen(scalars, query_index, chunk, per_group, chunks)

        def weigh(chunk=chunk):
            for unit in range(units):
                found = scores[unit, chunk]
                offset = shift[unit]
                summed = total[unit]
                parts = []
                for lane in range(0, key_rows, 128):
                    weight = jnp.exp2(found[:, lane:lane + 128] * score_log2 - offset)
                    summed = summed + weight
                    parts.append(weight.astype(jnp.bfloat16))
                total[unit] = summed
                acc[unit] = acc[unit] + mxu(jnp.concatenate(parts, axis=1), part(v_refs, chunk, unit), NN)

        guarded(flag, weigh)
    for unit in range(units):
        row_sum = jnp.sum(total[unit], axis=1, keepdims=True)
        o_ref[:, pair_lanes(unit)] = one_pair(acc[unit] / row_sum).astype(o_ref.dtype)
        lse = shift[unit] + jnp.log2(row_sum)
        lse_ref[unit] = lse.T[:8]


def backward_body(masked, units, chunks, key_rows, pieces, per_group, *refs):
    scalars = None
    if masked:
        scalars, refs = refs[:3], refs[3:]
    q_ref, do_ref, o_ref, lse_ref, refs = refs[0], refs[1], refs[2], refs[3], refs[4:]
    k_refs, v_refs, refs = refs[:pieces], refs[pieces:2 * pieces], refs[2 * pieces:]
    dq_ref, dk_refs, dv_refs, refs = refs[0], refs[1:1 + pieces], refs[1 + pieces:1 + 2 * pieces], refs[1 + 2 * pieces:]
    stacked, grads, delta, dq_acc, dk_acc, dv_acc = refs
    query_index = pl.program_id(1)

    def part(ref_list, chunk, unit):
        if pieces > 1:
            return ref_list[chunk][:, pair_lanes(unit)]
        return ref_list[0][chunk * key_rows:(chunk + 1) * key_rows, pair_lanes(unit)]

    @pl.when(query_index == 0)
    def clear():
        dk_acc[...] = jnp.zeros_like(dk_acc)
        dv_acc[...] = jnp.zeros_like(dv_acc)

    for unit in range(units):
        lanes = pair_lanes(unit)
        stacked[unit] = two_heads(q_ref[:, lanes])
        upstream = do_ref[:, lanes]
        grads[unit] = two_heads(upstream)
        product = (upstream.astype(jnp.float32) * o_ref[:, lanes].astype(jnp.float32)).T
        first = jnp.sum(product[:64], axis=0, keepdims=True)
        second = jnp.sum(product[64:], axis=0, keepdims=True)
        delta[unit] = jnp.broadcast_to(jnp.concatenate([first, second], axis=1), delta.shape[1:])
        dq_acc[unit] = jnp.zeros(dq_acc.shape[1:], jnp.float32)
    for chunk in range(chunks):
        flag = seen(scalars, query_index, chunk, per_group, chunks)

        def step(chunk=chunk):
            for unit in range(units):
                queries, upstream = stacked[unit], grads[unit]
                keys, values = part(k_refs, chunk, unit), part(v_refs, chunk, unit)
                found = mxu(keys, queries, NT)
                probs = jnp.exp2(found * score_log2 - lse_ref[unit, 0:1])
                grad_probs = mxu(values, upstream, NT)
                grad_scores = (probs * (grad_probs - delta[unit, 0:1])).astype(jnp.bfloat16)
                dv_acc[unit, chunk] += mxu(probs.astype(jnp.bfloat16), upstream, NN)
                dk_acc[unit, chunk] += mxu(grad_scores, queries, NN)
                dq_acc[unit] += mxu(grad_scores, keys, TN)

        guarded(flag, step)
    for unit in range(units):
        dq_ref[:, pair_lanes(unit)] = (one_pair(dq_acc[unit]) * 0.125).astype(dq_ref.dtype)

    @pl.when(query_index == pl.num_programs(1) - 1)
    def finish():
        for unit in range(units):
            for chunk in range(chunks):
                if pieces > 1:
                    rows = slice(None)
                    dk_ref, dv_ref = dk_refs[chunk], dv_refs[chunk]
                else:
                    rows = slice(chunk * key_rows, (chunk + 1) * key_rows)
                    dk_ref, dv_ref = dk_refs[0], dv_refs[0]
                dk_ref[rows, pair_lanes(unit)] = (dk_acc[unit, chunk] * 0.125).astype(dk_ref.dtype)
                dv_ref[rows, pair_lanes(unit)] = dv_acc[unit, chunk].astype(dv_ref.dtype)


def attention_forward(q, q_col, k_list, k_col, v_list, v_col, width, scalars, key_rows, units=2, per_group=2):
    pieces = len(k_list)
    lanes = units * 128
    rows = q.shape[0]
    keys = sum(k.shape[0] for k in k_list)
    chunks = keys // key_rows
    groups, blocks = width // lanes, rows // BLK
    masked = scalars is not None
    spec_q = pl.BlockSpec((BLK, lanes), lambda h, i, *_: (i, q_col + h))
    specs_k = [pl.BlockSpec((k.shape[0], lanes), lambda h, i, *_: (0, k_col + h)) for k in k_list]
    specs_v = [pl.BlockSpec((v.shape[0], lanes), lambda h, i, *_: (0, v_col + h)) for v in v_list]
    body = functools.partial(forward_body, masked, units, chunks, key_rows, pieces, per_group)
    pairs = rows * keys * (width // 64)
    return pl.pallas_call(
        body,
        grid_spec=pltpu.PrefetchScalarGridSpec(
            num_scalar_prefetch=3 if masked else 0,
            grid=(groups, blocks),
            in_specs=[spec_q] + specs_k + specs_v,
            out_specs=[
                pl.BlockSpec((BLK, lanes), lambda h, i, *_: (i, h)),
                pl.BlockSpec((units, 8, 2 * BLK), lambda h, i, *_: (h, 0, i)),
            ],
            scratch_shapes=[
                pltpu.VMEM((units, 2 * BLK, 128), jnp.bfloat16),
                pltpu.VMEM((units, chunks, 2 * BLK, key_rows), jnp.float32),
                pltpu.VMEM((units, 2 * BLK, 128), jnp.float32),
                pltpu.VMEM((units, 2 * BLK, 128), jnp.float32),
                pltpu.VMEM((units, 2 * BLK, 128), jnp.float32),
                pltpu.VMEM((units, 2 * BLK, 128), jnp.float32),
            ],
        ),
        out_shape=[
            jax.ShapeDtypeStruct((rows, width), jnp.bfloat16),
            jax.ShapeDtypeStruct((width // 128, 8, blocks * 2 * BLK), jnp.float32),
        ],
        compiler_params=pltpu.CompilerParams(vmem_limit_bytes=48 << 20),
        cost_estimate=pl.CostEstimate(flops=pairs * 512, transcendentals=pairs, bytes_accessed=4 * (rows + keys) * width),
    )(*(scalars or ()), q, *k_list, *v_list)


def attention_backward(q, q_col, do, o, lse, k_list, k_col, v_list, v_col, width, scalars, key_rows, units=2, per_group=2, o_col=0):
    pieces = len(k_list)
    lanes = units * 128
    rows = q.shape[0]
    keys = sum(k.shape[0] for k in k_list)
    chunks = keys // key_rows
    groups, blocks = width // lanes, rows // BLK
    masked = scalars is not None
    spec_q = pl.BlockSpec((BLK, lanes), lambda h, i, *_: (i, q_col + h))
    spec_o = pl.BlockSpec((BLK, lanes), lambda h, i, *_: (i, o_col + h))
    spec_dq = pl.BlockSpec((BLK, lanes), lambda h, i, *_: (i, h))
    spec_lse = pl.BlockSpec((units, 8, 2 * BLK), lambda h, i, *_: (o_col + h, 0, i))
    specs_k = [pl.BlockSpec((k.shape[0], lanes), lambda h, i, *_: (0, k_col + h)) for k in k_list]
    specs_v = [pl.BlockSpec((v.shape[0], lanes), lambda h, i, *_: (0, v_col + h)) for v in v_list]
    outs_k = [pl.BlockSpec((k.shape[0], lanes), lambda h, i, *_: (0, h)) for k in k_list]
    body = functools.partial(backward_body, masked, units, chunks, key_rows, pieces, per_group)
    pairs = rows * keys * (width // 64)
    shape_k = [jax.ShapeDtypeStruct((k.shape[0], width), jnp.bfloat16) for k in k_list]
    return pl.pallas_call(
        body,
        grid_spec=pltpu.PrefetchScalarGridSpec(
            num_scalar_prefetch=3 if masked else 0,
            grid=(groups, blocks),
            in_specs=[spec_q, spec_o, spec_o, spec_lse] + specs_k + specs_v,
            out_specs=[spec_dq] + outs_k + outs_k,
            scratch_shapes=[
                pltpu.VMEM((units, 2 * BLK, 128), jnp.bfloat16),
                pltpu.VMEM((units, 2 * BLK, 128), jnp.bfloat16),
                pltpu.VMEM((units, 8, 2 * BLK), jnp.float32),
                pltpu.VMEM((units, 2 * BLK, 128), jnp.float32),
                pltpu.VMEM((units, chunks, key_rows, 128), jnp.float32),
                pltpu.VMEM((units, chunks, key_rows, 128), jnp.float32),
            ],
        ),
        out_shape=[jax.ShapeDtypeStruct((rows, width), jnp.bfloat16)] + shape_k + shape_k,
        compiler_params=pltpu.CompilerParams(vmem_limit_bytes=48 << 20),
        cost_estimate=pl.CostEstimate(flops=pairs * 1280, transcendentals=pairs, bytes_accessed=8 * (rows + keys) * width),
    )(*(scalars or ()), q, do, o, lse, *k_list, *v_list)


def norm_sums(summed):
    mean = jnp.mean(summed, axis=-1, keepdims=True)
    centred = summed - mean
    inverse = lax.rsqrt(jnp.mean(centred * centred, axis=-1, keepdims=True) + epsilon)
    return centred * inverse, inverse


def feed_body(
    core_ref, hidden_ref, upstream_ref, weights_ref, expand_bias_ref, vectors_ref,
    out_ref, grad_hidden_ref, send_ref, keep_ref, grad_bias_ref, sums_ref,
    low, expanded, activated, total, grad_low,
):
    step = pl.program_id(0)
    blocks = pl.num_programs(0) // 2
    block = step % blocks
    width = hidden_ref.shape[1]
    first = weights_ref[:, 0, :128].reshape(width, width)
    second = weights_ref[:, 0, 128:].reshape(width, width)

    @pl.when(step == 0)
    def begin():
        low[...] = hidden_ref[...].astype(jnp.bfloat16)
        total[...] = residual_scale * hidden_ref[...] + vectors_ref[0:1]

    @pl.when(step < blocks)
    def forward():
        wide = mxu(low[...], first, NN) + expand_bias_ref[0]
        expanded[block] = wide
        active = gelu_tanh(wide).astype(jnp.bfloat16)
        activated[block] = active
        total[...] += mxu(active, second, NN)

    @pl.when(step == blocks)
    def turn():
        normed, inverse = norm_sums(total[...])
        gain = vectors_ref[1:2]
        out_ref[...] = (normed * gain + vectors_ref[2:3]).astype(out_ref.dtype)
        upstream = upstream_ref[...].astype(jnp.float32)
        scaled = upstream * gain
        grad = inverse * (
            scaled
            - jnp.mean(scaled, axis=-1, keepdims=True)
            - normed * jnp.mean(scaled * normed, axis=-1, keepdims=True)
        )
        grad_low[...] = grad.astype(jnp.bfloat16)
        grad_hidden_ref[...] = residual_scale * grad
        sums_ref[0:1] = jnp.sum(grad_low[...].astype(jnp.float32), axis=0, keepdims=True)
        sums_ref[1:2] = jnp.sum(upstream * normed, axis=0, keepdims=True)
        sums_ref[2:3] = jnp.sum(upstream, axis=0, keepdims=True)

    @pl.when(step >= blocks)
    def backward():
        grad_active = mxu(grad_low[...], second, NT)
        grad_wide = (grad_active * gelu_slope(expanded[block])).astype(jnp.bfloat16)
        grad_second = mxu(activated[block], grad_low[...], TN).astype(jnp.bfloat16).reshape(-1, 128, width)
        grad_first = mxu(low[...], grad_wide, TN).astype(jnp.bfloat16).reshape(-1, 128, width)

        @pl.when(block < blocks // 2)
        def to_send():
            send_ref[:, 0, 128:] = grad_second
            send_ref[:, 0, :128] = grad_first

        @pl.when(block >= blocks // 2)
        def to_keep():
            keep_ref[:, 0, 128:] = grad_second
            keep_ref[:, 0, :128] = grad_first

        grad_bias_ref[0] = jnp.sum(grad_wide.astype(jnp.float32), axis=0, keepdims=True)
        grad_hidden_ref[...] += mxu(grad_wide, first, NT)


def feed_forward(core, hidden, upstream, weights, expand_bias, vectors):
    rows, width = hidden.shape
    groups, blocks = weights.shape[:2]
    half = blocks // 2

    def at(i, core_ref):
        return (i + half * (1 - core_ref[0])) % blocks

    def back(i, core_ref):
        return (jnp.maximum(i - blocks, 0) + half * (1 - core_ref[0])) % blocks

    whole = pl.BlockSpec((rows, width), lambda i, c: (0, 0))
    once = pl.BlockSpec((rows, width), lambda i, c: (0, 0), pipeline_mode=pl.Buffered(1))
    f32, bf16 = jnp.float32, jnp.bfloat16
    part = (groups, 1, 256, width)
    return pl.pallas_call(
        feed_body,
        grid_spec=pltpu.PrefetchScalarGridSpec(
            num_scalar_prefetch=1,
            grid=(2 * blocks,),
            in_specs=[
                once, once,
                pl.BlockSpec(part, lambda i, c: (0, at(i, c), 0, 0)),
                pl.BlockSpec((1, 1, width), lambda i, c: (at(i, c), 0, 0)),
                pl.BlockSpec((8, width), lambda i, c: (0, 0)),
            ],
            out_specs=[
                whole, whole,
                pl.BlockSpec(part, lambda i, c: (0, jnp.clip(i - blocks, 0, half - 1), 0, 0)),
                pl.BlockSpec(part, lambda i, c: (0, jnp.clip(i - blocks - half, 0, half - 1), 0, 0)),
                pl.BlockSpec((1, 1, width), lambda i, c: (back(i, c), 0, 0)),
                pl.BlockSpec((8, width), lambda i, c: (0, 0)),
            ],
            scratch_shapes=[
                pltpu.VMEM((rows, width), bf16),
                pltpu.VMEM((blocks, rows, width), f32),
                pltpu.VMEM((blocks, rows, width), bf16),
                pltpu.VMEM((rows, width), f32),
                pltpu.VMEM((rows, width), bf16),
            ],
        ),
        out_shape=[
            jax.ShapeDtypeStruct((rows, width), bf16),
            jax.ShapeDtypeStruct((rows, width), f32),
            jax.ShapeDtypeStruct((groups, half, 256, width), bf16),
            jax.ShapeDtypeStruct((groups, half, 256, width), bf16),
            jax.ShapeDtypeStruct((blocks, 1, width), f32),
            jax.ShapeDtypeStruct((8, width), f32),
        ],
        compiler_params=pltpu.CompilerParams(vmem_limit_bytes=60 << 20),
        cost_estimate=pl.CostEstimate(flops=12 * rows * width * width * blocks, transcendentals=2 * rows * width * blocks, bytes_accessed=52 << 20),
    )(core.reshape(1).astype(jnp.int32), hidden, upstream, weights, expand_bias, vectors)


def core_perm():
    return [(c, c ^ 1) for c in range(4)]


def y_perm():
    return [(c, c ^ 2) for c in range(4)]


def diagonal_perm():
    return [(c, c ^ 3) for c in range(4)]


def x_perm():
    return [(f, f ^ 1) for f in range(8)]


def z_perm(k):
    return [(f, f ^ (2 * k)) for f in range(8)]


def to_core(v):
    return lax.ppermute(v, "ctx", core_perm())


def to_y(v):
    return lax.ppermute(v, "ctx", y_perm())


def to_diagonal(v):
    return lax.ppermute(v, "ctx", diagonal_perm())


def to_x(v):
    return lax.ppermute(v, "fsdp", x_perm())


def to_z(v, k):
    return lax.ppermute(v, "fsdp", z_perm(k))


def fsdp_pieces(own):
    along = [own] + [to_z(own, k) for k in (1, 2, 3)]
    return along + [to_x(piece) for piece in along]


def fsdp_sources(me):
    return [me ^ (2 * k + d) for d in (0, 1) for k in range(4)]


def place_body(plan, *refs):
    offsets, refs = refs[0], refs[1:]
    outs, sems = refs[-1 - len(plan):-1], refs[-1]
    pieces = refs[:-1 - len(plan)]
    copies = []
    for i, piece in enumerate(pieces):
        for s, (lead, first, rows) in enumerate(plan):
            source = piece if lead is None else piece.at[lead]
            start = pl.multiple_of(offsets[i] * rows, rows)
            copy = pltpu.make_async_copy(source.at[pl.ds(first, rows)], outs[s].at[pl.ds(start, rows)], sems.at[i, s])
            copy.start()
            copies.append(copy)
    for copy in copies:
        copy.wait()


def place(pieces, slots, plan):
    columns = pieces[0].shape[-1]
    count = len(pieces)
    out = [jax.ShapeDtypeStruct((count * rows, columns), pieces[0].dtype) for _, _, rows in plan]
    anywhere = pl.BlockSpec(memory_space=pl.ANY)
    moved = 4 * count * columns * sum(rows for _, _, rows in plan)
    return pl.pallas_call(
        functools.partial(place_body, plan),
        in_specs=[pl.BlockSpec(memory_space=pltpu.SMEM)] + [anywhere] * count,
        out_specs=[pl.BlockSpec(memory_space=pltpu.VMEM)] * len(plan),
        out_shape=out,
        scratch_shapes=[pltpu.SemaphoreType.DMA((count, len(plan)))],
        compiler_params=pltpu.CompilerParams(vmem_limit_bytes=(moved // 2) + (4 << 20)),
        cost_estimate=pl.CostEstimate(flops=0, transcendentals=0, bytes_accessed=moved),
    )(jnp.stack(slots).astype(jnp.int32), *pieces)


def after(value, other):
    return lax.optimization_barrier((value, other))[0]


def xor_take(stack, me):
    return jnp.concatenate([lax.dynamic_index_in_dim(stack, n ^ me, 0) for n in range(stack.shape[0])])


def from_fsdp(blocks):
    got = lax.all_to_all(blocks, "fsdp", 0, 0)
    return jnp.sum(got.astype(jnp.float32), axis=0)


def part_of(parts, index, axis):
    return lax.dynamic_index_in_dim(parts, index, axis, keepdims=False)


def added(keep, got):
    return (keep.astype(jnp.float32) + got.astype(jnp.float32)).astype(jnp.bfloat16)


def halves_dot(pairs, core):
    def side(index):
        terms = []
        for left, right in pairs:
            half = right.shape[1] // 2
            chosen = lax.dynamic_slice_in_dim(right, index * half, half, axis=1)
            terms.append(jnp.dot(left.T, chosen, preferred_element_type=jnp.float32).astype(jnp.bfloat16))
        return with_layout_constraint(jnp.concatenate(terms, axis=1), Layout(major_to_minor=(0, 1)))

    return side(core), side(core ^ 1)


def over_z(parts, z):
    got = [to_z(part_of(parts, z ^ k, 1), k) for k in (1, 2, 3)]
    total = part_of(parts, z, 1).astype(jnp.float32)
    return (total + got[0].astype(jnp.float32) + got[1].astype(jnp.float32) + got[2].astype(jnp.float32)).astype(jnp.bfloat16)


def ctx_pieces(own):
    line = to_y(own)
    return [own, to_core(own), line, to_core(line)]


def spread_feed_body(core_ref, *refs):
    (own, other), (expand_ref, reduce_ref) = refs[:2], refs[2:]
    for index, source in ((core_ref[0], own), (1 - core_ref[0], other)):
        for p in range(2):
            at = pl.multiple_of(index * 256 + p * 128, 128)
            reduce_ref[pl.ds(at, 128), :] = source[p, 128:].astype(jnp.float32)
            for f in range(8):
                expand_ref[:, pl.ds(at + f * 512, 128)] = source[p, :128, f * 128:(f + 1) * 128].astype(jnp.float32)


def spread_projection_body(me_ref, *refs):
    pieces, (out_ref, vectors_ref) = refs[:4], refs[4:]
    total = jnp.zeros((8, 384), jnp.float32)
    for k in range(4):
        at = pl.multiple_of((me_ref[0] ^ k) * 256, 128)
        for part in range(3):
            for pair in range(2):
                source = pieces[k][:128, pair * 384 + part * 128:pair * 384 + (part + 1) * 128]
                out_ref[:, pl.ds(at + part * 1024 + pair * 128, 128)] = source.astype(jnp.float32)
        total = total + pieces[k][128:136, 384:].astype(jnp.float32)
    for i in range(18):
        vectors_ref[i:i + 1] = total[i // 3:i // 3 + 1, (i % 3) * 128:(i % 3 + 1) * 128]


def spread_middle_body(core_ref, *refs):
    (early, early_other, late, late_other), (memory_ref, query_ref, cross_ref, self_ref) = refs[:4], refs[4:]
    for index, first, second in ((core_ref[0], early, late), (1 - core_ref[0], early_other, late_other)):
        for half, source in ((0, first), (512, second)):
            at = pl.multiple_of(half + index * 256, 256)
            memory_ref[:, pl.ds(at, 256)] = source[:, 0:256].astype(jnp.float32)
            memory_ref[:, pl.ds(at + 1024, 256)] = source[:, 256:512].astype(jnp.float32)
            query_ref[:, pl.ds(at, 256)] = source[:, 512:768].astype(jnp.float32)
        at = pl.multiple_of(index * 512, 512)
        cross_ref[:, pl.ds(at, 512)] = first[:, 768:].astype(jnp.float32)
        self_ref[:, pl.ds(at, 512)] = second[:, 768:].astype(jnp.float32)


def spread(body, index, pieces, shapes):
    whole = pl.BlockSpec(memory_space=pltpu.VMEM)
    moved = sum(p.size * 2 for p in pieces) + sum(a * b * 4 for a, b in shapes)
    return pl.pallas_call(
        body,
        in_specs=[pl.BlockSpec(memory_space=pltpu.SMEM)] + [whole] * len(pieces),
        out_specs=[whole] * len(shapes),
        out_shape=[jax.ShapeDtypeStruct(shape, jnp.float32) for shape in shapes],
        compiler_params=pltpu.CompilerParams(vmem_limit_bytes=moved + (4 << 20)),
        cost_estimate=pl.CostEstimate(flops=0, transcendentals=0, bytes_accessed=moved),
    )(index.reshape(1).astype(jnp.int32), *pieces)


def chip_sums(terms, rows):
    pairs = terms.reshape(2, 2, rows, terms.shape[1])
    got = to_core(pairs[:, 1])
    return pairs[0, 0].astype(jnp.float32) + got[0].astype(jnp.float32), added(pairs[1, 0], got[1])


def tiled_shards(
    tokens,
    memory,
    cotangent,
    block_map,
    block_order,
    self_projection,
    self_output,
    self_query_bias,
    self_value_bias,
    self_output_bias,
    first_gain,
    first_shift,
    cross_query,
    cross_memory,
    cross_output,
    cross_query_bias,
    cross_value_bias,
    cross_output_bias,
    second_gain,
    second_shift,
    expand_weight,
    reduce_weight,
    expand_bias,
    reduce_bias,
    third_gain,
    third_shift,
):
    bf16 = jnp.bfloat16
    f32 = jnp.float32
    own_rows = tokens[0]
    rows, width = own_rows.shape
    me_c, me_f = lax.axis_index("ctx"), lax.axis_index("fsdp")
    core, line, z, x = me_c % 2, me_c // 2, me_f // 2, me_f % 2
    share = width // 4

    def dot(left, right):
        return jnp.dot(left, right, preferred_element_type=f32)

    vectors = [self_query_bias, self_value_bias, self_output_bias, first_gain, first_shift, cross_query_bias,
               cross_value_bias, cross_output_bias, second_gain, second_shift, reduce_bias, third_gain, third_shift]
    vectors += [expand_bias[i * 128:(i + 1) * 128] for i in range(4)] + [jnp.zeros((128,), bf16)]
    vector_rows = jnp.stack([jnp.concatenate(vectors[i * 6:i * 6 + 6]) for i in range(3)])
    columns = [lax.dynamic_slice(self_projection, (0, part * width + me_c * share), (128, share)) for part in range(3)]
    own_piece = jnp.concatenate([jnp.concatenate(columns, axis=1), vector_rows, jnp.zeros((13, 3 * share), bf16)])
    projection_pieces = fsdp_pieces(own_piece)
    rows_y = to_y(own_rows)
    rows_core = to_core(own_rows)
    rows_diagonal = to_core(after(rows_y, projection_pieces[1:4]))
    sequence = jnp.concatenate([own_rows, rows_core, rows_y, rows_diagonal])
    sources = fsdp_sources(me_f)
    projection, vector_blocks = place(projection_pieces, sources, ((None, 0, 128), (None, 128, 16)))
    vector_blocks = vector_blocks.reshape(8, 16, 3 * share).astype(f32)
    gathered = [vector_blocks[:, i // 6, (i % 6) * 128:(i % 6 + 1) * 128].reshape(width) for i in range(17)]
    (query_bias, value_bias, out_bias, gain_one, shift_one, cross_qbias, cross_vbias, cross_obias,
     gain_two, shift_two, reduce_bias_full, gain_three, shift_three) = gathered[:13]
    expand_bias_blocks = jnp.stack(gathered[13:]).reshape(4, 1, width)

    middle = [cross_memory[:, :width], cross_memory[:, width:], self_output, cross_query, cross_output]
    middle_own = jnp.stack([lax.dynamic_slice_in_dim(weight, me_c * 32, 32) for weight in middle])
    middle_all = lax.all_gather(middle_own, ("fsdp", "ctx"), axis=0)
    memory_key_full, memory_value_full, self_out_full, cross_query_full, cross_out_full = [
        middle_all[:, i].reshape(width, width) for i in range(5)
    ]
    expand_columns = lax.dynamic_index_in_dim(expand_weight.reshape(128, 8, 4, 128), me_c, 2, keepdims=False)
    feed_own = jnp.concatenate([expand_columns.reshape(128, width), lax.dynamic_slice_in_dim(reduce_weight, me_c * 128, 128)])

    memory_rows = memory[0]
    memory_y = to_y(after(memory_rows, projection_pieces[4:]))
    memory_core = to_core(memory_rows)

    projected = dot(sequence, projection)
    bias = jnp.concatenate([
        lax.dynamic_slice_in_dim(query_bias, me_c * share, share),
        jnp.zeros((share,), f32),
        lax.dynamic_slice_in_dim(value_bias, me_c * share, share),
    ])
    qkv = (projected + bias).astype(bf16)
    scalars = (block_order[0], block_map[0].reshape(-1), me_c.reshape(1).astype(jnp.int32))
    heads_out, self_lse = attention_forward(qkv, 0, [qkv], 1, [qkv], 2, share, scalars, BLK)
    heads_out, memory_y = lax.optimization_barrier((heads_out, memory_y))
    memory_all = jnp.concatenate([memory_rows, memory_core, memory_y, to_core(memory_y)])

    feed_weights = lax.all_gather(after(feed_own, (middle_all, heads_out)), ("fsdp", "ctx"), axis=0, tiled=True)
    memory_keys = dot(memory_all, memory_key_full).astype(bf16)
    memory_values = (dot(memory_all, memory_value_full) + cross_vbias).astype(bf16)

    pieces = [heads_out[i * rows:(i + 1) * rows] for i in range(4)]
    others = after([to_core(pieces[1]), to_y(pieces[2]), to_diagonal(pieces[3])], (memory_keys, memory_values))
    arrived = jnp.stack([pieces[0]] + others)
    attended = jnp.concatenate([part_of(arrived, n ^ me_c, 0) for n in range(4)], axis=1)
    branch = dot(attended, self_out_full) + out_bias
    hidden_one, normed_one, inverse_one = layer_norm(residual_scale * own_rows.astype(f32) + branch, gain_one, shift_one)

    hidden_low = hidden_one.astype(bf16)
    cross_queries = (dot(hidden_low, cross_query_full) + cross_qbias).astype(bf16)
    cross_low, cross_lse = attention_forward(cross_queries, 0, [memory_keys], 0, [memory_values], 0, width, None, rows)
    cross_branch = dot(cross_low, cross_out_full) + cross_obias
    hidden_two, normed_two, inverse_two = layer_norm(residual_scale * hidden_one + cross_branch, gain_two, shift_two)

    feed_vectors = jnp.concatenate([jnp.stack([reduce_bias_full, gain_three, shift_three]), jnp.zeros((5, width), f32)])
    output, grad_hidden_two, feed_send, feed_keep, grad_expand_bias, feed_sums = feed_forward(
        core, hidden_two, cotangent[0], feed_weights.reshape(8, 4, 256, width), expand_bias_blocks, feed_vectors
    )
    feed_got = to_core(feed_send)

    grad_second, grad_second_gain, grad_second_shift = layer_norm_back(grad_hidden_two, gain_two, normed_two, inverse_two)
    grad_cross_branch = grad_second.astype(bf16)
    grad_cross_output_bias = jnp.sum(grad_cross_branch.astype(f32), axis=0)
    grad_cross_low = dot(grad_cross_branch, cross_out_full.T).astype(bf16)

    def cross_half(half, queries):
        return attention_backward(
            queries, 2 * half, grad_cross_low, cross_low, cross_lse, [memory_keys], 2 * half, [memory_values], 2 * half,
            width // 2, None, rows, o_col=2 * half
        )

    def line_split(summed):
        return summed.reshape(8, 2, 64, summed.shape[1])

    early_q, early_k, early_v = cross_half(0, cross_queries)
    feed_keep, feed_got = after((feed_keep, feed_got), early_q)
    feed_half = added(feed_keep, feed_got).reshape(8 * 512, width)
    feed_share = lax.psum_scatter(feed_half, "fsdp", scatter_dimension=0, tiled=True)
    first_q, first_k, first_v = after((early_q, early_k, early_v), feed_half)
    keep, send = halves_dot(
        [(memory_all, first_k), (memory_all, first_v), (hidden_low, first_q), (cross_low, grad_cross_branch)], core
    )
    early_got = to_core(send)
    late_q, late_k, late_v = cross_half(1, after(cross_queries, (keep, send)))
    late_q, late_k, late_v, early_got = lax.optimization_barrier((late_q, late_k, late_v, early_got))
    early = line_split(added(keep, early_got))
    early_send = part_of(early, line ^ 1, 1)
    early_got = to_y(early_send)
    late_q, early_q = after((late_q, early_q), early_send)

    grad_cross_queries = jnp.concatenate([early_q, late_q], axis=1)
    grad_cross_query_bias = jnp.sum(grad_cross_queries.astype(f32), axis=0)
    grad_hidden_one = residual_scale * grad_second + dot(grad_cross_queries, cross_query_full.T)
    grad_first, grad_first_gain, grad_first_shift = layer_norm_back(grad_hidden_one, gain_one, normed_one, inverse_one)
    grad_branch = grad_first.astype(bf16)
    grad_self_output_bias = jnp.sum(grad_branch.astype(f32), axis=0)
    grad_attended = dot(grad_branch, self_out_full.T).astype(bf16)
    by_heads = jnp.stack([grad_attended[:, i * share:(i + 1) * share] for i in range(4)])
    sends = [part_of(by_heads, k ^ me_c, 0) for k in range(4)]
    received = [to_core(sends[1]), to_y(sends[2]), to_diagonal(sends[3])]
    heads_grad = jnp.concatenate([sends[0]] + received)

    ready_q, ready_k, ready_v, ready_branch = after((late_q, late_k, late_v, grad_branch), received[0])
    grad_cross_value_bias = jnp.concatenate([jnp.sum(early_v.astype(f32), axis=0), jnp.sum(ready_v.astype(f32), axis=0)])
    memory_terms = dot(jnp.concatenate([early_k, early_v, ready_k, ready_v], axis=1), jnp.concatenate([
        memory_key_full[:, :width // 2], memory_value_full[:, :width // 2],
        memory_key_full[:, width // 2:], memory_value_full[:, width // 2:],
    ], axis=1).T).astype(bf16)
    memory_near, memory_far = chip_sums(memory_terms, rows)
    late_keep, late_send = halves_dot(
        [(memory_all, ready_k), (memory_all, ready_v), (hidden_low, ready_q), (attended, ready_branch)], core
    )
    late_got = to_core(late_send)
    early = added(part_of(early, line, 1), early_got).reshape(4, 2, 64, 5 * share)

    def heads_back(pair, upstream):
        return attention_backward(
            qkv, pair, upstream, heads_out, self_lse, [qkv], 2 + pair, [qkv], 4 + pair, share // 2, scalars, BLK,
            units=1, o_col=pair,
        )

    def own_blocks(grads):
        return dot(sequence.T, grads).astype(bf16).reshape(8, 128, grads.shape[1])

    heads_grad = after(heads_grad, (early, late_keep, late_send, memory_far))
    memory_got = to_y(memory_far)
    early_got = to_x(part_of(early, x ^ 1, 1))
    first_heads = jnp.concatenate(heads_back(0, heads_grad), axis=1)
    first_heads, early_got, late_got = lax.optimization_barrier((first_heads, early_got, late_got))
    first_blocks = own_blocks(first_heads)
    late = added(late_keep, late_got).reshape(4, 2, 128, 5 * share)
    late_got = to_x(part_of(late, x ^ 1, 1))
    early = added(part_of(early, x, 1), early_got)
    early_sends = [part_of(early, z ^ k, 0) for k in (1, 2, 3)]
    first_total = from_fsdp(first_blocks)
    second_heads = jnp.concatenate(heads_back(1, after(heads_grad, (first_blocks, late, early_sends))), axis=1)
    early_pieces = [to_z(piece, k) for piece, k in zip(early_sends, (1, 2, 3))]
    second_heads, early_pieces, late_got, memory_got, feed_share = lax.optimization_barrier(
        (second_heads, early_pieces, late_got, memory_got, feed_share)
    )
    second_blocks = own_blocks(second_heads)
    ready_first, ready_second = after((first_heads, second_heads), second_blocks)
    token_terms = (
        dot(ready_first, jnp.concatenate([projection[:, i * share:i * share + 128] for i in range(3)], axis=1).T)
        + dot(ready_second, jnp.concatenate([projection[:, i * share + 128:(i + 1) * share] for i in range(3)], axis=1).T)
    ).astype(bf16)
    token_near, token_far = chip_sums(token_terms, rows)
    token_got = to_y(token_far)
    token_grad = (residual_scale * grad_first + token_near + token_got.astype(f32))[None]
    memory_grad = (memory_near + memory_got.astype(f32))[None]

    both_heads = [first_heads.astype(f32), second_heads.astype(f32)]
    head_sums = jnp.stack([
        jnp.concatenate([jnp.sum(half[:, at:at + 128], axis=0) for half in both_heads]) for at in (0, 256)
    ])
    head_sums = lax.dynamic_update_slice(jnp.zeros((2, width), f32), head_sums, (0, me_c * share))
    vector_grads = jnp.concatenate([
        jnp.stack([
            grad_self_output_bias, grad_first_gain, grad_first_shift, grad_cross_query_bias, grad_cross_value_bias,
            grad_cross_output_bias, grad_second_gain, grad_second_shift,
        ]),
        feed_sums[:3],
        grad_expand_bias.reshape(4, width),
        head_sums,
        jnp.zeros((1, width), f32),
    ])
    vector_rows = vector_grads.reshape(6, 3, 8, 128).transpose(2, 0, 1, 3).reshape(8, 6, 384).astype(bf16)
    blocks = jnp.concatenate([second_blocks, vector_rows, jnp.zeros((8, 10, 384), bf16)], axis=1)
    second_total = from_fsdp(blocks)
    padded = jnp.concatenate([first_total, jnp.zeros((16, 384), f32)])
    total = after(jnp.concatenate([padded, second_total], axis=1).astype(bf16), token_got)

    early = part_of(early, z, 0).astype(f32)
    for piece in early_pieces:
        early = early + piece.astype(f32)
    early = early.astype(bf16)
    late = over_z(added(after(part_of(late, x, 1), (blocks, token_far)), late_got)[None], z)[0]
    early_got = to_y(early)
    early = jnp.concatenate([jnp.where(line == 0, early, early_got), jnp.where(line == 0, early_got, early)])
    late = added(late, to_y(late))
    grad_cross_memory, grad_cross_query, grad_cross_output, grad_self_output = spread(
        spread_middle_body, core, [early, to_core(early), late, to_core(late)],
        [(128, 2 * width), (128, width), (128, width), (128, width)],
    )

    grad_self_projection, sums = spread(
        spread_projection_body, me_c, ctx_pieces(total), [(128, 3 * width), (18, 128)]
    )

    feed_share = after(feed_share, (blocks, token_far))
    feed_own = added(feed_share, to_y(feed_share)).reshape(2, 256, width)
    grad_expand, grad_reduce = spread(spread_feed_body, core, [feed_own, to_core(feed_own)], [(128, 4 * width), (512, width)])

    return (
        output[None],
        token_grad,
        memory_grad,
        grad_self_projection,
        grad_self_output,
        sums[15],
        sums[16],
        sums[0],
        sums[1],
        sums[2],
        grad_cross_query,
        grad_cross_memory,
        grad_cross_output,
        sums[3],
        sums[4],
        sums[5],
        sums[6],
        sums[7],
        grad_expand,
        grad_reduce,
        sums[11:15].reshape(512),
        sums[8],
        sums[9],
        sums[10],
    )


def head_split(matrix):
    return matrix.reshape(matrix.shape[0], HEADS, HEAD_DIM)


def piece_size(length):
    return min(512, length)


def piece_masks(key_blocks, allowed_rows):
    length = key_blocks.shape[0]
    piece = piece_size(length)
    count = length // piece
    if allowed_rows is None:
        return jnp.ones((count, 1, 1), jnp.bool_)
    nblocks = allowed_rows.shape[1]
    onehot = (key_blocks[:, None] == jnp.arange(nblocks, dtype=jnp.int32)[None, :]).astype(
        jnp.float32
    )
    live = jnp.dot(allowed_rows, onehot.T) > 0.5
    return jnp.moveaxis(live.reshape(live.shape[0], count, piece), 1, 0)


def masked_scores(query_heads, key_piece, live):
    scores = (
        jnp.einsum("qhd,khd->hqk", query_heads, key_piece, preferred_element_type=jnp.float32)
        * score_scale
    )
    return jnp.where(live[None], scores, masked_score)


def run_guarded(guarded, live, work, fallback):
    if guarded:
        return lax.cond(jnp.any(live), work, lambda unused: fallback, live)
    return work(live)


def attend_forward(query_heads, key_heads, value_heads, live_pieces, guarded):
    count = live_pieces.shape[0]
    piece = key_heads.shape[0] // count
    key_pieces = key_heads.reshape((count, piece) + key_heads.shape[1:])
    value_pieces = value_heads.reshape((count, piece) + value_heads.shape[1:])
    rows = query_heads.shape[0]

    def first_step(carry, inputs):
        run_max, run_sum = carry
        key_piece, live = inputs

        def work(live_now):
            scores = masked_scores(query_heads, key_piece, live_now)
            new_max = jnp.maximum(run_max, jnp.max(scores, axis=-1))
            shifted = jnp.where(live_now[None], jnp.exp(scores - new_max[:, :, None]), 0.0)
            return (new_max, run_sum * jnp.exp(run_max - new_max) + jnp.sum(shifted, axis=-1))

        return (run_guarded(guarded, live, work, (run_max, run_sum)), None)

    start = (
        jnp.full((HEADS, rows), masked_score, jnp.float32),
        jnp.zeros((HEADS, rows), jnp.float32),
    )
    (final_max, final_sum), unused = lax.scan(first_step, start, (key_pieces, live_pieces))
    log_total = final_max + jnp.log(final_sum)

    def second_step(total, inputs):
        key_piece, value_piece, live = inputs

        def work(live_now):
            scores = masked_scores(query_heads, key_piece, live_now)
            probs = jnp.exp(scores - log_total[:, :, None]).astype(jnp.bfloat16)
            return total + jnp.einsum(
                "hqk,khd->qhd", probs, value_piece, preferred_element_type=jnp.float32
            )

        return (run_guarded(guarded, live, work, total), None)

    empty = jnp.zeros((rows, HEADS, HEAD_DIM), jnp.float32)
    attended, unused = lax.scan(second_step, empty, (key_pieces, value_pieces, live_pieces))
    return (attended, log_total)


def attend_backward(
    query_heads, key_heads, value_heads, log_total, grad_heads, delta, live_pieces, guarded
):
    count = live_pieces.shape[0]
    piece = key_heads.shape[0] // count
    key_pieces = key_heads.reshape((count, piece) + key_heads.shape[1:])
    value_pieces = value_heads.reshape((count, piece) + value_heads.shape[1:])
    rows = query_heads.shape[0]
    blank = jnp.zeros((piece, HEADS, HEAD_DIM), jnp.float32)

    def back_step(grad_query, inputs):
        key_piece, value_piece, live = inputs

        def work(live_now):
            scores = masked_scores(query_heads, key_piece, live_now)
            probs = jnp.exp(scores - log_total[:, :, None])
            grad_probs = jnp.einsum(
                "qhd,khd->hqk", grad_heads, value_piece, preferred_element_type=jnp.float32
            )
            grad_scores = (probs * (grad_probs - delta[:, :, None])).astype(jnp.bfloat16)
            new_query = (
                grad_query
                + jnp.einsum(
                    "hqk,khd->qhd", grad_scores, key_piece, preferred_element_type=jnp.float32
                )
                * score_scale
            )
            grad_key = (
                jnp.einsum(
                    "hqk,qhd->khd", grad_scores, query_heads, preferred_element_type=jnp.float32
                )
                * score_scale
            )
            grad_value = jnp.einsum(
                "hqk,qhd->khd",
                probs.astype(jnp.bfloat16),
                grad_heads,
                preferred_element_type=jnp.float32,
            )
            return (new_query, (grad_key, grad_value))

        return run_guarded(guarded, live, work, (grad_query, (blank, blank)))

    empty = jnp.zeros((rows, HEADS, HEAD_DIM), jnp.float32)
    grad_query, (key_grads, value_grads) = lax.scan(
        back_step, empty, (key_pieces, value_pieces, live_pieces)
    )
    width = HEADS * HEAD_DIM
    return (
        grad_query.reshape(rows, width),
        key_grads.reshape(-1, width),
        value_grads.reshape(-1, width),
    )


def plain_shards(
    tokens,
    memory,
    cotangent,
    block_map,
    block_order,
    self_projection,
    self_output,
    self_query_bias,
    self_value_bias,
    self_output_bias,
    first_gain,
    first_shift,
    cross_query,
    cross_memory,
    cross_output,
    cross_query_bias,
    cross_value_bias,
    cross_output_bias,
    second_gain,
    second_shift,
    expand_weight,
    reduce_weight,
    expand_bias,
    reduce_bias,
    third_gain,
    third_shift,
):
    bf16 = jnp.bfloat16
    f32 = jnp.float32
    rows_in = tokens[0]
    rows = rows_in.shape[0]
    width = rows_in.shape[1]
    ctx_count = lax.axis_size("ctx")
    slot = lax.axis_index("ctx")
    positions = jnp.arange(rows * ctx_count, dtype=jnp.int32)
    group_index = positions // rows
    group_match = group_index[:, None] == jnp.arange(ctx_count, dtype=jnp.int32)[None, :]
    group_place = jnp.sum(jnp.where(group_match, block_order[0][None, :], 0), axis=1)
    key_blocks = (group_place * rows + positions % rows) // BLK
    own_blocks = lax.dynamic_slice_in_dim(key_blocks, slot * rows, rows)
    nblocks = block_map.shape[1]
    own_onehot = (own_blocks[:, None] == jnp.arange(nblocks, dtype=jnp.int32)[None, :]).astype(f32)
    allowed_rows = jnp.dot(own_onehot, block_map[0].astype(f32))
    self_live = piece_masks(key_blocks, allowed_rows)
    (
        projection_full,
        self_out_full,
        query_bias_full,
        value_bias_full,
        out_bias_full,
        gain_one,
        shift_one,
    ) = (
        lax.all_gather(self_projection, "fsdp", axis=0, tiled=True),
        lax.all_gather(self_output, "fsdp", axis=0, tiled=True),
        lax.all_gather(self_query_bias, "fsdp", axis=0, tiled=True),
        lax.all_gather(self_value_bias, "fsdp", axis=0, tiled=True),
        lax.all_gather(self_output_bias, "fsdp", axis=0, tiled=True),
        lax.all_gather(first_gain, "fsdp", axis=0, tiled=True),
        lax.all_gather(first_shift, "fsdp", axis=0, tiled=True),
    )
    projected = jnp.dot(rows_in, projection_full, preferred_element_type=f32)
    queries = (projected[:, :width] + query_bias_full).astype(bf16)
    keys_own = projected[:, width : 2 * width].astype(bf16)
    values_own = (projected[:, 2 * width :] + value_bias_full).astype(bf16)
    keys_all, values_all = (
        lax.all_gather(keys_own, "ctx", axis=0, tiled=True),
        lax.all_gather(values_own, "ctx", axis=0, tiled=True),
    )
    query_heads = head_split(queries)
    key_heads = head_split(keys_all)
    value_heads = head_split(values_all)
    attended, self_total = attend_forward(query_heads, key_heads, value_heads, self_live, True)
    attended_low = attended.reshape(rows, width).astype(bf16)
    branch = jnp.dot(attended_low, self_out_full, preferred_element_type=f32) + out_bias_full
    hidden_one, normed_one, inverse_one = layer_norm(
        residual_scale * rows_in.astype(f32) + branch, gain_one, shift_one
    )
    (
        cross_query_full,
        cross_memory_full,
        cross_out_full,
        cross_qbias_full,
        cross_vbias_full,
        cross_obias_full,
        gain_two,
        shift_two,
    ) = (
        lax.all_gather(cross_query, "fsdp", axis=0, tiled=True),
        lax.all_gather(cross_memory, "fsdp", axis=0, tiled=True),
        lax.all_gather(cross_output, "fsdp", axis=0, tiled=True),
        lax.all_gather(cross_query_bias, "fsdp", axis=0, tiled=True),
        lax.all_gather(cross_value_bias, "fsdp", axis=0, tiled=True),
        lax.all_gather(cross_output_bias, "fsdp", axis=0, tiled=True),
        lax.all_gather(second_gain, "fsdp", axis=0, tiled=True),
        lax.all_gather(second_shift, "fsdp", axis=0, tiled=True),
    )
    hidden_low = hidden_one.astype(bf16)
    cross_queries = (
        jnp.dot(hidden_low, cross_query_full, preferred_element_type=f32) + cross_qbias_full
    ).astype(bf16)
    memory_rows = memory[0]
    memory_proj = jnp.dot(memory_rows, cross_memory_full, preferred_element_type=f32)
    memory_keys = memory_proj[:, :width].astype(bf16)
    memory_values = (memory_proj[:, width:] + cross_vbias_full).astype(bf16)
    memory_keys_all, memory_values_all = (
        lax.all_gather(memory_keys, "ctx", axis=0, tiled=True),
        lax.all_gather(memory_values, "ctx", axis=0, tiled=True),
    )
    cross_heads = head_split(cross_queries)
    memory_key_heads = head_split(memory_keys_all)
    memory_value_heads = head_split(memory_values_all)
    cross_live = piece_masks(jnp.zeros((memory_keys_all.shape[0],), jnp.int32), None)
    cross_attended, cross_total = attend_forward(
        cross_heads, memory_key_heads, memory_value_heads, cross_live, False
    )
    cross_low = cross_attended.reshape(rows, width).astype(bf16)
    cross_branch = jnp.dot(cross_low, cross_out_full, preferred_element_type=f32) + cross_obias_full
    hidden_two, normed_two, inverse_two = layer_norm(
        residual_scale * hidden_one + cross_branch, gain_two, shift_two
    )
    expand_full, reduce_full, expand_bias_full, reduce_bias_full, gain_three, shift_three = (
        lax.all_gather(expand_weight, "fsdp", axis=0, tiled=True),
        lax.all_gather(reduce_weight, "fsdp", axis=0, tiled=True),
        lax.all_gather(expand_bias, "fsdp", axis=0, tiled=True),
        lax.all_gather(reduce_bias, "fsdp", axis=0, tiled=True),
        lax.all_gather(third_gain, "fsdp", axis=0, tiled=True),
        lax.all_gather(third_shift, "fsdp", axis=0, tiled=True),
    )
    hidden_two_low = hidden_two.astype(bf16)
    expanded = jnp.dot(hidden_two_low, expand_full, preferred_element_type=f32) + expand_bias_full
    activated = gelu_tanh(expanded).astype(bf16)
    reduced = jnp.dot(activated, reduce_full, preferred_element_type=f32) + reduce_bias_full
    result, normed_three, inverse_three = layer_norm(
        residual_scale * hidden_two + reduced, gain_three, shift_three
    )
    output = result.astype(bf16)[None]
    upstream = cotangent[0].astype(f32)
    grad_third, grad_third_gain, grad_third_shift = layer_norm_back(
        upstream, gain_three, normed_three, inverse_three
    )
    grad_reduced = grad_third.astype(bf16)
    grad_reduce_bias = jnp.sum(grad_reduced.astype(f32), axis=0)
    grad_reduce_weight = jnp.dot(activated.T, grad_reduced, preferred_element_type=f32)
    grad_activated = jnp.dot(grad_reduced, reduce_full.T, preferred_element_type=f32)
    grad_expanded = (grad_activated * gelu_slope(expanded)).astype(bf16)
    grad_expand_bias = jnp.sum(grad_expanded.astype(f32), axis=0)
    grad_expand_weight = jnp.dot(hidden_two_low.T, grad_expanded, preferred_element_type=f32)
    grad_hidden_two = residual_scale * grad_third + jnp.dot(
        grad_expanded, expand_full.T, preferred_element_type=f32
    )
    grad_second, grad_second_gain, grad_second_shift = layer_norm_back(
        grad_hidden_two, gain_two, normed_two, inverse_two
    )
    grad_cross_branch = grad_second.astype(bf16)
    grad_cross_output_bias = jnp.sum(grad_cross_branch.astype(f32), axis=0)
    grad_cross_output = jnp.dot(cross_low.T, grad_cross_branch, preferred_element_type=f32)
    grad_cross_low = jnp.dot(
        grad_cross_branch, cross_out_full.T, preferred_element_type=f32
    ).astype(bf16)
    grad_cross_heads = head_split(grad_cross_low)
    cross_delta = jnp.sum(grad_cross_heads.astype(f32) * cross_attended, axis=-1).T
    grad_cross_queries, memory_key_terms, memory_value_terms = attend_backward(
        cross_heads,
        memory_key_heads,
        memory_value_heads,
        cross_total,
        grad_cross_heads,
        cross_delta,
        cross_live,
        False,
    )
    grad_memory_keys, grad_memory_values = (
        lax.psum_scatter(
            memory_key_terms.astype(jnp.bfloat16), "ctx", scatter_dimension=0, tiled=True
        ).astype(jnp.float32),
        lax.psum_scatter(
            memory_value_terms.astype(jnp.bfloat16), "ctx", scatter_dimension=0, tiled=True
        ).astype(jnp.float32),
    )
    grad_memory_pair = jnp.concatenate(
        [grad_memory_keys.astype(bf16), grad_memory_values.astype(bf16)], axis=1
    )
    grad_cross_value_bias = jnp.sum(grad_memory_pair[:, width:].astype(f32), axis=0)
    grad_cross_memory = jnp.dot(memory_rows.T, grad_memory_pair, preferred_element_type=f32)
    memory_grad = jnp.dot(grad_memory_pair, cross_memory_full.T, preferred_element_type=f32)[None]
    grad_cross_low_queries = grad_cross_queries.astype(bf16)
    grad_cross_query_bias = jnp.sum(grad_cross_low_queries.astype(f32), axis=0)
    grad_cross_query = jnp.dot(hidden_low.T, grad_cross_low_queries, preferred_element_type=f32)
    grad_hidden_one = residual_scale * grad_second + jnp.dot(
        grad_cross_low_queries, cross_query_full.T, preferred_element_type=f32
    )
    grad_first, grad_first_gain, grad_first_shift = layer_norm_back(
        grad_hidden_one, gain_one, normed_one, inverse_one
    )
    grad_branch = grad_first.astype(bf16)
    grad_self_output_bias = jnp.sum(grad_branch.astype(f32), axis=0)
    grad_self_output = jnp.dot(attended_low.T, grad_branch, preferred_element_type=f32)
    grad_attended = jnp.dot(grad_branch, self_out_full.T, preferred_element_type=f32).astype(bf16)
    grad_attended_heads = head_split(grad_attended)
    self_delta = jnp.sum(grad_attended_heads.astype(f32) * attended, axis=-1).T
    grad_queries, key_terms, value_terms = attend_backward(
        query_heads,
        key_heads,
        value_heads,
        self_total,
        grad_attended_heads,
        self_delta,
        self_live,
        True,
    )
    grad_keys, grad_values = (
        lax.psum_scatter(
            key_terms.astype(jnp.bfloat16), "ctx", scatter_dimension=0, tiled=True
        ).astype(jnp.float32),
        lax.psum_scatter(
            value_terms.astype(jnp.bfloat16), "ctx", scatter_dimension=0, tiled=True
        ).astype(jnp.float32),
    )
    grad_projected = jnp.concatenate(
        [grad_queries.astype(bf16), grad_keys.astype(bf16), grad_values.astype(bf16)], axis=1
    )
    grad_self_query_bias = jnp.sum(grad_projected[:, :width].astype(f32), axis=0)
    grad_self_value_bias = jnp.sum(grad_projected[:, 2 * width :].astype(f32), axis=0)
    grad_self_projection = jnp.dot(rows_in.T, grad_projected, preferred_element_type=f32)
    token_grad = (
        residual_scale * grad_first
        + jnp.dot(grad_projected, projection_full.T, preferred_element_type=f32)
    )[None]
    shares = (
        lax.psum_scatter(
            grad_self_projection.astype(jnp.bfloat16), "fsdp", scatter_dimension=0, tiled=True
        ).astype(jnp.float32),
        lax.psum_scatter(
            grad_self_output.astype(jnp.bfloat16), "fsdp", scatter_dimension=0, tiled=True
        ).astype(jnp.float32),
        lax.psum_scatter(
            grad_self_query_bias.astype(jnp.bfloat16), "fsdp", scatter_dimension=0, tiled=True
        ).astype(jnp.float32),
        lax.psum_scatter(
            grad_self_value_bias.astype(jnp.bfloat16), "fsdp", scatter_dimension=0, tiled=True
        ).astype(jnp.float32),
        lax.psum_scatter(
            grad_self_output_bias.astype(jnp.bfloat16), "fsdp", scatter_dimension=0, tiled=True
        ).astype(jnp.float32),
        lax.psum_scatter(
            grad_first_gain.astype(jnp.bfloat16), "fsdp", scatter_dimension=0, tiled=True
        ).astype(jnp.float32),
        lax.psum_scatter(
            grad_first_shift.astype(jnp.bfloat16), "fsdp", scatter_dimension=0, tiled=True
        ).astype(jnp.float32),
        lax.psum_scatter(
            grad_cross_query.astype(jnp.bfloat16), "fsdp", scatter_dimension=0, tiled=True
        ).astype(jnp.float32),
        lax.psum_scatter(
            grad_cross_memory.astype(jnp.bfloat16), "fsdp", scatter_dimension=0, tiled=True
        ).astype(jnp.float32),
        lax.psum_scatter(
            grad_cross_output.astype(jnp.bfloat16), "fsdp", scatter_dimension=0, tiled=True
        ).astype(jnp.float32),
        lax.psum_scatter(
            grad_cross_query_bias.astype(jnp.bfloat16), "fsdp", scatter_dimension=0, tiled=True
        ).astype(jnp.float32),
        lax.psum_scatter(
            grad_cross_value_bias.astype(jnp.bfloat16), "fsdp", scatter_dimension=0, tiled=True
        ).astype(jnp.float32),
        lax.psum_scatter(
            grad_cross_output_bias.astype(jnp.bfloat16), "fsdp", scatter_dimension=0, tiled=True
        ).astype(jnp.float32),
        lax.psum_scatter(
            grad_second_gain.astype(jnp.bfloat16), "fsdp", scatter_dimension=0, tiled=True
        ).astype(jnp.float32),
        lax.psum_scatter(
            grad_second_shift.astype(jnp.bfloat16), "fsdp", scatter_dimension=0, tiled=True
        ).astype(jnp.float32),
        lax.psum_scatter(
            grad_expand_weight.astype(jnp.bfloat16), "fsdp", scatter_dimension=0, tiled=True
        ).astype(jnp.float32),
        lax.psum_scatter(
            grad_reduce_weight.astype(jnp.bfloat16), "fsdp", scatter_dimension=0, tiled=True
        ).astype(jnp.float32),
        lax.psum_scatter(
            grad_expand_bias.astype(jnp.bfloat16), "fsdp", scatter_dimension=0, tiled=True
        ).astype(jnp.float32),
        lax.psum_scatter(
            grad_reduce_bias.astype(jnp.bfloat16), "fsdp", scatter_dimension=0, tiled=True
        ).astype(jnp.float32),
        lax.psum_scatter(
            grad_third_gain.astype(jnp.bfloat16), "fsdp", scatter_dimension=0, tiled=True
        ).astype(jnp.float32),
        lax.psum_scatter(
            grad_third_shift.astype(jnp.bfloat16), "fsdp", scatter_dimension=0, tiled=True
        ).astype(jnp.float32),
    )
    summed = (
        lax.psum(shares[0].astype(jnp.bfloat16), "ctx").astype(jnp.float32),
        lax.psum(shares[1].astype(jnp.bfloat16), "ctx").astype(jnp.float32),
        lax.psum(shares[2].astype(jnp.bfloat16), "ctx").astype(jnp.float32),
        lax.psum(shares[3].astype(jnp.bfloat16), "ctx").astype(jnp.float32),
        lax.psum(shares[4].astype(jnp.bfloat16), "ctx").astype(jnp.float32),
        lax.psum(shares[5].astype(jnp.bfloat16), "ctx").astype(jnp.float32),
        lax.psum(shares[6].astype(jnp.bfloat16), "ctx").astype(jnp.float32),
        lax.psum(shares[7].astype(jnp.bfloat16), "ctx").astype(jnp.float32),
        lax.psum(shares[8].astype(jnp.bfloat16), "ctx").astype(jnp.float32),
        lax.psum(shares[9].astype(jnp.bfloat16), "ctx").astype(jnp.float32),
        lax.psum(shares[10].astype(jnp.bfloat16), "ctx").astype(jnp.float32),
        lax.psum(shares[11].astype(jnp.bfloat16), "ctx").astype(jnp.float32),
        lax.psum(shares[12].astype(jnp.bfloat16), "ctx").astype(jnp.float32),
        lax.psum(shares[13].astype(jnp.bfloat16), "ctx").astype(jnp.float32),
        lax.psum(shares[14].astype(jnp.bfloat16), "ctx").astype(jnp.float32),
        lax.psum(shares[15].astype(jnp.bfloat16), "ctx").astype(jnp.float32),
        lax.psum(shares[16].astype(jnp.bfloat16), "ctx").astype(jnp.float32),
        lax.psum(shares[17].astype(jnp.bfloat16), "ctx").astype(jnp.float32),
        lax.psum(shares[18].astype(jnp.bfloat16), "ctx").astype(jnp.float32),
        lax.psum(shares[19].astype(jnp.bfloat16), "ctx").astype(jnp.float32),
        lax.psum(shares[20].astype(jnp.bfloat16), "ctx").astype(jnp.float32),
    )
    return (
        output,
        token_grad,
        memory_grad,
        summed[0],
        summed[1],
        summed[2],
        summed[3],
        summed[4],
        summed[5],
        summed[6],
        summed[7],
        summed[8],
        summed[9],
        summed[10],
        summed[11],
        summed[12],
        summed[13],
        summed[14],
        summed[15],
        summed[16],
        summed[17],
        summed[18],
        summed[19],
        summed[20],
    )


def solution(mesh):
    placed = (
        P("fsdp", "ctx", None),
        P("fsdp", "ctx", None),
        P("fsdp", "ctx", None),
        P("fsdp", None, None),
        P("fsdp", None),
        P("fsdp", None),
        P("fsdp", None),
        P("fsdp"),
        P("fsdp"),
        P("fsdp"),
        P("fsdp"),
        P("fsdp"),
        P("fsdp", None),
        P("fsdp", None),
        P("fsdp", None),
        P("fsdp"),
        P("fsdp"),
        P("fsdp"),
        P("fsdp"),
        P("fsdp"),
        P("fsdp", None),
        P("fsdp", None),
        P("fsdp"),
        P("fsdp"),
        P("fsdp"),
        P("fsdp"),
    )
    sizes = (mesh.shape["ctx"], mesh.shape["fsdp"])
    return jax.shard_map(
        tiled_shards if sizes == (4, 8) else plain_shards,
        mesh=mesh,
        in_specs=placed,
        out_specs=(
            P("fsdp", "ctx", None),
            P("fsdp", "ctx", None),
            P("fsdp", "ctx", None),
            P("fsdp", None),
            P("fsdp", None),
            P("fsdp"),
            P("fsdp"),
            P("fsdp"),
            P("fsdp"),
            P("fsdp"),
            P("fsdp", None),
            P("fsdp", None),
            P("fsdp", None),
            P("fsdp"),
            P("fsdp"),
            P("fsdp"),
            P("fsdp"),
            P("fsdp"),
            P("fsdp", None),
            P("fsdp", None),
            P("fsdp"),
            P("fsdp"),
            P("fsdp"),
            P("fsdp"),
        ),
        check_vma=False,
    )
```

```python
import functools
import math

import jax
import jax.numpy as jnp
from jax import lax
from jax.experimental import pallas as pl
from jax.experimental.layout import Layout, with_layout_constraint
from jax.experimental.pallas import tpu as pltpu
from jax.sharding import PartitionSpec as P

HEADS = 16
HEAD_DIM = 64
BLK = 256


epsilon = 1e-05
residual_scale = 18.0**0.25
score_scale = 0.125
masked_score = -1e30
gelu_coeff = math.sqrt(2.0 / math.pi)


def gelu_tanh(value):
    return 0.5 * value * (1.0 + jnp.tanh(gelu_coeff * (value + 0.044715 * value * value * value)))


def gelu_slope(value):
    inner = jnp.tanh(gelu_coeff * (value + 0.044715 * value * value * value))
    return 0.5 * (1.0 + inner) + 0.5 * value * (1.0 - inner * inner) * gelu_coeff * (
        1.0 + 3.0 * 0.044715 * value * value
    )


def layer_norm(summed, gain, shift):
    centred = summed - jnp.mean(summed, axis=-1, keepdims=True)
    inverse = lax.rsqrt(jnp.mean(centred * centred, axis=-1, keepdims=True) + epsilon)
    normed = centred * inverse
    return (normed * gain + shift, normed, inverse)


def layer_norm_back(upstream, gain, normed, inverse):
    scaled = upstream * gain
    inner = (
        scaled
        - jnp.mean(scaled, axis=-1, keepdims=True)
        - normed * jnp.mean(scaled * normed, axis=-1, keepdims=True)
    )
    return (inner * inverse, jnp.sum(upstream * normed, axis=0), jnp.sum(upstream, axis=0))


score_log2 = 0.125 * math.log2(math.e)
NT = (((1,), (1,)), ((), ()))
NN = (((1,), (0,)), ((), ()))
TN = (((0,), (0,)), ((), ()))


def mxu(left, right, dims):
    return lax.dot_general(left, right, dims, preferred_element_type=jnp.float32)


def two_heads(pair):
    low = lax.broadcasted_iota(jnp.int32, pair.shape, 1) < 64
    zero = jnp.zeros_like(pair)
    return jnp.concatenate([jnp.where(low, pair, zero), jnp.where(low, zero, pair)], axis=0)


def one_pair(stacked):
    rows = stacked.shape[0] // 2
    top = stacked[:rows]
    low = lax.broadcasted_iota(jnp.int32, top.shape, 1) < 64
    return jnp.where(low, top, stacked[rows:])


def place_of(order_ref, slot_ref, index, per_group):
    return order_ref[slot_ref[0] ^ (index // per_group)] * per_group + index % per_group


def seen(scalars, query_index, key_index, per_group, count):
    if scalars is None:
        return None
    order_ref, map_ref, slot_ref = scalars
    row = place_of(order_ref, slot_ref, query_index, per_group)
    column = place_of(order_ref, slot_ref, key_index, per_group)
    return map_ref[row * count + column] > 0


def guarded(flag, work):
    if flag is None:
        work()
    else:
        pl.when(flag)(work)


def pair_lanes(unit):
    return slice(unit * 128, (unit + 1) * 128)


def forward_body(masked, units, chunks, key_rows, pieces, per_group, *refs):
    scalars = None
    if masked:
        scalars, refs = refs[:3], refs[3:]
    q_ref, refs = refs[0], refs[1:]
    k_refs, v_refs, refs = refs[:pieces], refs[pieces:2 * pieces], refs[2 * pieces:]
    o_ref, lse_ref, stacked, scores, top, shift, total, acc = refs
    rows = stacked.shape[1]
    query_index = pl.program_id(1)

    def part(ref_list, chunk, unit):
        if pieces > 1:
            return ref_list[chunk][:, pair_lanes(unit)]
        return ref_list[0][chunk * key_rows:(chunk + 1) * key_rows, pair_lanes(unit)]

    for unit in range(units):
        stacked[unit] = two_heads(q_ref[:, pair_lanes(unit)])
        top[unit] = jnp.full((rows, 128), -1e30, jnp.float32)
        total[unit] = jnp.zeros((rows, 128), jnp.float32)
        acc[unit] = jnp.zeros((rows, 128), jnp.float32)
    for chunk in range(chunks):
        flag = seen(scalars, query_index, chunk, per_group, chunks)

        def scan_max(chunk=chunk):
            for unit in range(units):
                found = mxu(stacked[unit], part(k_refs, chunk, unit), NT)
                scores[unit, chunk] = found
                best = top[unit]
                for lane in range(0, key_rows, 128):
                    best = jnp.maximum(best, found[:, lane:lane + 128])
                top[unit] = best

        guarded(flag, scan_max)
    for unit in range(units):
        peak = jnp.max(top[unit], axis=1, keepdims=True) * score_log2
        shift[unit] = jnp.broadcast_to(peak, (rows, 128))
    for chunk in range(chunks):
        flag = seen(scalars, query_index, chunk, per_group, chunks)

        def weigh(chunk=chunk):
            for unit in range(units):
                found = scores[unit, chunk]
                offset = shift[unit]
                summed = total[unit]
                parts = []
                for lane in range(0, key_rows, 128):
                    weight = jnp.exp2(found[:, lane:lane + 128] * score_log2 - offset)
                    summed = summed + weight
                    parts.append(weight.astype(jnp.bfloat16))
                total[unit] = summed
                acc[unit] = acc[unit] + mxu(jnp.concatenate(parts, axis=1), part(v_refs, chunk, unit), NN)

        guarded(flag, weigh)
    for unit in range(units):
        row_sum = jnp.sum(total[unit], axis=1, keepdims=True)
        o_ref[:, pair_lanes(unit)] = one_pair(acc[unit] / row_sum).astype(o_ref.dtype)
        lse = shift[unit] + jnp.log2(row_sum)
        lse_ref[unit] = lse.T[:8]


def backward_body(masked, units, chunks, key_rows, pieces, per_group, *refs):
    scalars = None
    if masked:
        scalars, refs = refs[:3], refs[3:]
    q_ref, do_ref, o_ref, lse_ref, refs = refs[0], refs[1], refs[2], refs[3], refs[4:]
    k_refs, v_refs, refs = refs[:pieces], refs[pieces:2 * pieces], refs[2 * pieces:]
    dq_ref, dk_refs, dv_refs, refs = refs[0], refs[1:1 + pieces], refs[1 + pieces:1 + 2 * pieces], refs[1 + 2 * pieces:]
    stacked, grads, delta, dq_acc, dk_acc, dv_acc = refs
    query_index = pl.program_id(1)

    def part(ref_list, chunk, unit):
        if pieces > 1:
            return ref_list[chunk][:, pair_lanes(unit)]
        return ref_list[0][chunk * key_rows:(chunk + 1) * key_rows, pair_lanes(unit)]

    @pl.when(query_index == 0)
    def clear():
        dk_acc[...] = jnp.zeros_like(dk_acc)
        dv_acc[...] = jnp.zeros_like(dv_acc)

    for unit in range(units):
        lanes = pair_lanes(unit)
        stacked[unit] = two_heads(q_ref[:, lanes])
        upstream = do_ref[:, lanes]
        grads[unit] = two_heads(upstream)
        product = (upstream.astype(jnp.float32) * o_ref[:, lanes].astype(jnp.float32)).T
        first = jnp.sum(product[:64], axis=0, keepdims=True)
        second = jnp.sum(product[64:], axis=0, keepdims=True)
        delta[unit] = jnp.broadcast_to(jnp.concatenate([first, second], axis=1), delta.shape[1:])
        dq_acc[unit] = jnp.zeros(dq_acc.shape[1:], jnp.float32)
    for chunk in range(chunks):
        flag = seen(scalars, query_index, chunk, per_group, chunks)

        def step(chunk=chunk):
            for unit in range(units):
                queries, upstream = stacked[unit], grads[unit]
                keys, values = part(k_refs, chunk, unit), part(v_refs, chunk, unit)
                found = mxu(keys, queries, NT)
                probs = jnp.exp2(found * score_log2 - lse_ref[unit, 0:1])
                grad_probs = mxu(values, upstream, NT)
                grad_scores = (probs * (grad_probs - delta[unit, 0:1])).astype(jnp.bfloat16)
                dv_acc[unit, chunk] += mxu(probs.astype(jnp.bfloat16), upstream, NN)
                dk_acc[unit, chunk] += mxu(grad_scores, queries, NN)
                dq_acc[unit] += mxu(grad_scores, keys, TN)

        guarded(flag, step)
    for unit in range(units):
        dq_ref[:, pair_lanes(unit)] = (one_pair(dq_acc[unit]) * 0.125).astype(dq_ref.dtype)

    @pl.when(query_index == pl.num_programs(1) - 1)
    def finish():
        for unit in range(units):
            for chunk in range(chunks):
                if pieces > 1:
                    rows = slice(None)
                    dk_ref, dv_ref = dk_refs[chunk], dv_refs[chunk]
                else:
                    rows = slice(chunk * key_rows, (chunk + 1) * key_rows)
                    dk_ref, dv_ref = dk_refs[0], dv_refs[0]
                dk_ref[rows, pair_lanes(unit)] = (dk_acc[unit, chunk] * 0.125).astype(dk_ref.dtype)
                dv_ref[rows, pair_lanes(unit)] = dv_acc[unit, chunk].astype(dv_ref.dtype)


def attention_forward(q, q_col, k_list, k_col, v_list, v_col, width, scalars, key_rows, units=2, per_group=2):
    pieces = len(k_list)
    lanes = units * 128
    rows = q.shape[0]
    keys = sum(k.shape[0] for k in k_list)
    chunks = keys // key_rows
    groups, blocks = width // lanes, rows // BLK
    masked = scalars is not None
    spec_q = pl.BlockSpec((BLK, lanes), lambda h, i, *_: (i, q_col + h))
    specs_k = [pl.BlockSpec((k.shape[0], lanes), lambda h, i, *_: (0, k_col + h)) for k in k_list]
    specs_v = [pl.BlockSpec((v.shape[0], lanes), lambda h, i, *_: (0, v_col + h)) for v in v_list]
    body = functools.partial(forward_body, masked, units, chunks, key_rows, pieces, per_group)
    pairs = rows * keys * (width // 64)
    return pl.pallas_call(
        body,
        grid_spec=pltpu.PrefetchScalarGridSpec(
            num_scalar_prefetch=3 if masked else 0,
            grid=(groups, blocks),
            in_specs=[spec_q] + specs_k + specs_v,
            out_specs=[
                pl.BlockSpec((BLK, lanes), lambda h, i, *_: (i, h)),
                pl.BlockSpec((units, 8, 2 * BLK), lambda h, i, *_: (h, 0, i)),
            ],
            scratch_shapes=[
                pltpu.VMEM((units, 2 * BLK, 128), jnp.bfloat16),
                pltpu.VMEM((units, chunks, 2 * BLK, key_rows), jnp.float32),
                pltpu.VMEM((units, 2 * BLK, 128), jnp.float32),
                pltpu.VMEM((units, 2 * BLK, 128), jnp.float32),
                pltpu.VMEM((units, 2 * BLK, 128), jnp.float32),
                pltpu.VMEM((units, 2 * BLK, 128), jnp.float32),
            ],
        ),
        out_shape=[
            jax.ShapeDtypeStruct((rows, width), jnp.bfloat16),
            jax.ShapeDtypeStruct((width // 128, 8, blocks * 2 * BLK), jnp.float32),
        ],
        compiler_params=pltpu.CompilerParams(vmem_limit_bytes=48 << 20),
        cost_estimate=pl.CostEstimate(flops=pairs * 512, transcendentals=pairs, bytes_accessed=4 * (rows + keys) * width),
    )(*(scalars or ()), q, *k_list, *v_list)


def attention_backward(q, q_col, do, o, lse, k_list, k_col, v_list, v_col, width, scalars, key_rows, units=2, per_group=2, o_col=0):
    pieces = len(k_list)
    lanes = units * 128
    rows = q.shape[0]
    keys = sum(k.shape[0] for k in k_list)
    chunks = keys // key_rows
    groups, blocks = width // lanes, rows // BLK
    masked = scalars is not None
    spec_q = pl.BlockSpec((BLK, lanes), lambda h, i, *_: (i, q_col + h))
    spec_o = pl.BlockSpec((BLK, lanes), lambda h, i, *_: (i, o_col + h))
    spec_dq = pl.BlockSpec((BLK, lanes), lambda h, i, *_: (i, h))
    spec_lse = pl.BlockSpec((units, 8, 2 * BLK), lambda h, i, *_: (o_col + h, 0, i))
    specs_k = [pl.BlockSpec((k.shape[0], lanes), lambda h, i, *_: (0, k_col + h)) for k in k_list]
    specs_v = [pl.BlockSpec((v.shape[0], lanes), lambda h, i, *_: (0, v_col + h)) for v in v_list]
    outs_k = [pl.BlockSpec((k.shape[0], lanes), lambda h, i, *_: (0, h)) for k in k_list]
    body = functools.partial(backward_body, masked, units, chunks, key_rows, pieces, per_group)
    pairs = rows * keys * (width // 64)
    shape_k = [jax.ShapeDtypeStruct((k.shape[0], width), jnp.bfloat16) for k in k_list]
    return pl.pallas_call(
        body,
        grid_spec=pltpu.PrefetchScalarGridSpec(
            num_scalar_prefetch=3 if masked else 0,
            grid=(groups, blocks),
            in_specs=[spec_q, spec_o, spec_o, spec_lse] + specs_k + specs_v,
            out_specs=[spec_dq] + outs_k + outs_k,
            scratch_shapes=[
                pltpu.VMEM((units, 2 * BLK, 128), jnp.bfloat16),
                pltpu.VMEM((units, 2 * BLK, 128), jnp.bfloat16),
                pltpu.VMEM((units, 8, 2 * BLK), jnp.float32),
                pltpu.VMEM((units, 2 * BLK, 128), jnp.float32),
                pltpu.VMEM((units, chunks, key_rows, 128), jnp.float32),
                pltpu.VMEM((units, chunks, key_rows, 128), jnp.float32),
            ],
        ),
        out_shape=[jax.ShapeDtypeStruct((rows, width), jnp.bfloat16)] + shape_k + shape_k,
        compiler_params=pltpu.CompilerParams(vmem_limit_bytes=48 << 20),
        cost_estimate=pl.CostEstimate(flops=pairs * 1280, transcendentals=pairs, bytes_accessed=8 * (rows + keys) * width),
    )(*(scalars or ()), q, do, o, lse, *k_list, *v_list)


def norm_sums(summed):
    mean = jnp.mean(summed, axis=-1, keepdims=True)
    centred = summed - mean
    inverse = lax.rsqrt(jnp.mean(centred * centred, axis=-1, keepdims=True) + epsilon)
    return centred * inverse, inverse


def feed_body(
    core_ref, hidden_ref, upstream_ref, weights_ref, expand_bias_ref, vectors_ref,
    out_ref, grad_hidden_ref, send_ref, keep_ref, grad_bias_ref, sums_ref,
    low, expanded, activated, total, grad_low,
):
    step = pl.program_id(0)
    blocks = pl.num_programs(0) // 2
    block = step % blocks
    width = hidden_ref.shape[1]
    first = weights_ref[:, 0, :128].reshape(width, width)
    second = weights_ref[:, 0, 128:].reshape(width, width)

    @pl.when(step == 0)
    def begin():
        low[...] = hidden_ref[...].astype(jnp.bfloat16)
        total[...] = residual_scale * hidden_ref[...] + vectors_ref[0:1]

    @pl.when(step < blocks)
    def forward():
        wide = mxu(low[...], first, NN) + expand_bias_ref[0]
        expanded[block] = wide
        active = gelu_tanh(wide).astype(jnp.bfloat16)
        activated[block] = active
        total[...] += mxu(active, second, NN)

    @pl.when(step == blocks)
    def turn():
        normed, inverse = norm_sums(total[...])
        gain = vectors_ref[1:2]
        out_ref[...] = (normed * gain + vectors_ref[2:3]).astype(out_ref.dtype)
        upstream = upstream_ref[...].astype(jnp.float32)
        scaled = upstream * gain
        grad = inverse * (
            scaled
            - jnp.mean(scaled, axis=-1, keepdims=True)
            - normed * jnp.mean(scaled * normed, axis=-1, keepdims=True)
        )
        grad_low[...] = grad.astype(jnp.bfloat16)
        grad_hidden_ref[...] = residual_scale * grad
        sums_ref[0:1] = jnp.sum(grad_low[...].astype(jnp.float32), axis=0, keepdims=True)
        sums_ref[1:2] = jnp.sum(upstream * normed, axis=0, keepdims=True)
        sums_ref[2:3] = jnp.sum(upstream, axis=0, keepdims=True)

    @pl.when(step >= blocks)
    def backward():
        grad_active = mxu(grad_low[...], second, NT)
        grad_wide = (grad_active * gelu_slope(expanded[block])).astype(jnp.bfloat16)
        grad_second = mxu(activated[block], grad_low[...], TN).astype(jnp.bfloat16).reshape(-1, 128, width)
        grad_first = mxu(low[...], grad_wide, TN).astype(jnp.bfloat16).reshape(-1, 128, width)

        @pl.when(block < blocks // 2)
        def to_send():
            send_ref[:, 0, 128:] = grad_second
            send_ref[:, 0, :128] = grad_first

        @pl.when(block >= blocks // 2)
        def to_keep():
            keep_ref[:, 0, 128:] = grad_second
            keep_ref[:, 0, :128] = grad_first

        grad_bias_ref[0] = jnp.sum(grad_wide.astype(jnp.float32), axis=0, keepdims=True)
        grad_hidden_ref[...] += mxu(grad_wide, first, NT)


def feed_forward(core, hidden, upstream, weights, expand_bias, vectors):
    rows, width = hidden.shape
    groups, blocks = weights.shape[:2]
    half = blocks // 2

    def at(i, core_ref):
        return (i + half * (1 - core_ref[0])) % blocks

    def back(i, core_ref):
        return (jnp.maximum(i - blocks, 0) + half * (1 - core_ref[0])) % blocks

    whole = pl.BlockSpec((rows, width), lambda i, c: (0, 0))
    once = pl.BlockSpec((rows, width), lambda i, c: (0, 0), pipeline_mode=pl.Buffered(1))
    f32, bf16 = jnp.float32, jnp.bfloat16
    part = (groups, 1, 256, width)
    return pl.pallas_call(
        feed_body,
        grid_spec=pltpu.PrefetchScalarGridSpec(
            num_scalar_prefetch=1,
            grid=(2 * blocks,),
            in_specs=[
                once, once,
                pl.BlockSpec(part, lambda i, c: (0, at(i, c), 0, 0)),
                pl.BlockSpec((1, 1, width), lambda i, c: (at(i, c), 0, 0)),
                pl.BlockSpec((8, width), lambda i, c: (0, 0)),
            ],
            out_specs=[
                whole, whole,
                pl.BlockSpec(part, lambda i, c: (0, jnp.clip(i - blocks, 0, half - 1), 0, 0)),
                pl.BlockSpec(part, lambda i, c: (0, jnp.clip(i - blocks - half, 0, half - 1), 0, 0)),
                pl.BlockSpec((1, 1, width), lambda i, c: (back(i, c), 0, 0)),
                pl.BlockSpec((8, width), lambda i, c: (0, 0)),
            ],
            scratch_shapes=[
                pltpu.VMEM((rows, width), bf16),
                pltpu.VMEM((blocks, rows, width), f32),
                pltpu.VMEM((blocks, rows, width), bf16),
                pltpu.VMEM((rows, width), f32),
                pltpu.VMEM((rows, width), bf16),
            ],
        ),
        out_shape=[
            jax.ShapeDtypeStruct((rows, width), bf16),
            jax.ShapeDtypeStruct((rows, width), f32),
            jax.ShapeDtypeStruct((groups, half, 256, width), bf16),
            jax.ShapeDtypeStruct((groups, half, 256, width), bf16),
            jax.ShapeDtypeStruct((blocks, 1, width), f32),
            jax.ShapeDtypeStruct((8, width), f32),
        ],
        compiler_params=pltpu.CompilerParams(vmem_limit_bytes=60 << 20),
        cost_estimate=pl.CostEstimate(flops=12 * rows * width * width * blocks, transcendentals=2 * rows * width * blocks, bytes_accessed=52 << 20),
    )(core.reshape(1).astype(jnp.int32), hidden, upstream, weights, expand_bias, vectors)


def core_perm():
    return [(c, c ^ 1) for c in range(4)]


def y_perm():
    return [(c, c ^ 2) for c in range(4)]


def diagonal_perm():
    return [(c, c ^ 3) for c in range(4)]


def x_perm():
    return [(f, f ^ 1) for f in range(8)]


def z_perm(k):
    return [(f, f ^ (2 * k)) for f in range(8)]


def to_core(v):
    return lax.ppermute(v, "ctx", core_perm())


def to_y(v):
    return lax.ppermute(v, "ctx", y_perm())


def to_diagonal(v):
    return lax.ppermute(v, "ctx", diagonal_perm())


def to_x(v):
    return lax.ppermute(v, "fsdp", x_perm())


def to_z(v, k):
    return lax.ppermute(v, "fsdp", z_perm(k))


def fsdp_pieces(own):
    along = [own] + [to_z(own, k) for k in (1, 2, 3)]
    return along + [to_x(piece) for piece in along]


def fsdp_sources(me):
    return [me ^ (2 * k + d) for d in (0, 1) for k in range(4)]


def place_body(plan, *refs):
    offsets, refs = refs[0], refs[1:]
    outs, sems = refs[-1 - len(plan):-1], refs[-1]
    pieces = refs[:-1 - len(plan)]
    copies = []
    for i, piece in enumerate(pieces):
        for s, (lead, first, rows) in enumerate(plan):
            source = piece if lead is None else piece.at[lead]
            start = pl.multiple_of(offsets[i] * rows, rows)
            copy = pltpu.make_async_copy(source.at[pl.ds(first, rows)], outs[s].at[pl.ds(start, rows)], sems.at[i, s])
            copy.start()
            copies.append(copy)
    for copy in copies:
        copy.wait()


def place(pieces, slots, plan):
    columns = pieces[0].shape[-1]
    count = len(pieces)
    out = [jax.ShapeDtypeStruct((count * rows, columns), pieces[0].dtype) for _, _, rows in plan]
    anywhere = pl.BlockSpec(memory_space=pl.ANY)
    moved = 4 * count * columns * sum(rows for _, _, rows in plan)
    return pl.pallas_call(
        functools.partial(place_body, plan),
        in_specs=[pl.BlockSpec(memory_space=pltpu.SMEM)] + [anywhere] * count,
        out_specs=[pl.BlockSpec(memory_space=pltpu.VMEM)] * len(plan),
        out_shape=out,
        scratch_shapes=[pltpu.SemaphoreType.DMA((count, len(plan)))],
        compiler_params=pltpu.CompilerParams(vmem_limit_bytes=(moved // 2) + (4 << 20)),
        cost_estimate=pl.CostEstimate(flops=0, transcendentals=0, bytes_accessed=moved),
    )(jnp.stack(slots).astype(jnp.int32), *pieces)


def after(value, other):
    return lax.optimization_barrier((value, other))[0]


def xor_take(stack, me):
    return jnp.concatenate([lax.dynamic_index_in_dim(stack, n ^ me, 0) for n in range(stack.shape[0])])


def from_fsdp(blocks):
    got = lax.all_to_all(blocks, "fsdp", 0, 0)
    return jnp.sum(got.astype(jnp.float32), axis=0)


def part_of(parts, index, axis):
    return lax.dynamic_index_in_dim(parts, index, axis, keepdims=False)


def added(keep, got):
    return (keep.astype(jnp.float32) + got.astype(jnp.float32)).astype(jnp.bfloat16)


def halves_dot(pairs, core):
    def side(index):
        terms = []
        for left, right in pairs:
            half = right.shape[1] // 2
            chosen = lax.dynamic_slice_in_dim(right, index * half, half, axis=1)
            terms.append(jnp.dot(left.T, chosen, preferred_element_type=jnp.float32).astype(jnp.bfloat16))
        return with_layout_constraint(jnp.concatenate(terms, axis=1), Layout(major_to_minor=(0, 1)))

    return side(core), side(core ^ 1)


def over_z(parts, z):
    got = [to_z(part_of(parts, z ^ k, 1), k) for k in (1, 2, 3)]
    total = part_of(parts, z, 1).astype(jnp.float32)
    return (total + got[0].astype(jnp.float32) + got[1].astype(jnp.float32) + got[2].astype(jnp.float32)).astype(jnp.bfloat16)


def ctx_pieces(own):
    line = to_y(own)
    return [own, to_core(own), line, to_core(line)]


def spread_feed_body(core_ref, *refs):
    (own, other), (expand_ref, reduce_ref) = refs[:2], refs[2:]
    for index, source in ((core_ref[0], own), (1 - core_ref[0], other)):
        for p in range(2):
            at = pl.multiple_of(index * 256 + p * 128, 128)
            reduce_ref[pl.ds(at, 128), :] = source[p, 128:].astype(jnp.float32)
            for f in range(8):
                expand_ref[:, pl.ds(at + f * 512, 128)] = source[p, :128, f * 128:(f + 1) * 128].astype(jnp.float32)


def spread_projection_body(me_ref, *refs):
    pieces, (out_ref, vectors_ref) = refs[:4], refs[4:]
    total = jnp.zeros((8, 384), jnp.float32)
    for k in range(4):
        at = pl.multiple_of((me_ref[0] ^ k) * 256, 128)
        for part in range(3):
            for pair in range(2):
                source = pieces[k][:128, pair * 384 + part * 128:pair * 384 + (part + 1) * 128]
                out_ref[:, pl.ds(at + part * 1024 + pair * 128, 128)] = source.astype(jnp.float32)
        total = total + pieces[k][128:136, 384:].astype(jnp.float32)
    for i in range(18):
        vectors_ref[i:i + 1] = total[i // 3:i // 3 + 1, (i % 3) * 128:(i % 3 + 1) * 128]


def spread_middle_body(core_ref, *refs):
    (early, early_other, late, late_other), (memory_ref, query_ref, cross_ref, self_ref) = refs[:4], refs[4:]
    for index, first, second in ((core_ref[0], early, late), (1 - core_ref[0], early_other, late_other)):
        for half, source in ((0, first), (512, second)):
            at = pl.multiple_of(half + index * 256, 256)
            memory_ref[:, pl.ds(at, 256)] = source[:, 0:256].astype(jnp.float32)
            memory_ref[:, pl.ds(at + 1024, 256)] = source[:, 256:512].astype(jnp.float32)
            query_ref[:, pl.ds(at, 256)] = source[:, 512:768].astype(jnp.float32)
        at = pl.multiple_of(index * 512, 512)
        cross_ref[:, pl.ds(at, 512)] = first[:, 768:].astype(jnp.float32)
        self_ref[:, pl.ds(at, 512)] = second[:, 768:].astype(jnp.float32)


def spread(body, index, pieces, shapes):
    whole = pl.BlockSpec(memory_space=pltpu.VMEM)
    moved = sum(p.size * 2 for p in pieces) + sum(a * b * 4 for a, b in shapes)
    return pl.pallas_call(
        body,
        in_specs=[pl.BlockSpec(memory_space=pltpu.SMEM)] + [whole] * len(pieces),
        out_specs=[whole] * len(shapes),
        out_shape=[jax.ShapeDtypeStruct(shape, jnp.float32) for shape in shapes],
        compiler_params=pltpu.CompilerParams(vmem_limit_bytes=moved + (4 << 20)),
        cost_estimate=pl.CostEstimate(flops=0, transcendentals=0, bytes_accessed=moved),
    )(index.reshape(1).astype(jnp.int32), *pieces)


def chip_sums(terms, rows):
    pairs = terms.reshape(2, 2, rows, terms.shape[1])
    got = to_core(pairs[:, 1])
    return pairs[0, 0].astype(jnp.float32) + got[0].astype(jnp.float32), added(pairs[1, 0], got[1])


def tiled_shards(
    tokens,
    memory,
    cotangent,
    block_map,
    block_order,
    self_projection,
    self_output,
    self_query_bias,
    self_value_bias,
    self_output_bias,
    first_gain,
    first_shift,
    cross_query,
    cross_memory,
    cross_output,
    cross_query_bias,
    cross_value_bias,
    cross_output_bias,
    second_gain,
    second_shift,
    expand_weight,
    reduce_weight,
    expand_bias,
    reduce_bias,
    third_gain,
    third_shift,
):
    bf16 = jnp.bfloat16
    f32 = jnp.float32
    own_rows = tokens[0]
    rows, width = own_rows.shape
    me_c, me_f = lax.axis_index("ctx"), lax.axis_index("fsdp")
    core, line, z, x = me_c % 2, me_c // 2, me_f // 2, me_f % 2
    share = width // 4

    def dot(left, right):
        return jnp.dot(left, right, preferred_element_type=f32)

    vectors = [self_query_bias, self_value_bias, self_output_bias, first_gain, first_shift, cross_query_bias,
               cross_value_bias, cross_output_bias, second_gain, second_shift, reduce_bias, third_gain, third_shift]
    vectors += [expand_bias[i * 128:(i + 1) * 128] for i in range(4)] + [jnp.zeros((128,), bf16)]
    vector_rows = jnp.stack([jnp.concatenate(vectors[i * 6:i * 6 + 6]) for i in range(3)])
    columns = [lax.dynamic_slice(self_projection, (0, part * width + me_c * share), (128, share)) for part in range(3)]
    own_piece = jnp.concatenate([jnp.concatenate(columns, axis=1), vector_rows, jnp.zeros((13, 3 * share), bf16)])
    projection_pieces = fsdp_pieces(own_piece)
    rows_y = to_y(own_rows)
    rows_core = to_core(own_rows)
    rows_diagonal = to_core(after(rows_y, projection_pieces[1:4]))
    sequence = jnp.concatenate([own_rows, rows_core, rows_y, rows_diagonal])
    sources = fsdp_sources(me_f)
    projection, vector_blocks = place(projection_pieces, sources, ((None, 0, 128), (None, 128, 16)))
    vector_blocks = vector_blocks.reshape(8, 16, 3 * share).astype(f32)
    gathered = [vector_blocks[:, i // 6, (i % 6) * 128:(i % 6 + 1) * 128].reshape(width) for i in range(17)]
    (query_bias, value_bias, out_bias, gain_one, shift_one, cross_qbias, cross_vbias, cross_obias,
     gain_two, shift_two, reduce_bias_full, gain_three, shift_three) = gathered[:13]
    expand_bias_blocks = jnp.stack(gathered[13:]).reshape(4, 1, width)

    middle = [cross_memory[:, :width], cross_memory[:, width:], self_output, cross_query, cross_output]
    middle_own = jnp.stack([lax.dynamic_slice_in_dim(weight, me_c * 32, 32) for weight in middle])
    middle_all = lax.all_gather(middle_own, ("fsdp", "ctx"), axis=0)
    memory_key_full, memory_value_full, self_out_full, cross_query_full, cross_out_full = [
        middle_all[:, i].reshape(width, width) for i in range(5)
    ]
    expand_columns = lax.dynamic_index_in_dim(expand_weight.reshape(128, 8, 4, 128), me_c, 2, keepdims=False)
    feed_own = jnp.concatenate([expand_columns.reshape(128, width), lax.dynamic_slice_in_dim(reduce_weight, me_c * 128, 128)])

    memory_rows = memory[0]
    memory_y = to_y(after(memory_rows, projection_pieces[4:]))
    memory_core = to_core(memory_rows)

    projected = dot(sequence, projection)
    bias = jnp.concatenate([
        lax.dynamic_slice_in_dim(query_bias, me_c * share, share),
        jnp.zeros((share,), f32),
        lax.dynamic_slice_in_dim(value_bias, me_c * share, share),
    ])
    qkv = (projected + bias).astype(bf16)
    scalars = (block_order[0], block_map[0].reshape(-1), me_c.reshape(1).astype(jnp.int32))
    heads_out, self_lse = attention_forward(qkv, 0, [qkv], 1, [qkv], 2, share, scalars, BLK)
    heads_out, memory_y = lax.optimization_barrier((heads_out, memory_y))
    memory_all = jnp.concatenate([memory_rows, memory_core, memory_y, to_core(memory_y)])

    feed_weights = lax.all_gather(after(feed_own, (middle_all, heads_out)), ("fsdp", "ctx"), axis=0, tiled=True)
    memory_keys = dot(memory_all, memory_key_full).astype(bf16)
    memory_values = (dot(memory_all, memory_value_full) + cross_vbias).astype(bf16)

    pieces = [heads_out[i * rows:(i + 1) * rows] for i in range(4)]
    others = after([to_core(pieces[1]), to_y(pieces[2]), to_diagonal(pieces[3])], (memory_keys, memory_values))
    arrived = jnp.stack([pieces[0]] + others)
    attended = jnp.concatenate([part_of(arrived, n ^ me_c, 0) for n in range(4)], axis=1)
    branch = dot(attended, self_out_full) + out_bias
    hidden_one, normed_one, inverse_one = layer_norm(residual_scale * own_rows.astype(f32) + branch, gain_one, shift_one)

    hidden_low = hidden_one.astype(bf16)
    cross_queries = (dot(hidden_low, cross_query_full) + cross_qbias).astype(bf16)
    cross_low, cross_lse = attention_forward(cross_queries, 0, [memory_keys], 0, [memory_values], 0, width, None, rows)
    cross_branch = dot(cross_low, cross_out_full) + cross_obias
    hidden_two, normed_two, inverse_two = layer_norm(residual_scale * hidden_one + cross_branch, gain_two, shift_two)

    feed_vectors = jnp.concatenate([jnp.stack([reduce_bias_full, gain_three, shift_three]), jnp.zeros((5, width), f32)])
    output, grad_hidden_two, feed_send, feed_keep, grad_expand_bias, feed_sums = feed_forward(
        core, hidden_two, cotangent[0], feed_weights.reshape(8, 4, 256, width), expand_bias_blocks, feed_vectors
    )
    feed_got = to_core(feed_send)

    grad_second, grad_second_gain, grad_second_shift = layer_norm_back(grad_hidden_two, gain_two, normed_two, inverse_two)
    grad_cross_branch = grad_second.astype(bf16)
    grad_cross_output_bias = jnp.sum(grad_cross_branch.astype(f32), axis=0)
    grad_cross_low = dot(grad_cross_branch, cross_out_full.T).astype(bf16)

    def cross_half(half, queries):
        return attention_backward(
            queries, 2 * half, grad_cross_low, cross_low, cross_lse, [memory_keys], 2 * half, [memory_values], 2 * half,
            width // 2, None, rows, o_col=2 * half
        )

    def line_split(summed):
        return summed.reshape(8, 2, 64, summed.shape[1])

    early_q, early_k, early_v = cross_half(0, cross_queries)
    feed_keep, feed_got = after((feed_keep, feed_got), early_q)
    feed_half = added(feed_keep, feed_got).reshape(8 * 512, width)
    feed_share = lax.psum_scatter(feed_half, "fsdp", scatter_dimension=0, tiled=True)
    first_q, first_k, first_v = after((early_q, early_k, early_v), feed_half)
    keep, send = halves_dot(
        [(memory_all, first_k), (memory_all, first_v), (hidden_low, first_q), (cross_low, grad_cross_branch)], core
    )
    early_got = to_core(send)
    late_q, late_k, late_v = cross_half(1, after(cross_queries, (keep, send)))
    late_q, late_k, late_v, early_got = lax.optimization_barrier((late_q, late_k, late_v, early_got))
    early = line_split(added(keep, early_got))
    early_send = part_of(early, line ^ 1, 1)
    early_got = to_y(early_send)
    late_q, early_q = after((late_q, early_q), early_send)

    grad_cross_queries = jnp.concatenate([early_q, late_q], axis=1)
    grad_cross_query_bias = jnp.sum(grad_cross_queries.astype(f32), axis=0)
    grad_hidden_one = residual_scale * grad_second + dot(grad_cross_queries, cross_query_full.T)
    grad_first, grad_first_gain, grad_first_shift = layer_norm_back(grad_hidden_one, gain_one, normed_one, inverse_one)
    grad_branch = grad_first.astype(bf16)
    grad_self_output_bias = jnp.sum(grad_branch.astype(f32), axis=0)
    grad_attended = dot(grad_branch, self_out_full.T).astype(bf16)
    by_heads = jnp.stack([grad_attended[:, i * share:(i + 1) * share] for i in range(4)])
    sends = [part_of(by_heads, k ^ me_c, 0) for k in range(4)]
    received = [to_core(sends[1]), to_y(sends[2]), to_diagonal(sends[3])]
    heads_grad = jnp.concatenate([sends[0]] + received)

    ready_q, ready_k, ready_v, ready_branch = after((late_q, late_k, late_v, grad_branch), received[0])
    grad_cross_value_bias = jnp.concatenate([jnp.sum(early_v.astype(f32), axis=0), jnp.sum(ready_v.astype(f32), axis=0)])
    memory_terms = dot(jnp.concatenate([early_k, early_v, ready_k, ready_v], axis=1), jnp.concatenate([
        memory_key_full[:, :width // 2], memory_value_full[:, :width // 2],
        memory_key_full[:, width // 2:], memory_value_full[:, width // 2:],
    ], axis=1).T).astype(bf16)
    memory_near, memory_far = chip_sums(memory_terms, rows)
    late_keep, late_send = halves_dot(
        [(memory_all, ready_k), (memory_all, ready_v), (hidden_low, ready_q), (attended, ready_branch)], core
    )
    late_got = to_core(late_send)
    early = added(part_of(early, line, 1), early_got).reshape(4, 2, 64, 5 * share)

    def heads_back(pair, upstream):
        return attention_backward(
            qkv, pair, upstream, heads_out, self_lse, [qkv], 2 + pair, [qkv], 4 + pair, share // 2, scalars, BLK,
            units=1, o_col=pair,
        )

    def own_blocks(grads):
        return dot(sequence.T, grads).astype(bf16).reshape(8, 128, grads.shape[1])

    vector_grads = jnp.concatenate([
        jnp.stack([
            grad_self_output_bias, grad_first_gain, grad_first_shift, grad_cross_query_bias, grad_cross_value_bias,
            grad_cross_output_bias, grad_second_gain, grad_second_shift,
        ]),
        feed_sums[:3],
        grad_expand_bias.reshape(4, width),
    ])
    vector_rows = vector_grads.reshape(5, 3, 8, 128).transpose(2, 0, 1, 3).reshape(8, 5, 384).astype(bf16)
    heads_grad = after(heads_grad, (early, late_keep, late_send, memory_far, vector_rows))
    memory_got = to_y(memory_far)
    early_got = to_x(part_of(early, x ^ 1, 1))
    first_heads = jnp.concatenate(heads_back(0, heads_grad), axis=1)
    first_heads, early_got, late_got = lax.optimization_barrier((first_heads, early_got, late_got))
    first_blocks = own_blocks(first_heads)
    late = added(late_keep, late_got).reshape(4, 2, 128, 5 * share)
    late_got = to_x(part_of(late, x ^ 1, 1))
    early = added(part_of(early, x, 1), early_got)
    early_sends = [part_of(early, z ^ k, 0) for k in (1, 2, 3)]
    first_total = from_fsdp(first_blocks)
    second_heads = jnp.concatenate(heads_back(1, after(heads_grad, (first_blocks, late, early_sends))), axis=1)
    early_pieces = [to_z(piece, k) for piece, k in zip(early_sends, (1, 2, 3))]
    second_heads, early_pieces, late_got, memory_got, feed_share = lax.optimization_barrier(
        (second_heads, early_pieces, late_got, memory_got, feed_share)
    )
    second_blocks = own_blocks(second_heads)
    ready_first, ready_second = after((first_heads, second_heads), second_blocks)
    token_terms = (
        dot(ready_first, jnp.concatenate([projection[:, i * share:i * share + 128] for i in range(3)], axis=1).T)
        + dot(ready_second, jnp.concatenate([projection[:, i * share + 128:(i + 1) * share] for i in range(3)], axis=1).T)
    ).astype(bf16)
    token_near, token_far = chip_sums(token_terms, rows)
    feed_near = feed_share
    feed_far = to_y(feed_share)
    token_got = to_y(after(token_far, feed_far))
    token_grad = (residual_scale * grad_first + token_near + token_got.astype(f32))[None]
    memory_grad = (memory_near + memory_got.astype(f32))[None]

    both_heads = [first_heads.astype(f32), second_heads.astype(f32)]
    head_sums = jnp.stack([
        jnp.concatenate([jnp.sum(half[:, at:at + 128], axis=0) for half in both_heads]) for at in (0, 256)
    ])
    head_sums = lax.dynamic_update_slice(jnp.zeros((2, width), f32), head_sums, (0, me_c * share))
    head_rows = jnp.concatenate([head_sums, jnp.zeros((1, width), f32)])
    head_rows = head_rows.reshape(3, 8, 128).transpose(1, 0, 2).reshape(8, 1, 384).astype(bf16)
    blocks = jnp.concatenate([second_blocks, vector_rows, head_rows, jnp.zeros((8, 10, 384), bf16)], axis=1)
    second_total = from_fsdp(blocks)
    padded = jnp.concatenate([first_total, jnp.zeros((16, 384), f32)])
    total = after(jnp.concatenate([padded, second_total], axis=1).astype(bf16), token_got)

    early = part_of(early, z, 0).astype(f32)
    for piece in early_pieces:
        early = early + piece.astype(f32)
    early = early.astype(bf16)
    late = over_z(added(after(part_of(late, x, 1), (blocks, token_far)), late_got)[None], z)[0]
    early_got = to_y(early)
    early = jnp.concatenate([jnp.where(line == 0, early, early_got), jnp.where(line == 0, early_got, early)])
    late = added(late, to_y(late))
    grad_cross_memory, grad_cross_query, grad_cross_output, grad_self_output = spread(
        spread_middle_body, core, [early, to_core(early), late, to_core(late)],
        [(128, 2 * width), (128, width), (128, width), (128, width)],
    )

    grad_self_projection, sums = spread(
        spread_projection_body, me_c, ctx_pieces(total), [(128, 3 * width), (18, 128)]
    )

    feed_own = added(feed_near, feed_far).reshape(2, 256, width)
    grad_expand, grad_reduce = spread(spread_feed_body, core, [feed_own, to_core(feed_own)], [(128, 4 * width), (512, width)])

    return (
        output[None],
        token_grad,
        memory_grad,
        grad_self_projection,
        grad_self_output,
        sums[15],
        sums[16],
        sums[0],
        sums[1],
        sums[2],
        grad_cross_query,
        grad_cross_memory,
        grad_cross_output,
        sums[3],
        sums[4],
        sums[5],
        sums[6],
        sums[7],
        grad_expand,
        grad_reduce,
        sums[11:15].reshape(512),
        sums[8],
        sums[9],
        sums[10],
    )


def head_split(matrix):
    return matrix.reshape(matrix.shape[0], HEADS, HEAD_DIM)


def piece_size(length):
    return min(512, length)


def piece_masks(key_blocks, allowed_rows):
    length = key_blocks.shape[0]
    piece = piece_size(length)
    count = length // piece
    if allowed_rows is None:
        return jnp.ones((count, 1, 1), jnp.bool_)
    nblocks = allowed_rows.shape[1]
    onehot = (key_blocks[:, None] == jnp.arange(nblocks, dtype=jnp.int32)[None, :]).astype(
        jnp.float32
    )
    live = jnp.dot(allowed_rows, onehot.T) > 0.5
    return jnp.moveaxis(live.reshape(live.shape[0], count, piece), 1, 0)


def masked_scores(query_heads, key_piece, live):
    scores = (
        jnp.einsum("qhd,khd->hqk", query_heads, key_piece, preferred_element_type=jnp.float32)
        * score_scale
    )
    return jnp.where(live[None], scores, masked_score)


def run_guarded(guarded, live, work, fallback):
    if guarded:
        return lax.cond(jnp.any(live), work, lambda unused: fallback, live)
    return work(live)


def attend_forward(query_heads, key_heads, value_heads, live_pieces, guarded):
    count = live_pieces.shape[0]
    piece = key_heads.shape[0] // count
    key_pieces = key_heads.reshape((count, piece) + key_heads.shape[1:])
    value_pieces = value_heads.reshape((count, piece) + value_heads.shape[1:])
    rows = query_heads.shape[0]

    def first_step(carry, inputs):
        run_max, run_sum = carry
        key_piece, live = inputs

        def work(live_now):
            scores = masked_scores(query_heads, key_piece, live_now)
            new_max = jnp.maximum(run_max, jnp.max(scores, axis=-1))
            shifted = jnp.where(live_now[None], jnp.exp(scores - new_max[:, :, None]), 0.0)
            return (new_max, run_sum * jnp.exp(run_max - new_max) + jnp.sum(shifted, axis=-1))

        return (run_guarded(guarded, live, work, (run_max, run_sum)), None)

    start = (
        jnp.full((HEADS, rows), masked_score, jnp.float32),
        jnp.zeros((HEADS, rows), jnp.float32),
    )
    (final_max, final_sum), unused = lax.scan(first_step, start, (key_pieces, live_pieces))
    log_total = final_max + jnp.log(final_sum)

    def second_step(total, inputs):
        key_piece, value_piece, live = inputs

        def work(live_now):
            scores = masked_scores(query_heads, key_piece, live_now)
            probs = jnp.exp(scores - log_total[:, :, None]).astype(jnp.bfloat16)
            return total + jnp.einsum(
                "hqk,khd->qhd", probs, value_piece, preferred_element_type=jnp.float32
            )

        return (run_guarded(guarded, live, work, total), None)

    empty = jnp.zeros((rows, HEADS, HEAD_DIM), jnp.float32)
    attended, unused = lax.scan(second_step, empty, (key_pieces, value_pieces, live_pieces))
    return (attended, log_total)


def attend_backward(
    query_heads, key_heads, value_heads, log_total, grad_heads, delta, live_pieces, guarded
):
    count = live_pieces.shape[0]
    piece = key_heads.shape[0] // count
    key_pieces = key_heads.reshape((count, piece) + key_heads.shape[1:])
    value_pieces = value_heads.reshape((count, piece) + value_heads.shape[1:])
    rows = query_heads.shape[0]
    blank = jnp.zeros((piece, HEADS, HEAD_DIM), jnp.float32)

    def back_step(grad_query, inputs):
        key_piece, value_piece, live = inputs

        def work(live_now):
            scores = masked_scores(query_heads, key_piece, live_now)
            probs = jnp.exp(scores - log_total[:, :, None])
            grad_probs = jnp.einsum(
                "qhd,khd->hqk", grad_heads, value_piece, preferred_element_type=jnp.float32
            )
            grad_scores = (probs * (grad_probs - delta[:, :, None])).astype(jnp.bfloat16)
            new_query = (
                grad_query
                + jnp.einsum(
                    "hqk,khd->qhd", grad_scores, key_piece, preferred_element_type=jnp.float32
                )
                * score_scale
            )
            grad_key = (
                jnp.einsum(
                    "hqk,qhd->khd", grad_scores, query_heads, preferred_element_type=jnp.float32
                )
                * score_scale
            )
            grad_value = jnp.einsum(
                "hqk,qhd->khd",
                probs.astype(jnp.bfloat16),
                grad_heads,
                preferred_element_type=jnp.float32,
            )
            return (new_query, (grad_key, grad_value))

        return run_guarded(guarded, live, work, (grad_query, (blank, blank)))

    empty = jnp.zeros((rows, HEADS, HEAD_DIM), jnp.float32)
    grad_query, (key_grads, value_grads) = lax.scan(
        back_step, empty, (key_pieces, value_pieces, live_pieces)
    )
    width = HEADS * HEAD_DIM
    return (
        grad_query.reshape(rows, width),
        key_grads.reshape(-1, width),
        value_grads.reshape(-1, width),
    )


def plain_shards(
    tokens,
    memory,
    cotangent,
    block_map,
    block_order,
    self_projection,
    self_output,
    self_query_bias,
    self_value_bias,
    self_output_bias,
    first_gain,
    first_shift,
    cross_query,
    cross_memory,
    cross_output,
    cross_query_bias,
    cross_value_bias,
    cross_output_bias,
    second_gain,
    second_shift,
    expand_weight,
    reduce_weight,
    expand_bias,
    reduce_bias,
    third_gain,
    third_shift,
):
    bf16 = jnp.bfloat16
    f32 = jnp.float32
    rows_in = tokens[0]
    rows = rows_in.shape[0]
    width = rows_in.shape[1]
    ctx_count = lax.axis_size("ctx")
    slot = lax.axis_index("ctx")
    positions = jnp.arange(rows * ctx_count, dtype=jnp.int32)
    group_index = positions // rows
    group_match = group_index[:, None] == jnp.arange(ctx_count, dtype=jnp.int32)[None, :]
    group_place = jnp.sum(jnp.where(group_match, block_order[0][None, :], 0), axis=1)
    key_blocks = (group_place * rows + positions % rows) // BLK
    own_blocks = lax.dynamic_slice_in_dim(key_blocks, slot * rows, rows)
    nblocks = block_map.shape[1]
    own_onehot = (own_blocks[:, None] == jnp.arange(nblocks, dtype=jnp.int32)[None, :]).astype(f32)
    allowed_rows = jnp.dot(own_onehot, block_map[0].astype(f32))
    self_live = piece_masks(key_blocks, allowed_rows)
    (
        projection_full,
        self_out_full,
        query_bias_full,
        value_bias_full,
        out_bias_full,
        gain_one,
        shift_one,
    ) = (
        lax.all_gather(self_projection, "fsdp", axis=0, tiled=True),
        lax.all_gather(self_output, "fsdp", axis=0, tiled=True),
        lax.all_gather(self_query_bias, "fsdp", axis=0, tiled=True),
        lax.all_gather(self_value_bias, "fsdp", axis=0, tiled=True),
        lax.all_gather(self_output_bias, "fsdp", axis=0, tiled=True),
        lax.all_gather(first_gain, "fsdp", axis=0, tiled=True),
        lax.all_gather(first_shift, "fsdp", axis=0, tiled=True),
    )
    projected = jnp.dot(rows_in, projection_full, preferred_element_type=f32)
    queries = (projected[:, :width] + query_bias_full).astype(bf16)
    keys_own = projected[:, width : 2 * width].astype(bf16)
    values_own = (projected[:, 2 * width :] + value_bias_full).astype(bf16)
    keys_all, values_all = (
        lax.all_gather(keys_own, "ctx", axis=0, tiled=True),
        lax.all_gather(values_own, "ctx", axis=0, tiled=True),
    )
    query_heads = head_split(queries)
    key_heads = head_split(keys_all)
    value_heads = head_split(values_all)
    attended, self_total = attend_forward(query_heads, key_heads, value_heads, self_live, True)
    attended_low = attended.reshape(rows, width).astype(bf16)
    branch = jnp.dot(attended_low, self_out_full, preferred_element_type=f32) + out_bias_full
    hidden_one, normed_one, inverse_one = layer_norm(
        residual_scale * rows_in.astype(f32) + branch, gain_one, shift_one
    )
    (
        cross_query_full,
        cross_memory_full,
        cross_out_full,
        cross_qbias_full,
        cross_vbias_full,
        cross_obias_full,
        gain_two,
        shift_two,
    ) = (
        lax.all_gather(cross_query, "fsdp", axis=0, tiled=True),
        lax.all_gather(cross_memory, "fsdp", axis=0, tiled=True),
        lax.all_gather(cross_output, "fsdp", axis=0, tiled=True),
        lax.all_gather(cross_query_bias, "fsdp", axis=0, tiled=True),
        lax.all_gather(cross_value_bias, "fsdp", axis=0, tiled=True),
        lax.all_gather(cross_output_bias, "fsdp", axis=0, tiled=True),
        lax.all_gather(second_gain, "fsdp", axis=0, tiled=True),
        lax.all_gather(second_shift, "fsdp", axis=0, tiled=True),
    )
    hidden_low = hidden_one.astype(bf16)
    cross_queries = (
        jnp.dot(hidden_low, cross_query_full, preferred_element_type=f32) + cross_qbias_full
    ).astype(bf16)
    memory_rows = memory[0]
    memory_proj = jnp.dot(memory_rows, cross_memory_full, preferred_element_type=f32)
    memory_keys = memory_proj[:, :width].astype(bf16)
    memory_values = (memory_proj[:, width:] + cross_vbias_full).astype(bf16)
    memory_keys_all, memory_values_all = (
        lax.all_gather(memory_keys, "ctx", axis=0, tiled=True),
        lax.all_gather(memory_values, "ctx", axis=0, tiled=True),
    )
    cross_heads = head_split(cross_queries)
    memory_key_heads = head_split(memory_keys_all)
    memory_value_heads = head_split(memory_values_all)
    cross_live = piece_masks(jnp.zeros((memory_keys_all.shape[0],), jnp.int32), None)
    cross_attended, cross_total = attend_forward(
        cross_heads, memory_key_heads, memory_value_heads, cross_live, False
    )
    cross_low = cross_attended.reshape(rows, width).astype(bf16)
    cross_branch = jnp.dot(cross_low, cross_out_full, preferred_element_type=f32) + cross_obias_full
    hidden_two, normed_two, inverse_two = layer_norm(
        residual_scale * hidden_one + cross_branch, gain_two, shift_two
    )
    expand_full, reduce_full, expand_bias_full, reduce_bias_full, gain_three, shift_three = (
        lax.all_gather(expand_weight, "fsdp", axis=0, tiled=True),
        lax.all_gather(reduce_weight, "fsdp", axis=0, tiled=True),
        lax.all_gather(expand_bias, "fsdp", axis=0, tiled=True),
        lax.all_gather(reduce_bias, "fsdp", axis=0, tiled=True),
        lax.all_gather(third_gain, "fsdp", axis=0, tiled=True),
        lax.all_gather(third_shift, "fsdp", axis=0, tiled=True),
    )
    hidden_two_low = hidden_two.astype(bf16)
    expanded = jnp.dot(hidden_two_low, expand_full, preferred_element_type=f32) + expand_bias_full
    activated = gelu_tanh(expanded).astype(bf16)
    reduced = jnp.dot(activated, reduce_full, preferred_element_type=f32) + reduce_bias_full
    result, normed_three, inverse_three = layer_norm(
        residual_scale * hidden_two + reduced, gain_three, shift_three
    )
    output = result.astype(bf16)[None]
    upstream = cotangent[0].astype(f32)
    grad_third, grad_third_gain, grad_third_shift = layer_norm_back(
        upstream, gain_three, normed_three, inverse_three
    )
    grad_reduced = grad_third.astype(bf16)
    grad_reduce_bias = jnp.sum(grad_reduced.astype(f32), axis=0)
    grad_reduce_weight = jnp.dot(activated.T, grad_reduced, preferred_element_type=f32)
    grad_activated = jnp.dot(grad_reduced, reduce_full.T, preferred_element_type=f32)
    grad_expanded = (grad_activated * gelu_slope(expanded)).astype(bf16)
    grad_expand_bias = jnp.sum(grad_expanded.astype(f32), axis=0)
    grad_expand_weight = jnp.dot(hidden_two_low.T, grad_expanded, preferred_element_type=f32)
    grad_hidden_two = residual_scale * grad_third + jnp.dot(
        grad_expanded, expand_full.T, preferred_element_type=f32
    )
    grad_second, grad_second_gain, grad_second_shift = layer_norm_back(
        grad_hidden_two, gain_two, normed_two, inverse_two
    )
    grad_cross_branch = grad_second.astype(bf16)
    grad_cross_output_bias = jnp.sum(grad_cross_branch.astype(f32), axis=0)
    grad_cross_output = jnp.dot(cross_low.T, grad_cross_branch, preferred_element_type=f32)
    grad_cross_low = jnp.dot(
        grad_cross_branch, cross_out_full.T, preferred_element_type=f32
    ).astype(bf16)
    grad_cross_heads = head_split(grad_cross_low)
    cross_delta = jnp.sum(grad_cross_heads.astype(f32) * cross_attended, axis=-1).T
    grad_cross_queries, memory_key_terms, memory_value_terms = attend_backward(
        cross_heads,
        memory_key_heads,
        memory_value_heads,
        cross_total,
        grad_cross_heads,
        cross_delta,
        cross_live,
        False,
    )
    grad_memory_keys, grad_memory_values = (
        lax.psum_scatter(
            memory_key_terms.astype(jnp.bfloat16), "ctx", scatter_dimension=0, tiled=True
        ).astype(jnp.float32),
        lax.psum_scatter(
            memory_value_terms.astype(jnp.bfloat16), "ctx", scatter_dimension=0, tiled=True
        ).astype(jnp.float32),
    )
    grad_memory_pair = jnp.concatenate(
        [grad_memory_keys.astype(bf16), grad_memory_values.astype(bf16)], axis=1
    )
    grad_cross_value_bias = jnp.sum(grad_memory_pair[:, width:].astype(f32), axis=0)
    grad_cross_memory = jnp.dot(memory_rows.T, grad_memory_pair, preferred_element_type=f32)
    memory_grad = jnp.dot(grad_memory_pair, cross_memory_full.T, preferred_element_type=f32)[None]
    grad_cross_low_queries = grad_cross_queries.astype(bf16)
    grad_cross_query_bias = jnp.sum(grad_cross_low_queries.astype(f32), axis=0)
    grad_cross_query = jnp.dot(hidden_low.T, grad_cross_low_queries, preferred_element_type=f32)
    grad_hidden_one = residual_scale * grad_second + jnp.dot(
        grad_cross_low_queries, cross_query_full.T, preferred_element_type=f32
    )
    grad_first, grad_first_gain, grad_first_shift = layer_norm_back(
        grad_hidden_one, gain_one, normed_one, inverse_one
    )
    grad_branch = grad_first.astype(bf16)
    grad_self_output_bias = jnp.sum(grad_branch.astype(f32), axis=0)
    grad_self_output = jnp.dot(attended_low.T, grad_branch, preferred_element_type=f32)
    grad_attended = jnp.dot(grad_branch, self_out_full.T, preferred_element_type=f32).astype(bf16)
    grad_attended_heads = head_split(grad_attended)
    self_delta = jnp.sum(grad_attended_heads.astype(f32) * attended, axis=-1).T
    grad_queries, key_terms, value_terms = attend_backward(
        query_heads,
        key_heads,
        value_heads,
        self_total,
        grad_attended_heads,
        self_delta,
        self_live,
        True,
    )
    grad_keys, grad_values = (
        lax.psum_scatter(
            key_terms.astype(jnp.bfloat16), "ctx", scatter_dimension=0, tiled=True
        ).astype(jnp.float32),
        lax.psum_scatter(
            value_terms.astype(jnp.bfloat16), "ctx", scatter_dimension=0, tiled=True
        ).astype(jnp.float32),
    )
    grad_projected = jnp.concatenate(
        [grad_queries.astype(bf16), grad_keys.astype(bf16), grad_values.astype(bf16)], axis=1
    )
    grad_self_query_bias = jnp.sum(grad_projected[:, :width].astype(f32), axis=0)
    grad_self_value_bias = jnp.sum(grad_projected[:, 2 * width :].astype(f32), axis=0)
    grad_self_projection = jnp.dot(rows_in.T, grad_projected, preferred_element_type=f32)
    token_grad = (
        residual_scale * grad_first
        + jnp.dot(grad_projected, projection_full.T, preferred_element_type=f32)
    )[None]
    shares = (
        lax.psum_scatter(
            grad_self_projection.astype(jnp.bfloat16), "fsdp", scatter_dimension=0, tiled=True
        ).astype(jnp.float32),
        lax.psum_scatter(
            grad_self_output.astype(jnp.bfloat16), "fsdp", scatter_dimension=0, tiled=True
        ).astype(jnp.float32),
        lax.psum_scatter(
            grad_self_query_bias.astype(jnp.bfloat16), "fsdp", scatter_dimension=0, tiled=True
        ).astype(jnp.float32),
        lax.psum_scatter(
            grad_self_value_bias.astype(jnp.bfloat16), "fsdp", scatter_dimension=0, tiled=True
        ).astype(jnp.float32),
        lax.psum_scatter(
            grad_self_output_bias.astype(jnp.bfloat16), "fsdp", scatter_dimension=0, tiled=True
        ).astype(jnp.float32),
        lax.psum_scatter(
            grad_first_gain.astype(jnp.bfloat16), "fsdp", scatter_dimension=0, tiled=True
        ).astype(jnp.float32),
        lax.psum_scatter(
            grad_first_shift.astype(jnp.bfloat16), "fsdp", scatter_dimension=0, tiled=True
        ).astype(jnp.float32),
        lax.psum_scatter(
            grad_cross_query.astype(jnp.bfloat16), "fsdp", scatter_dimension=0, tiled=True
        ).astype(jnp.float32),
        lax.psum_scatter(
            grad_cross_memory.astype(jnp.bfloat16), "fsdp", scatter_dimension=0, tiled=True
        ).astype(jnp.float32),
        lax.psum_scatter(
            grad_cross_output.astype(jnp.bfloat16), "fsdp", scatter_dimension=0, tiled=True
        ).astype(jnp.float32),
        lax.psum_scatter(
            grad_cross_query_bias.astype(jnp.bfloat16), "fsdp", scatter_dimension=0, tiled=True
        ).astype(jnp.float32),
        lax.psum_scatter(
            grad_cross_value_bias.astype(jnp.bfloat16), "fsdp", scatter_dimension=0, tiled=True
        ).astype(jnp.float32),
        lax.psum_scatter(
            grad_cross_output_bias.astype(jnp.bfloat16), "fsdp", scatter_dimension=0, tiled=True
        ).astype(jnp.float32),
        lax.psum_scatter(
            grad_second_gain.astype(jnp.bfloat16), "fsdp", scatter_dimension=0, tiled=True
        ).astype(jnp.float32),
        lax.psum_scatter(
            grad_second_shift.astype(jnp.bfloat16), "fsdp", scatter_dimension=0, tiled=True
        ).astype(jnp.float32),
        lax.psum_scatter(
            grad_expand_weight.astype(jnp.bfloat16), "fsdp", scatter_dimension=0, tiled=True
        ).astype(jnp.float32),
        lax.psum_scatter(
            grad_reduce_weight.astype(jnp.bfloat16), "fsdp", scatter_dimension=0, tiled=True
        ).astype(jnp.float32),
        lax.psum_scatter(
            grad_expand_bias.astype(jnp.bfloat16), "fsdp", scatter_dimension=0, tiled=True
        ).astype(jnp.float32),
        lax.psum_scatter(
            grad_reduce_bias.astype(jnp.bfloat16), "fsdp", scatter_dimension=0, tiled=True
        ).astype(jnp.float32),
        lax.psum_scatter(
            grad_third_gain.astype(jnp.bfloat16), "fsdp", scatter_dimension=0, tiled=True
        ).astype(jnp.float32),
        lax.psum_scatter(
            grad_third_shift.astype(jnp.bfloat16), "fsdp", scatter_dimension=0, tiled=True
        ).astype(jnp.float32),
    )
    summed = (
        lax.psum(shares[0].astype(jnp.bfloat16), "ctx").astype(jnp.float32),
        lax.psum(shares[1].astype(jnp.bfloat16), "ctx").astype(jnp.float32),
        lax.psum(shares[2].astype(jnp.bfloat16), "ctx").astype(jnp.float32),
        lax.psum(shares[3].astype(jnp.bfloat16), "ctx").astype(jnp.float32),
        lax.psum(shares[4].astype(jnp.bfloat16), "ctx").astype(jnp.float32),
        lax.psum(shares[5].astype(jnp.bfloat16), "ctx").astype(jnp.float32),
        lax.psum(shares[6].astype(jnp.bfloat16), "ctx").astype(jnp.float32),
        lax.psum(shares[7].astype(jnp.bfloat16), "ctx").astype(jnp.float32),
        lax.psum(shares[8].astype(jnp.bfloat16), "ctx").astype(jnp.float32),
        lax.psum(shares[9].astype(jnp.bfloat16), "ctx").astype(jnp.float32),
        lax.psum(shares[10].astype(jnp.bfloat16), "ctx").astype(jnp.float32),
        lax.psum(shares[11].astype(jnp.bfloat16), "ctx").astype(jnp.float32),
        lax.psum(shares[12].astype(jnp.bfloat16), "ctx").astype(jnp.float32),
        lax.psum(shares[13].astype(jnp.bfloat16), "ctx").astype(jnp.float32),
        lax.psum(shares[14].astype(jnp.bfloat16), "ctx").astype(jnp.float32),
        lax.psum(shares[15].astype(jnp.bfloat16), "ctx").astype(jnp.float32),
        lax.psum(shares[16].astype(jnp.bfloat16), "ctx").astype(jnp.float32),
        lax.psum(shares[17].astype(jnp.bfloat16), "ctx").astype(jnp.float32),
        lax.psum(shares[18].astype(jnp.bfloat16), "ctx").astype(jnp.float32),
        lax.psum(shares[19].astype(jnp.bfloat16), "ctx").astype(jnp.float32),
        lax.psum(shares[20].astype(jnp.bfloat16), "ctx").astype(jnp.float32),
    )
    return (
        output,
        token_grad,
        memory_grad,
        summed[0],
        summed[1],
        summed[2],
        summed[3],
        summed[4],
        summed[5],
        summed[6],
        summed[7],
        summed[8],
        summed[9],
        summed[10],
        summed[11],
        summed[12],
        summed[13],
        summed[14],
        summed[15],
        summed[16],
        summed[17],
        summed[18],
        summed[19],
        summed[20],
    )


def solution(mesh):
    placed = (
        P("fsdp", "ctx", None),
        P("fsdp", "ctx", None),
        P("fsdp", "ctx", None),
        P("fsdp", None, None),
        P("fsdp", None),
        P("fsdp", None),
        P("fsdp", None),
        P("fsdp"),
        P("fsdp"),
        P("fsdp"),
        P("fsdp"),
        P("fsdp"),
        P("fsdp", None),
        P("fsdp", None),
        P("fsdp", None),
        P("fsdp"),
        P("fsdp"),
        P("fsdp"),
        P("fsdp"),
        P("fsdp"),
        P("fsdp", None),
        P("fsdp", None),
        P("fsdp"),
        P("fsdp"),
        P("fsdp"),
        P("fsdp"),
    )
    sizes = (mesh.shape["ctx"], mesh.shape["fsdp"])
    return jax.shard_map(
        tiled_shards if sizes == (4, 8) else plain_shards,
        mesh=mesh,
        in_specs=placed,
        out_specs=(
            P("fsdp", "ctx", None),
            P("fsdp", "ctx", None),
            P("fsdp", "ctx", None),
            P("fsdp", None),
            P("fsdp", None),
            P("fsdp"),
            P("fsdp"),
            P("fsdp"),
            P("fsdp"),
            P("fsdp"),
            P("fsdp", None),
            P("fsdp", None),
            P("fsdp", None),
            P("fsdp"),
            P("fsdp"),
            P("fsdp"),
            P("fsdp"),
            P("fsdp"),
            P("fsdp", None),
            P("fsdp", None),
            P("fsdp"),
            P("fsdp"),
            P("fsdp"),
            P("fsdp"),
        ),
        check_vma=False,
    )
```

```python
import functools
import math

import jax
import jax.numpy as jnp
from jax import lax
from jax.experimental import pallas as pl
from jax.experimental.layout import Layout, with_layout_constraint
from jax.experimental.pallas import tpu as pltpu
from jax.sharding import PartitionSpec as P

HEADS = 16
HEAD_DIM = 64
BLK = 256


epsilon = 1e-05
residual_scale = 18.0**0.25
score_scale = 0.125
masked_score = -1e30
gelu_coeff = math.sqrt(2.0 / math.pi)


def gelu_tanh(value):
    return 0.5 * value * (1.0 + jnp.tanh(gelu_coeff * (value + 0.044715 * value * value * value)))


def gelu_slope(value):
    inner = jnp.tanh(gelu_coeff * (value + 0.044715 * value * value * value))
    return 0.5 * (1.0 + inner) + 0.5 * value * (1.0 - inner * inner) * gelu_coeff * (
        1.0 + 3.0 * 0.044715 * value * value
    )


def layer_norm(summed, gain, shift):
    centred = summed - jnp.mean(summed, axis=-1, keepdims=True)
    inverse = lax.rsqrt(jnp.mean(centred * centred, axis=-1, keepdims=True) + epsilon)
    normed = centred * inverse
    return (normed * gain + shift, normed, inverse)


def layer_norm_back(upstream, gain, normed, inverse):
    scaled = upstream * gain
    inner = (
        scaled
        - jnp.mean(scaled, axis=-1, keepdims=True)
        - normed * jnp.mean(scaled * normed, axis=-1, keepdims=True)
    )
    return (inner * inverse, jnp.sum(upstream * normed, axis=0), jnp.sum(upstream, axis=0))


score_log2 = 0.125 * math.log2(math.e)
NT = (((1,), (1,)), ((), ()))
NN = (((1,), (0,)), ((), ()))
TN = (((0,), (0,)), ((), ()))


def mxu(left, right, dims):
    return lax.dot_general(left, right, dims, preferred_element_type=jnp.float32)


def two_heads(pair):
    low = lax.broadcasted_iota(jnp.int32, pair.shape, 1) < 64
    zero = jnp.zeros_like(pair)
    return jnp.concatenate([jnp.where(low, pair, zero), jnp.where(low, zero, pair)], axis=0)


def one_pair(stacked):
    rows = stacked.shape[0] // 2
    top = stacked[:rows]
    low = lax.broadcasted_iota(jnp.int32, top.shape, 1) < 64
    return jnp.where(low, top, stacked[rows:])


def place_of(order_ref, slot_ref, index, per_group):
    return order_ref[slot_ref[0] ^ (index // per_group)] * per_group + index % per_group


def seen(scalars, query_index, key_index, per_group, count):
    if scalars is None:
        return None
    order_ref, map_ref, slot_ref = scalars
    row = place_of(order_ref, slot_ref, query_index, per_group)
    column = place_of(order_ref, slot_ref, key_index, per_group)
    return map_ref[row * count + column] > 0


def guarded(flag, work):
    if flag is None:
        work()
    else:
        pl.when(flag)(work)


def pair_lanes(unit):
    return slice(unit * 128, (unit + 1) * 128)


def forward_body(masked, units, chunks, key_rows, pieces, per_group, *refs):
    scalars = None
    if masked:
        scalars, refs = refs[:3], refs[3:]
    q_ref, refs = refs[0], refs[1:]
    k_refs, v_refs, refs = refs[:pieces], refs[pieces:2 * pieces], refs[2 * pieces:]
    o_ref, lse_ref, stacked, scores, top, shift, total, acc = refs
    rows = stacked.shape[1]
    query_index = pl.program_id(1)

    def part(ref_list, chunk, unit):
        if pieces > 1:
            return ref_list[chunk][:, pair_lanes(unit)]
        return ref_list[0][chunk * key_rows:(chunk + 1) * key_rows, pair_lanes(unit)]

    for unit in range(units):
        stacked[unit] = two_heads(q_ref[:, pair_lanes(unit)])
        top[unit] = jnp.full((rows, 128), -1e30, jnp.float32)
        total[unit] = jnp.zeros((rows, 128), jnp.float32)
        acc[unit] = jnp.zeros((rows, 128), jnp.float32)
    for chunk in range(chunks):
        flag = seen(scalars, query_index, chunk, per_group, chunks)

        def scan_max(chunk=chunk):
            for unit in range(units):
                found = mxu(stacked[unit], part(k_refs, chunk, unit), NT)
                scores[unit, chunk] = found
                best = top[unit]
                for lane in range(0, key_rows, 128):
                    best = jnp.maximum(best, found[:, lane:lane + 128])
                top[unit] = best

        guarded(flag, scan_max)
    for unit in range(units):
        peak = jnp.max(top[unit], axis=1, keepdims=True) * score_log2
        shift[unit] = jnp.broadcast_to(peak, (rows, 128))
    for chunk in range(chunks):
        flag = seen(scalars, query_index, chunk, per_group, chunks)

        def weigh(chunk=chunk):
            for unit in range(units):
                found = scores[unit, chunk]
                offset = shift[unit]
                summed = total[unit]
                parts = []
                for lane in range(0, key_rows, 128):
                    weight = jnp.exp2(found[:, lane:lane + 128] * score_log2 - offset)
                    summed = summed + weight
                    parts.append(weight.astype(jnp.bfloat16))
                total[unit] = summed
                acc[unit] = acc[unit] + mxu(jnp.concatenate(parts, axis=1), part(v_refs, chunk, unit), NN)

        guarded(flag, weigh)
    for unit in range(units):
        row_sum = jnp.sum(total[unit], axis=1, keepdims=True)
        o_ref[:, pair_lanes(unit)] = one_pair(acc[unit] / row_sum).astype(o_ref.dtype)
        lse = shift[unit] + jnp.log2(row_sum)
        lse_ref[unit] = lse.T[:8]


def backward_body(masked, units, chunks, key_rows, pieces, per_group, *refs):
    scalars = None
    if masked:
        scalars, refs = refs[:3], refs[3:]
    q_ref, do_ref, o_ref, lse_ref, refs = refs[0], refs[1], refs[2], refs[3], refs[4:]
    k_refs, v_refs, refs = refs[:pieces], refs[pieces:2 * pieces], refs[2 * pieces:]
    dq_ref, dk_refs, dv_refs, refs = refs[0], refs[1:1 + pieces], refs[1 + pieces:1 + 2 * pieces], refs[1 + 2 * pieces:]
    stacked, grads, delta, dq_acc, dk_acc, dv_acc = refs
    query_index = pl.program_id(1)

    @pl.when(query_index == 0)
    def clear():
        dk_acc[...] = jnp.zeros_like(dk_acc)
        dv_acc[...] = jnp.zeros_like(dv_acc)

    for unit in range(units):
        lanes = pair_lanes(unit)
        stacked[unit] = two_heads(q_ref[:, lanes])
        upstream = do_ref[:, lanes]
        grads[unit] = two_heads(upstream)
        product = (upstream.astype(jnp.float32) * o_ref[:, lanes].astype(jnp.float32)).T
        first = jnp.sum(product[:64], axis=0, keepdims=True)
        second = jnp.sum(product[64:], axis=0, keepdims=True)
        delta[unit] = jnp.broadcast_to(jnp.concatenate([first, second], axis=1), delta.shape[1:])
        dq_acc[unit] = jnp.zeros(dq_acc.shape[1:], jnp.float32)
    def step(first, count):
        rows = slice(first * key_rows, (first + count) * key_rows)
        for unit in range(units):
            queries, upstream = stacked[unit], grads[unit]
            keys, values = k_refs[0][rows, pair_lanes(unit)], v_refs[0][rows, pair_lanes(unit)]
            found = mxu(keys, queries, NT)
            probs = jnp.exp2(found * score_log2 - lse_ref[unit, 0:1])
            grad_probs = mxu(values, upstream, NT)
            grad_scores = (probs * (grad_probs - delta[unit, 0:1])).astype(jnp.bfloat16)
            dv_acc[unit, rows] += mxu(probs.astype(jnp.bfloat16), upstream, NN)
            dk_acc[unit, rows] += mxu(grad_scores, queries, NN)
            dq_acc[unit] += mxu(grad_scores, keys, TN)

    if masked:
        for chunk in range(0, chunks, 2):
            first = seen(scalars, query_index, chunk, per_group, chunks)
            second = seen(scalars, query_index, chunk + 1, per_group, chunks)
            pl.when(first & second)(functools.partial(step, chunk, 2))
            pl.when(first & jnp.logical_not(second))(functools.partial(step, chunk, 1))
            pl.when(second & jnp.logical_not(first))(functools.partial(step, chunk + 1, 1))
    else:
        for chunk in range(chunks):
            step(chunk, 1)
    for unit in range(units):
        dq_ref[:, pair_lanes(unit)] = (one_pair(dq_acc[unit]) * 0.125).astype(dq_ref.dtype)

    @pl.when(query_index == pl.num_programs(1) - 1)
    def finish():
        for unit in range(units):
            dk_refs[0][:, pair_lanes(unit)] = (dk_acc[unit] * 0.125).astype(jnp.bfloat16)
            dv_refs[0][:, pair_lanes(unit)] = dv_acc[unit].astype(jnp.bfloat16)


def attention_forward(q, q_col, k_list, k_col, v_list, v_col, width, scalars, key_rows, units=2, per_group=2):
    pieces = len(k_list)
    lanes = units * 128
    rows = q.shape[0]
    keys = sum(k.shape[0] for k in k_list)
    chunks = keys // key_rows
    groups, blocks = width // lanes, rows // BLK
    masked = scalars is not None
    spec_q = pl.BlockSpec((BLK, lanes), lambda h, i, *_: (i, q_col + h))
    specs_k = [pl.BlockSpec((k.shape[0], lanes), lambda h, i, *_: (0, k_col + h)) for k in k_list]
    specs_v = [pl.BlockSpec((v.shape[0], lanes), lambda h, i, *_: (0, v_col + h)) for v in v_list]
    body = functools.partial(forward_body, masked, units, chunks, key_rows, pieces, per_group)
    pairs = rows * keys * (width // 64)
    return pl.pallas_call(
        body,
        grid_spec=pltpu.PrefetchScalarGridSpec(
            num_scalar_prefetch=3 if masked else 0,
            grid=(groups, blocks),
            in_specs=[spec_q] + specs_k + specs_v,
            out_specs=[
                pl.BlockSpec((BLK, lanes), lambda h, i, *_: (i, h)),
                pl.BlockSpec((units, 8, 2 * BLK), lambda h, i, *_: (h, 0, i)),
            ],
            scratch_shapes=[
                pltpu.VMEM((units, 2 * BLK, 128), jnp.bfloat16),
                pltpu.VMEM((units, chunks, 2 * BLK, key_rows), jnp.float32),
                pltpu.VMEM((units, 2 * BLK, 128), jnp.float32),
                pltpu.VMEM((units, 2 * BLK, 128), jnp.float32),
                pltpu.VMEM((units, 2 * BLK, 128), jnp.float32),
                pltpu.VMEM((units, 2 * BLK, 128), jnp.float32),
            ],
        ),
        out_shape=[
            jax.ShapeDtypeStruct((rows, width), jnp.bfloat16),
            jax.ShapeDtypeStruct((width // 128, 8, blocks * 2 * BLK), jnp.float32),
        ],
        compiler_params=pltpu.CompilerParams(vmem_limit_bytes=48 << 20),
        cost_estimate=pl.CostEstimate(flops=pairs * 512, transcendentals=pairs, bytes_accessed=4 * (rows + keys) * width),
    )(*(scalars or ()), q, *k_list, *v_list)


def attention_backward(q, q_col, do, o, lse, k_list, k_col, v_list, v_col, width, scalars, key_rows, units=2, per_group=2, o_col=0):
    pieces = len(k_list)
    lanes = units * 128
    rows = q.shape[0]
    keys = sum(k.shape[0] for k in k_list)
    chunks = keys // key_rows
    groups, blocks = width // lanes, rows // BLK
    masked = scalars is not None
    spec_q = pl.BlockSpec((BLK, lanes), lambda h, i, *_: (i, q_col + h))
    spec_o = pl.BlockSpec((BLK, lanes), lambda h, i, *_: (i, o_col + h))
    spec_dq = pl.BlockSpec((BLK, lanes), lambda h, i, *_: (i, h))
    spec_lse = pl.BlockSpec((units, 8, 2 * BLK), lambda h, i, *_: (o_col + h, 0, i))
    specs_k = [pl.BlockSpec((k.shape[0], lanes), lambda h, i, *_: (0, k_col + h)) for k in k_list]
    specs_v = [pl.BlockSpec((v.shape[0], lanes), lambda h, i, *_: (0, v_col + h)) for v in v_list]
    outs_k = [pl.BlockSpec((k.shape[0], lanes), lambda h, i, *_: (0, h)) for k in k_list]
    body = functools.partial(backward_body, masked, units, chunks, key_rows, pieces, per_group)
    pairs = rows * keys * (width // 64)
    shape_k = [jax.ShapeDtypeStruct((k.shape[0], width), jnp.bfloat16) for k in k_list]
    return pl.pallas_call(
        body,
        grid_spec=pltpu.PrefetchScalarGridSpec(
            num_scalar_prefetch=3 if masked else 0,
            grid=(groups, blocks),
            in_specs=[spec_q, spec_o, spec_o, spec_lse] + specs_k + specs_v,
            out_specs=[spec_dq] + outs_k + outs_k,
            scratch_shapes=[
                pltpu.VMEM((units, 2 * BLK, 128), jnp.bfloat16),
                pltpu.VMEM((units, 2 * BLK, 128), jnp.bfloat16),
                pltpu.VMEM((units, 8, 2 * BLK), jnp.float32),
                pltpu.VMEM((units, 2 * BLK, 128), jnp.float32),
                pltpu.VMEM((units, keys, 128), jnp.float32),
                pltpu.VMEM((units, keys, 128), jnp.float32),
            ],
        ),
        out_shape=[jax.ShapeDtypeStruct((rows, width), jnp.bfloat16)] + shape_k + shape_k,
        compiler_params=pltpu.CompilerParams(vmem_limit_bytes=48 << 20),
        cost_estimate=pl.CostEstimate(flops=pairs * 1280, transcendentals=pairs, bytes_accessed=8 * (rows + keys) * width),
    )(*(scalars or ()), q, do, o, lse, *k_list, *v_list)


def norm_sums(summed):
    mean = jnp.mean(summed, axis=-1, keepdims=True)
    centred = summed - mean
    inverse = lax.rsqrt(jnp.mean(centred * centred, axis=-1, keepdims=True) + epsilon)
    return centred * inverse, inverse


def feed_body(
    core_ref, hidden_ref, upstream_ref, weights_ref, expand_bias_ref, vectors_ref,
    out_ref, grad_hidden_ref, send_ref, keep_ref, grad_bias_ref, sums_ref,
    low, expanded, activated, total, grad_low,
):
    step = pl.program_id(0)
    blocks = pl.num_programs(0) // 2
    block = step % blocks
    width = hidden_ref.shape[1]
    first = weights_ref[:, 0, :128].reshape(width, width)
    second = weights_ref[:, 0, 128:].reshape(width, width)

    @pl.when(step == 0)
    def begin():
        low[...] = hidden_ref[...].astype(jnp.bfloat16)
        total[...] = residual_scale * hidden_ref[...] + vectors_ref[0:1]

    @pl.when(step < blocks)
    def forward():
        wide = mxu(low[...], first, NN) + expand_bias_ref[0]
        expanded[block] = wide
        active = gelu_tanh(wide).astype(jnp.bfloat16)
        activated[block] = active
        total[...] += mxu(active, second, NN)

    @pl.when(step == blocks)
    def turn():
        normed, inverse = norm_sums(total[...])
        gain = vectors_ref[1:2]
        out_ref[...] = (normed * gain + vectors_ref[2:3]).astype(out_ref.dtype)
        upstream = upstream_ref[...].astype(jnp.float32)
        scaled = upstream * gain
        grad = inverse * (
            scaled
            - jnp.mean(scaled, axis=-1, keepdims=True)
            - normed * jnp.mean(scaled * normed, axis=-1, keepdims=True)
        )
        grad_low[...] = grad.astype(jnp.bfloat16)
        grad_hidden_ref[...] = residual_scale * grad
        sums_ref[0:1] = jnp.sum(grad_low[...].astype(jnp.float32), axis=0, keepdims=True)
        sums_ref[1:2] = jnp.sum(upstream * normed, axis=0, keepdims=True)
        sums_ref[2:3] = jnp.sum(upstream, axis=0, keepdims=True)

    @pl.when(step >= blocks)
    def backward():
        grad_active = mxu(grad_low[...], second, NT)
        grad_wide = (grad_active * gelu_slope(expanded[block])).astype(jnp.bfloat16)
        grad_second = mxu(activated[block], grad_low[...], TN).astype(jnp.bfloat16).reshape(-1, 128, width)
        grad_first = mxu(low[...], grad_wide, TN).astype(jnp.bfloat16).reshape(-1, 128, width)

        @pl.when(block < blocks // 2)
        def to_send():
            send_ref[:, 0, 128:] = grad_second
            send_ref[:, 0, :128] = grad_first

        @pl.when(block >= blocks // 2)
        def to_keep():
            keep_ref[:, 0, 128:] = grad_second
            keep_ref[:, 0, :128] = grad_first

        grad_bias_ref[0] = jnp.sum(grad_wide.astype(jnp.float32), axis=0, keepdims=True)
        grad_hidden_ref[...] += mxu(grad_wide, first, NT)


def feed_forward(core, hidden, upstream, weights, expand_bias, vectors):
    rows, width = hidden.shape
    groups, blocks = weights.shape[:2]
    half = blocks // 2

    def at(i, core_ref):
        return (i + half * (1 - core_ref[0])) % blocks

    def back(i, core_ref):
        return (jnp.maximum(i - blocks, 0) + half * (1 - core_ref[0])) % blocks

    whole = pl.BlockSpec((rows, width), lambda i, c: (0, 0))
    once = pl.BlockSpec((rows, width), lambda i, c: (0, 0), pipeline_mode=pl.Buffered(1))
    f32, bf16 = jnp.float32, jnp.bfloat16
    part = (groups, 1, 256, width)
    return pl.pallas_call(
        feed_body,
        grid_spec=pltpu.PrefetchScalarGridSpec(
            num_scalar_prefetch=1,
            grid=(2 * blocks,),
            in_specs=[
                once, once,
                pl.BlockSpec(part, lambda i, c: (0, at(i, c), 0, 0)),
                pl.BlockSpec((1, 1, width), lambda i, c: (at(i, c), 0, 0)),
                pl.BlockSpec((8, width), lambda i, c: (0, 0)),
            ],
            out_specs=[
                whole, whole,
                pl.BlockSpec(part, lambda i, c: (0, jnp.clip(i - blocks, 0, half - 1), 0, 0)),
                pl.BlockSpec(part, lambda i, c: (0, jnp.clip(i - blocks - half, 0, half - 1), 0, 0)),
                pl.BlockSpec((1, 1, width), lambda i, c: (back(i, c), 0, 0)),
                pl.BlockSpec((8, width), lambda i, c: (0, 0)),
            ],
            scratch_shapes=[
                pltpu.VMEM((rows, width), bf16),
                pltpu.VMEM((blocks, rows, width), f32),
                pltpu.VMEM((blocks, rows, width), bf16),
                pltpu.VMEM((rows, width), f32),
                pltpu.VMEM((rows, width), bf16),
            ],
        ),
        out_shape=[
            jax.ShapeDtypeStruct((rows, width), bf16),
            jax.ShapeDtypeStruct((rows, width), f32),
            jax.ShapeDtypeStruct((groups, half, 256, width), bf16),
            jax.ShapeDtypeStruct((groups, half, 256, width), bf16),
            jax.ShapeDtypeStruct((blocks, 1, width), f32),
            jax.ShapeDtypeStruct((8, width), f32),
        ],
        compiler_params=pltpu.CompilerParams(vmem_limit_bytes=60 << 20),
        cost_estimate=pl.CostEstimate(flops=12 * rows * width * width * blocks, transcendentals=2 * rows * width * blocks, bytes_accessed=52 << 20),
    )(core.reshape(1).astype(jnp.int32), hidden, upstream, weights, expand_bias, vectors)


def core_perm():
    return [(c, c ^ 1) for c in range(4)]


def y_perm():
    return [(c, c ^ 2) for c in range(4)]


def diagonal_perm():
    return [(c, c ^ 3) for c in range(4)]


def x_perm():
    return [(f, f ^ 1) for f in range(8)]


def z_perm(k):
    return [(f, f ^ (2 * k)) for f in range(8)]


def to_core(v):
    return lax.ppermute(v, "ctx", core_perm())


def to_y(v):
    return lax.ppermute(v, "ctx", y_perm())


def to_diagonal(v):
    return lax.ppermute(v, "ctx", diagonal_perm())


def to_x(v):
    return lax.ppermute(v, "fsdp", x_perm())


def to_z(v, k):
    return lax.ppermute(v, "fsdp", z_perm(k))


def fsdp_pieces(own):
    along = [own] + [to_z(own, k) for k in (1, 2, 3)]
    return along + [to_x(piece) for piece in along]


def fsdp_sources(me):
    return [me ^ (2 * k + d) for d in (0, 1) for k in range(4)]


def place_body(plan, *refs):
    offsets, refs = refs[0], refs[1:]
    outs, sems = refs[-1 - len(plan):-1], refs[-1]
    pieces = refs[:-1 - len(plan)]
    copies = []
    for i, piece in enumerate(pieces):
        for s, (lead, first, rows) in enumerate(plan):
            source = piece if lead is None else piece.at[lead]
            start = pl.multiple_of(offsets[i] * rows, rows)
            copy = pltpu.make_async_copy(source.at[pl.ds(first, rows)], outs[s].at[pl.ds(start, rows)], sems.at[i, s])
            copy.start()
            copies.append(copy)
    for copy in copies:
        copy.wait()


def place(pieces, slots, plan):
    columns = pieces[0].shape[-1]
    count = len(pieces)
    out = [jax.ShapeDtypeStruct((count * rows, columns), pieces[0].dtype) for _, _, rows in plan]
    anywhere = pl.BlockSpec(memory_space=pl.ANY)
    moved = 4 * count * columns * sum(rows for _, _, rows in plan)
    return pl.pallas_call(
        functools.partial(place_body, plan),
        in_specs=[pl.BlockSpec(memory_space=pltpu.SMEM)] + [anywhere] * count,
        out_specs=[pl.BlockSpec(memory_space=pltpu.VMEM)] * len(plan),
        out_shape=out,
        scratch_shapes=[pltpu.SemaphoreType.DMA((count, len(plan)))],
        compiler_params=pltpu.CompilerParams(vmem_limit_bytes=(moved // 2) + (4 << 20)),
        cost_estimate=pl.CostEstimate(flops=0, transcendentals=0, bytes_accessed=moved),
    )(jnp.stack(slots).astype(jnp.int32), *pieces)


def after(value, other):
    return lax.optimization_barrier((value, other))[0]


def xor_take(stack, me):
    return jnp.concatenate([lax.dynamic_index_in_dim(stack, n ^ me, 0) for n in range(stack.shape[0])])


def from_fsdp(blocks):
    got = lax.all_to_all(blocks, "fsdp", 0, 0)
    return jnp.sum(got.astype(jnp.float32), axis=0)


def part_of(parts, index, axis):
    return lax.dynamic_index_in_dim(parts, index, axis, keepdims=False)


def added(keep, got):
    return (keep.astype(jnp.float32) + got.astype(jnp.float32)).astype(jnp.bfloat16)


def halves_dot(pairs, core):
    def side(index):
        terms = []
        for left, right in pairs:
            half = right.shape[1] // 2
            chosen = lax.dynamic_slice_in_dim(right, index * half, half, axis=1)
            terms.append(jnp.dot(left.T, chosen, preferred_element_type=jnp.float32).astype(jnp.bfloat16))
        return with_layout_constraint(jnp.concatenate(terms, axis=1), Layout(major_to_minor=(0, 1)))

    return side(core), side(core ^ 1)


def over_z(parts, z):
    got = [to_z(part_of(parts, z ^ k, 1), k) for k in (1, 2, 3)]
    total = part_of(parts, z, 1).astype(jnp.float32)
    return (total + got[0].astype(jnp.float32) + got[1].astype(jnp.float32) + got[2].astype(jnp.float32)).astype(jnp.bfloat16)


def ctx_pieces(own):
    line = to_y(own)
    return [own, to_core(own), line, to_core(line)]


def spread_feed_body(core_ref, *refs):
    (own, other), (expand_ref, reduce_ref) = refs[:2], refs[2:]
    for index, source in ((core_ref[0], own), (1 - core_ref[0], other)):
        for p in range(2):
            at = pl.multiple_of(index * 256 + p * 128, 128)
            reduce_ref[pl.ds(at, 128), :] = source[p, 128:].astype(jnp.float32)
            for f in range(8):
                expand_ref[:, pl.ds(at + f * 512, 128)] = source[p, :128, f * 128:(f + 1) * 128].astype(jnp.float32)


def spread_projection_body(me_ref, *refs):
    pieces, (out_ref, vectors_ref) = refs[:4], refs[4:]
    total = jnp.zeros((8, 384), jnp.float32)
    for k in range(4):
        at = pl.multiple_of((me_ref[0] ^ k) * 256, 128)
        for part in range(3):
            for pair in range(2):
                source = pieces[k][:128, pair * 384 + part * 128:pair * 384 + (part + 1) * 128]
                out_ref[:, pl.ds(at + part * 1024 + pair * 128, 128)] = source.astype(jnp.float32)
        total = total + pieces[k][128:136, 384:].astype(jnp.float32)
    for i in range(18):
        vectors_ref[i:i + 1] = total[i // 3:i // 3 + 1, (i % 3) * 128:(i % 3 + 1) * 128]


def spread_middle_body(core_ref, *refs):
    (early, early_other, late, late_other), (memory_ref, query_ref, cross_ref, self_ref) = refs[:4], refs[4:]
    for index, first, second in ((core_ref[0], early, late), (1 - core_ref[0], early_other, late_other)):
        for half, source in ((0, first), (512, second)):
            at = pl.multiple_of(half + index * 256, 256)
            memory_ref[:, pl.ds(at, 256)] = source[:, 0:256].astype(jnp.float32)
            memory_ref[:, pl.ds(at + 1024, 256)] = source[:, 256:512].astype(jnp.float32)
            query_ref[:, pl.ds(at, 256)] = source[:, 512:768].astype(jnp.float32)
        at = pl.multiple_of(index * 512, 512)
        cross_ref[:, pl.ds(at, 512)] = first[:, 768:].astype(jnp.float32)
        self_ref[:, pl.ds(at, 512)] = second[:, 768:].astype(jnp.float32)


def spread(body, index, pieces, shapes):
    whole = pl.BlockSpec(memory_space=pltpu.VMEM)
    moved = sum(p.size * 2 for p in pieces) + sum(a * b * 4 for a, b in shapes)
    return pl.pallas_call(
        body,
        in_specs=[pl.BlockSpec(memory_space=pltpu.SMEM)] + [whole] * len(pieces),
        out_specs=[whole] * len(shapes),
        out_shape=[jax.ShapeDtypeStruct(shape, jnp.float32) for shape in shapes],
        compiler_params=pltpu.CompilerParams(vmem_limit_bytes=moved + (4 << 20)),
        cost_estimate=pl.CostEstimate(flops=0, transcendentals=0, bytes_accessed=moved),
    )(index.reshape(1).astype(jnp.int32), *pieces)


def chip_sums(terms, rows):
    pairs = terms.reshape(2, 2, rows, terms.shape[1])
    got = to_core(pairs[:, 1])
    return pairs[0, 0].astype(jnp.float32) + got[0].astype(jnp.float32), added(pairs[1, 0], got[1])


def tiled_shards(
    tokens,
    memory,
    cotangent,
    block_map,
    block_order,
    self_projection,
    self_output,
    self_query_bias,
    self_value_bias,
    self_output_bias,
    first_gain,
    first_shift,
    cross_query,
    cross_memory,
    cross_output,
    cross_query_bias,
    cross_value_bias,
    cross_output_bias,
    second_gain,
    second_shift,
    expand_weight,
    reduce_weight,
    expand_bias,
    reduce_bias,
    third_gain,
    third_shift,
):
    bf16 = jnp.bfloat16
    f32 = jnp.float32
    own_rows = tokens[0]
    rows, width = own_rows.shape
    me_c, me_f = lax.axis_index("ctx"), lax.axis_index("fsdp")
    core, line, z, x = me_c % 2, me_c // 2, me_f // 2, me_f % 2
    share = width // 4

    def dot(left, right):
        return jnp.dot(left, right, preferred_element_type=f32)

    vectors = [self_query_bias, self_value_bias, self_output_bias, first_gain, first_shift, cross_query_bias,
               cross_value_bias, cross_output_bias, second_gain, second_shift, reduce_bias, third_gain, third_shift]
    vectors += [expand_bias[i * 128:(i + 1) * 128] for i in range(4)] + [jnp.zeros((128,), bf16)]
    vector_rows = jnp.stack([jnp.concatenate(vectors[i * 6:i * 6 + 6]) for i in range(3)])
    columns = [lax.dynamic_slice(self_projection, (0, part * width + me_c * share), (128, share)) for part in range(3)]
    own_piece = jnp.concatenate([jnp.concatenate(columns, axis=1), vector_rows, jnp.zeros((13, 3 * share), bf16)])
    projection_pieces = fsdp_pieces(own_piece)
    rows_y = to_y(own_rows)
    rows_core = to_core(own_rows)
    rows_diagonal = to_core(after(rows_y, projection_pieces[1:4]))
    sequence = jnp.concatenate([own_rows, rows_core, rows_y, rows_diagonal])
    sources = fsdp_sources(me_f)
    projection, vector_blocks = place(projection_pieces, sources, ((None, 0, 128), (None, 128, 16)))
    vector_blocks = vector_blocks.reshape(8, 16, 3 * share).astype(f32)
    gathered = [vector_blocks[:, i // 6, (i % 6) * 128:(i % 6 + 1) * 128].reshape(width) for i in range(17)]
    (query_bias, value_bias, out_bias, gain_one, shift_one, cross_qbias, cross_vbias, cross_obias,
     gain_two, shift_two, reduce_bias_full, gain_three, shift_three) = gathered[:13]
    expand_bias_blocks = jnp.stack(gathered[13:]).reshape(4, 1, width)

    middle = [cross_memory[:, :width], cross_memory[:, width:], self_output, cross_query, cross_output]
    middle_own = jnp.stack([lax.dynamic_slice_in_dim(weight, me_c * 32, 32) for weight in middle])
    middle_all = lax.all_gather(middle_own, ("fsdp", "ctx"), axis=0)
    memory_key_full, memory_value_full, self_out_full, cross_query_full, cross_out_full = [
        middle_all[:, i].reshape(width, width) for i in range(5)
    ]
    expand_columns = lax.dynamic_index_in_dim(expand_weight.reshape(128, 8, 4, 128), me_c, 2, keepdims=False)
    feed_own = jnp.concatenate([expand_columns.reshape(128, width), lax.dynamic_slice_in_dim(reduce_weight, me_c * 128, 128)])

    memory_rows = memory[0]
    memory_y = to_y(after(memory_rows, projection_pieces[4:]))
    memory_core = to_core(memory_rows)

    projected = dot(sequence, projection)
    bias = jnp.concatenate([
        lax.dynamic_slice_in_dim(query_bias, me_c * share, share),
        jnp.zeros((share,), f32),
        lax.dynamic_slice_in_dim(value_bias, me_c * share, share),
    ])
    qkv = (projected + bias).astype(bf16)
    scalars = (block_order[0], block_map[0].reshape(-1), me_c.reshape(1).astype(jnp.int32))
    heads_out, self_lse = attention_forward(qkv, 0, [qkv], 1, [qkv], 2, share, scalars, BLK)
    heads_out, memory_y = lax.optimization_barrier((heads_out, memory_y))
    memory_all = jnp.concatenate([memory_rows, memory_core, memory_y, to_core(memory_y)])

    feed_weights = lax.all_gather(after(feed_own, (middle_all, heads_out)), ("fsdp", "ctx"), axis=0, tiled=True)
    memory_keys = dot(memory_all, memory_key_full).astype(bf16)
    memory_values = (dot(memory_all, memory_value_full) + cross_vbias).astype(bf16)

    pieces = [heads_out[i * rows:(i + 1) * rows] for i in range(4)]
    others = after([to_core(pieces[1]), to_y(pieces[2]), to_diagonal(pieces[3])], (memory_keys, memory_values))
    arrived = jnp.stack([pieces[0]] + others)
    attended = jnp.concatenate([part_of(arrived, n ^ me_c, 0) for n in range(4)], axis=1)
    branch = dot(attended, self_out_full) + out_bias
    hidden_one, normed_one, inverse_one = layer_norm(residual_scale * own_rows.astype(f32) + branch, gain_one, shift_one)

    hidden_low = hidden_one.astype(bf16)
    cross_queries = (dot(hidden_low, cross_query_full) + cross_qbias).astype(bf16)
    cross_low, cross_lse = attention_forward(cross_queries, 0, [memory_keys], 0, [memory_values], 0, width, None, rows)
    cross_branch = dot(cross_low, cross_out_full) + cross_obias
    hidden_two, normed_two, inverse_two = layer_norm(residual_scale * hidden_one + cross_branch, gain_two, shift_two)

    feed_vectors = jnp.concatenate([jnp.stack([reduce_bias_full, gain_three, shift_three]), jnp.zeros((5, width), f32)])
    output, grad_hidden_two, feed_send, feed_keep, grad_expand_bias, feed_sums = feed_forward(
        core, hidden_two, cotangent[0], feed_weights.reshape(8, 4, 256, width), expand_bias_blocks, feed_vectors
    )
    feed_got = to_core(feed_send)

    grad_second, grad_second_gain, grad_second_shift = layer_norm_back(grad_hidden_two, gain_two, normed_two, inverse_two)
    grad_cross_branch = grad_second.astype(bf16)
    grad_cross_output_bias = jnp.sum(grad_cross_branch.astype(f32), axis=0)
    grad_cross_low = dot(grad_cross_branch, cross_out_full.T).astype(bf16)

    def cross_half(half, queries):
        return attention_backward(
            queries, 2 * half, grad_cross_low, cross_low, cross_lse, [memory_keys], 2 * half, [memory_values], 2 * half,
            width // 2, None, rows, o_col=2 * half
        )

    def line_split(summed):
        return summed.reshape(8, 2, 64, summed.shape[1])

    early_q, early_k, early_v = cross_half(0, cross_queries)
    feed_keep, feed_got = after((feed_keep, feed_got), early_q)
    feed_half = added(feed_keep, feed_got).reshape(8 * 512, width)
    feed_share = lax.psum_scatter(feed_half, "fsdp", scatter_dimension=0, tiled=True)
    first_q, first_k, first_v = after((early_q, early_k, early_v), feed_half)
    keep, send = halves_dot(
        [(memory_all, first_k), (memory_all, first_v), (hidden_low, first_q), (cross_low, grad_cross_branch)], core
    )
    early_got = to_core(send)
    late_q, late_k, late_v = cross_half(1, after(cross_queries, (keep, send)))
    late_q, late_k, late_v, early_got = lax.optimization_barrier((late_q, late_k, late_v, early_got))
    early = line_split(added(keep, early_got))
    early_send = part_of(early, line ^ 1, 1)
    early_got = to_y(early_send)
    late_q, early_q = after((late_q, early_q), early_send)

    grad_cross_queries = jnp.concatenate([early_q, late_q], axis=1)
    grad_cross_query_bias = jnp.sum(grad_cross_queries.astype(f32), axis=0)
    grad_hidden_one = residual_scale * grad_second + dot(grad_cross_queries, cross_query_full.T)
    grad_first, grad_first_gain, grad_first_shift = layer_norm_back(grad_hidden_one, gain_one, normed_one, inverse_one)
    grad_branch = grad_first.astype(bf16)
    grad_self_output_bias = jnp.sum(grad_branch.astype(f32), axis=0)
    grad_attended = dot(grad_branch, self_out_full.T).astype(bf16)
    by_heads = jnp.stack([grad_attended[:, i * share:(i + 1) * share] for i in range(4)])
    sends = [part_of(by_heads, k ^ me_c, 0) for k in range(4)]
    received = [to_core(sends[1]), to_y(sends[2]), to_diagonal(sends[3])]
    heads_grad = jnp.concatenate([sends[0]] + received)

    ready_q, ready_k, ready_v, ready_branch = after((late_q, late_k, late_v, grad_branch), received[0])
    grad_cross_value_bias = jnp.concatenate([jnp.sum(early_v.astype(f32), axis=0), jnp.sum(ready_v.astype(f32), axis=0)])
    memory_terms = dot(jnp.concatenate([early_k, early_v, ready_k, ready_v], axis=1), jnp.concatenate([
        memory_key_full[:, :width // 2], memory_value_full[:, :width // 2],
        memory_key_full[:, width // 2:], memory_value_full[:, width // 2:],
    ], axis=1).T).astype(bf16)
    memory_near, memory_far = chip_sums(memory_terms, rows)
    late_keep, late_send = halves_dot(
        [(memory_all, ready_k), (memory_all, ready_v), (hidden_low, ready_q), (attended, ready_branch)], core
    )
    late_got = to_core(late_send)
    early = added(part_of(early, line, 1), early_got).reshape(4, 2, 64, 5 * share)

    def heads_back(pair, upstream):
        return attention_backward(
            qkv, pair, upstream, heads_out, self_lse, [qkv], 2 + pair, [qkv], 4 + pair, share // 2, scalars, BLK,
            units=1, o_col=pair,
        )

    def own_blocks(grads):
        return dot(sequence.T, grads).astype(bf16).reshape(8, 128, grads.shape[1])

    vector_grads = jnp.concatenate([
        jnp.stack([
            grad_self_output_bias, grad_first_gain, grad_first_shift, grad_cross_query_bias, grad_cross_value_bias,
            grad_cross_output_bias, grad_second_gain, grad_second_shift,
        ]),
        feed_sums[:3],
        grad_expand_bias.reshape(4, width),
    ])
    vector_rows = vector_grads.reshape(5, 3, 8, 128).transpose(2, 0, 1, 3).reshape(8, 5, 384).astype(bf16)
    heads_grad = after(heads_grad, (early, late_keep, late_send, memory_far, vector_rows))
    memory_got = to_y(memory_far)
    early_got = to_x(part_of(early, x ^ 1, 1))
    first_heads = jnp.concatenate(heads_back(0, heads_grad), axis=1)
    first_heads, early_got, late_got = lax.optimization_barrier((first_heads, early_got, late_got))
    first_blocks = own_blocks(first_heads)
    late = added(late_keep, late_got).reshape(4, 2, 128, 5 * share)
    late_got = to_x(part_of(late, x ^ 1, 1))
    early = added(part_of(early, x, 1), early_got)
    early_sends = [part_of(early, z ^ k, 0) for k in (1, 2, 3)]
    first_total = from_fsdp(first_blocks)
    second_heads = jnp.concatenate(heads_back(1, after(heads_grad, (first_blocks, late, early_sends))), axis=1)
    early_pieces = [to_z(piece, k) for piece, k in zip(early_sends, (1, 2, 3))]
    second_heads, early_pieces, late_got, memory_got, feed_share = lax.optimization_barrier(
        (second_heads, early_pieces, late_got, memory_got, feed_share)
    )
    second_blocks = own_blocks(second_heads)
    ready_first, ready_second = after((first_heads, second_heads), second_blocks)
    token_terms = (
        dot(ready_first, jnp.concatenate([projection[:, i * share:i * share + 128] for i in range(3)], axis=1).T)
        + dot(ready_second, jnp.concatenate([projection[:, i * share + 128:(i + 1) * share] for i in range(3)], axis=1).T)
    ).astype(bf16)
    token_near, token_far = chip_sums(token_terms, rows)
    feed_near = feed_share
    feed_far = to_y(feed_share)
    token_got = to_y(after(token_far, feed_far))
    token_grad = (residual_scale * grad_first + token_near + token_got.astype(f32))[None]
    memory_grad = (memory_near + memory_got.astype(f32))[None]

    both_heads = [first_heads.astype(f32), second_heads.astype(f32)]
    head_sums = jnp.stack([
        jnp.concatenate([jnp.sum(half[:, at:at + 128], axis=0) for half in both_heads]) for at in (0, 256)
    ])
    head_sums = lax.dynamic_update_slice(jnp.zeros((2, width), f32), head_sums, (0, me_c * share))
    head_rows = jnp.concatenate([head_sums, jnp.zeros((1, width), f32)])
    head_rows = head_rows.reshape(3, 8, 128).transpose(1, 0, 2).reshape(8, 1, 384).astype(bf16)
    blocks = jnp.concatenate([second_blocks, vector_rows, head_rows, jnp.zeros((8, 10, 384), bf16)], axis=1)
    second_total = from_fsdp(blocks)
    padded = jnp.concatenate([first_total, jnp.zeros((16, 384), f32)])
    total = after(jnp.concatenate([padded, second_total], axis=1).astype(bf16), token_got)

    early = part_of(early, z, 0).astype(f32)
    for piece in early_pieces:
        early = early + piece.astype(f32)
    early = early.astype(bf16)
    late = over_z(added(after(part_of(late, x, 1), (blocks, token_far)), late_got)[None], z)[0]
    early_got = to_y(early)
    early = jnp.concatenate([jnp.where(line == 0, early, early_got), jnp.where(line == 0, early_got, early)])
    late = added(late, to_y(late))
    grad_cross_memory, grad_cross_query, grad_cross_output, grad_self_output = spread(
        spread_middle_body, core, [early, to_core(early), late, to_core(late)],
        [(128, 2 * width), (128, width), (128, width), (128, width)],
    )

    grad_self_projection, sums = spread(
        spread_projection_body, me_c, ctx_pieces(total), [(128, 3 * width), (18, 128)]
    )

    feed_own = added(feed_near, feed_far).reshape(2, 256, width)
    grad_expand, grad_reduce = spread(spread_feed_body, core, [feed_own, to_core(feed_own)], [(128, 4 * width), (512, width)])

    return (
        output[None],
        token_grad,
        memory_grad,
        grad_self_projection,
        grad_self_output,
        sums[15],
        sums[16],
        sums[0],
        sums[1],
        sums[2],
        grad_cross_query,
        grad_cross_memory,
        grad_cross_output,
        sums[3],
        sums[4],
        sums[5],
        sums[6],
        sums[7],
        grad_expand,
        grad_reduce,
        sums[11:15].reshape(512),
        sums[8],
        sums[9],
        sums[10],
    )


def head_split(matrix):
    return matrix.reshape(matrix.shape[0], HEADS, HEAD_DIM)


def piece_size(length):
    return min(512, length)


def piece_masks(key_blocks, allowed_rows):
    length = key_blocks.shape[0]
    piece = piece_size(length)
    count = length // piece
    if allowed_rows is None:
        return jnp.ones((count, 1, 1), jnp.bool_)
    nblocks = allowed_rows.shape[1]
    onehot = (key_blocks[:, None] == jnp.arange(nblocks, dtype=jnp.int32)[None, :]).astype(
        jnp.float32
    )
    live = jnp.dot(allowed_rows, onehot.T) > 0.5
    return jnp.moveaxis(live.reshape(live.shape[0], count, piece), 1, 0)


def masked_scores(query_heads, key_piece, live):
    scores = (
        jnp.einsum("qhd,khd->hqk", query_heads, key_piece, preferred_element_type=jnp.float32)
        * score_scale
    )
    return jnp.where(live[None], scores, masked_score)


def run_guarded(guarded, live, work, fallback):
    if guarded:
        return lax.cond(jnp.any(live), work, lambda unused: fallback, live)
    return work(live)


def attend_forward(query_heads, key_heads, value_heads, live_pieces, guarded):
    count = live_pieces.shape[0]
    piece = key_heads.shape[0] // count
    key_pieces = key_heads.reshape((count, piece) + key_heads.shape[1:])
    value_pieces = value_heads.reshape((count, piece) + value_heads.shape[1:])
    rows = query_heads.shape[0]

    def first_step(carry, inputs):
        run_max, run_sum = carry
        key_piece, live = inputs

        def work(live_now):
            scores = masked_scores(query_heads, key_piece, live_now)
            new_max = jnp.maximum(run_max, jnp.max(scores, axis=-1))
            shifted = jnp.where(live_now[None], jnp.exp(scores - new_max[:, :, None]), 0.0)
            return (new_max, run_sum * jnp.exp(run_max - new_max) + jnp.sum(shifted, axis=-1))

        return (run_guarded(guarded, live, work, (run_max, run_sum)), None)

    start = (
        jnp.full((HEADS, rows), masked_score, jnp.float32),
        jnp.zeros((HEADS, rows), jnp.float32),
    )
    (final_max, final_sum), unused = lax.scan(first_step, start, (key_pieces, live_pieces))
    log_total = final_max + jnp.log(final_sum)

    def second_step(total, inputs):
        key_piece, value_piece, live = inputs

        def work(live_now):
            scores = masked_scores(query_heads, key_piece, live_now)
            probs = jnp.exp(scores - log_total[:, :, None]).astype(jnp.bfloat16)
            return total + jnp.einsum(
                "hqk,khd->qhd", probs, value_piece, preferred_element_type=jnp.float32
            )

        return (run_guarded(guarded, live, work, total), None)

    empty = jnp.zeros((rows, HEADS, HEAD_DIM), jnp.float32)
    attended, unused = lax.scan(second_step, empty, (key_pieces, value_pieces, live_pieces))
    return (attended, log_total)


def attend_backward(
    query_heads, key_heads, value_heads, log_total, grad_heads, delta, live_pieces, guarded
):
    count = live_pieces.shape[0]
    piece = key_heads.shape[0] // count
    key_pieces = key_heads.reshape((count, piece) + key_heads.shape[1:])
    value_pieces = value_heads.reshape((count, piece) + value_heads.shape[1:])
    rows = query_heads.shape[0]
    blank = jnp.zeros((piece, HEADS, HEAD_DIM), jnp.float32)

    def back_step(grad_query, inputs):
        key_piece, value_piece, live = inputs

        def work(live_now):
            scores = masked_scores(query_heads, key_piece, live_now)
            probs = jnp.exp(scores - log_total[:, :, None])
            grad_probs = jnp.einsum(
                "qhd,khd->hqk", grad_heads, value_piece, preferred_element_type=jnp.float32
            )
            grad_scores = (probs * (grad_probs - delta[:, :, None])).astype(jnp.bfloat16)
            new_query = (
                grad_query
                + jnp.einsum(
                    "hqk,khd->qhd", grad_scores, key_piece, preferred_element_type=jnp.float32
                )
                * score_scale
            )
            grad_key = (
                jnp.einsum(
                    "hqk,qhd->khd", grad_scores, query_heads, preferred_element_type=jnp.float32
                )
                * score_scale
            )
            grad_value = jnp.einsum(
                "hqk,qhd->khd",
                probs.astype(jnp.bfloat16),
                grad_heads,
                preferred_element_type=jnp.float32,
            )
            return (new_query, (grad_key, grad_value))

        return run_guarded(guarded, live, work, (grad_query, (blank, blank)))

    empty = jnp.zeros((rows, HEADS, HEAD_DIM), jnp.float32)
    grad_query, (key_grads, value_grads) = lax.scan(
        back_step, empty, (key_pieces, value_pieces, live_pieces)
    )
    width = HEADS * HEAD_DIM
    return (
        grad_query.reshape(rows, width),
        key_grads.reshape(-1, width),
        value_grads.reshape(-1, width),
    )


def plain_shards(
    tokens,
    memory,
    cotangent,
    block_map,
    block_order,
    self_projection,
    self_output,
    self_query_bias,
    self_value_bias,
    self_output_bias,
    first_gain,
    first_shift,
    cross_query,
    cross_memory,
    cross_output,
    cross_query_bias,
    cross_value_bias,
    cross_output_bias,
    second_gain,
    second_shift,
    expand_weight,
    reduce_weight,
    expand_bias,
    reduce_bias,
    third_gain,
    third_shift,
):
    bf16 = jnp.bfloat16
    f32 = jnp.float32
    rows_in = tokens[0]
    rows = rows_in.shape[0]
    width = rows_in.shape[1]
    ctx_count = lax.axis_size("ctx")
    slot = lax.axis_index("ctx")
    positions = jnp.arange(rows * ctx_count, dtype=jnp.int32)
    group_index = positions // rows
    group_match = group_index[:, None] == jnp.arange(ctx_count, dtype=jnp.int32)[None, :]
    group_place = jnp.sum(jnp.where(group_match, block_order[0][None, :], 0), axis=1)
    key_blocks = (group_place * rows + positions % rows) // BLK
    own_blocks = lax.dynamic_slice_in_dim(key_blocks, slot * rows, rows)
    nblocks = block_map.shape[1]
    own_onehot = (own_blocks[:, None] == jnp.arange(nblocks, dtype=jnp.int32)[None, :]).astype(f32)
    allowed_rows = jnp.dot(own_onehot, block_map[0].astype(f32))
    self_live = piece_masks(key_blocks, allowed_rows)
    (
        projection_full,
        self_out_full,
        query_bias_full,
        value_bias_full,
        out_bias_full,
        gain_one,
        shift_one,
    ) = (
        lax.all_gather(self_projection, "fsdp", axis=0, tiled=True),
        lax.all_gather(self_output, "fsdp", axis=0, tiled=True),
        lax.all_gather(self_query_bias, "fsdp", axis=0, tiled=True),
        lax.all_gather(self_value_bias, "fsdp", axis=0, tiled=True),
        lax.all_gather(self_output_bias, "fsdp", axis=0, tiled=True),
        lax.all_gather(first_gain, "fsdp", axis=0, tiled=True),
        lax.all_gather(first_shift, "fsdp", axis=0, tiled=True),
    )
    projected = jnp.dot(rows_in, projection_full, preferred_element_type=f32)
    queries = (projected[:, :width] + query_bias_full).astype(bf16)
    keys_own = projected[:, width : 2 * width].astype(bf16)
    values_own = (projected[:, 2 * width :] + value_bias_full).astype(bf16)
    keys_all, values_all = (
        lax.all_gather(keys_own, "ctx", axis=0, tiled=True),
        lax.all_gather(values_own, "ctx", axis=0, tiled=True),
    )
    query_heads = head_split(queries)
    key_heads = head_split(keys_all)
    value_heads = head_split(values_all)
    attended, self_total = attend_forward(query_heads, key_heads, value_heads, self_live, True)
    attended_low = attended.reshape(rows, width).astype(bf16)
    branch = jnp.dot(attended_low, self_out_full, preferred_element_type=f32) + out_bias_full
    hidden_one, normed_one, inverse_one = layer_norm(
        residual_scale * rows_in.astype(f32) + branch, gain_one, shift_one
    )
    (
        cross_query_full,
        cross_memory_full,
        cross_out_full,
        cross_qbias_full,
        cross_vbias_full,
        cross_obias_full,
        gain_two,
        shift_two,
    ) = (
        lax.all_gather(cross_query, "fsdp", axis=0, tiled=True),
        lax.all_gather(cross_memory, "fsdp", axis=0, tiled=True),
        lax.all_gather(cross_output, "fsdp", axis=0, tiled=True),
        lax.all_gather(cross_query_bias, "fsdp", axis=0, tiled=True),
        lax.all_gather(cross_value_bias, "fsdp", axis=0, tiled=True),
        lax.all_gather(cross_output_bias, "fsdp", axis=0, tiled=True),
        lax.all_gather(second_gain, "fsdp", axis=0, tiled=True),
        lax.all_gather(second_shift, "fsdp", axis=0, tiled=True),
    )
    hidden_low = hidden_one.astype(bf16)
    cross_queries = (
        jnp.dot(hidden_low, cross_query_full, preferred_element_type=f32) + cross_qbias_full
    ).astype(bf16)
    memory_rows = memory[0]
    memory_proj = jnp.dot(memory_rows, cross_memory_full, preferred_element_type=f32)
    memory_keys = memory_proj[:, :width].astype(bf16)
    memory_values = (memory_proj[:, width:] + cross_vbias_full).astype(bf16)
    memory_keys_all, memory_values_all = (
        lax.all_gather(memory_keys, "ctx", axis=0, tiled=True),
        lax.all_gather(memory_values, "ctx", axis=0, tiled=True),
    )
    cross_heads = head_split(cross_queries)
    memory_key_heads = head_split(memory_keys_all)
    memory_value_heads = head_split(memory_values_all)
    cross_live = piece_masks(jnp.zeros((memory_keys_all.shape[0],), jnp.int32), None)
    cross_attended, cross_total = attend_forward(
        cross_heads, memory_key_heads, memory_value_heads, cross_live, False
    )
    cross_low = cross_attended.reshape(rows, width).astype(bf16)
    cross_branch = jnp.dot(cross_low, cross_out_full, preferred_element_type=f32) + cross_obias_full
    hidden_two, normed_two, inverse_two = layer_norm(
        residual_scale * hidden_one + cross_branch, gain_two, shift_two
    )
    expand_full, reduce_full, expand_bias_full, reduce_bias_full, gain_three, shift_three = (
        lax.all_gather(expand_weight, "fsdp", axis=0, tiled=True),
        lax.all_gather(reduce_weight, "fsdp", axis=0, tiled=True),
        lax.all_gather(expand_bias, "fsdp", axis=0, tiled=True),
        lax.all_gather(reduce_bias, "fsdp", axis=0, tiled=True),
        lax.all_gather(third_gain, "fsdp", axis=0, tiled=True),
        lax.all_gather(third_shift, "fsdp", axis=0, tiled=True),
    )
    hidden_two_low = hidden_two.astype(bf16)
    expanded = jnp.dot(hidden_two_low, expand_full, preferred_element_type=f32) + expand_bias_full
    activated = gelu_tanh(expanded).astype(bf16)
    reduced = jnp.dot(activated, reduce_full, preferred_element_type=f32) + reduce_bias_full
    result, normed_three, inverse_three = layer_norm(
        residual_scale * hidden_two + reduced, gain_three, shift_three
    )
    output = result.astype(bf16)[None]
    upstream = cotangent[0].astype(f32)
    grad_third, grad_third_gain, grad_third_shift = layer_norm_back(
        upstream, gain_three, normed_three, inverse_three
    )
    grad_reduced = grad_third.astype(bf16)
    grad_reduce_bias = jnp.sum(grad_reduced.astype(f32), axis=0)
    grad_reduce_weight = jnp.dot(activated.T, grad_reduced, preferred_element_type=f32)
    grad_activated = jnp.dot(grad_reduced, reduce_full.T, preferred_element_type=f32)
    grad_expanded = (grad_activated * gelu_slope(expanded)).astype(bf16)
    grad_expand_bias = jnp.sum(grad_expanded.astype(f32), axis=0)
    grad_expand_weight = jnp.dot(hidden_two_low.T, grad_expanded, preferred_element_type=f32)
    grad_hidden_two = residual_scale * grad_third + jnp.dot(
        grad_expanded, expand_full.T, preferred_element_type=f32
    )
    grad_second, grad_second_gain, grad_second_shift = layer_norm_back(
        grad_hidden_two, gain_two, normed_two, inverse_two
    )
    grad_cross_branch = grad_second.astype(bf16)
    grad_cross_output_bias = jnp.sum(grad_cross_branch.astype(f32), axis=0)
    grad_cross_output = jnp.dot(cross_low.T, grad_cross_branch, preferred_element_type=f32)
    grad_cross_low = jnp.dot(
        grad_cross_branch, cross_out_full.T, preferred_element_type=f32
    ).astype(bf16)
    grad_cross_heads = head_split(grad_cross_low)
    cross_delta = jnp.sum(grad_cross_heads.astype(f32) * cross_attended, axis=-1).T
    grad_cross_queries, memory_key_terms, memory_value_terms = attend_backward(
        cross_heads,
        memory_key_heads,
        memory_value_heads,
        cross_total,
        grad_cross_heads,
        cross_delta,
        cross_live,
        False,
    )
    grad_memory_keys, grad_memory_values = (
        lax.psum_scatter(
            memory_key_terms.astype(jnp.bfloat16), "ctx", scatter_dimension=0, tiled=True
        ).astype(jnp.float32),
        lax.psum_scatter(
            memory_value_terms.astype(jnp.bfloat16), "ctx", scatter_dimension=0, tiled=True
        ).astype(jnp.float32),
    )
    grad_memory_pair = jnp.concatenate(
        [grad_memory_keys.astype(bf16), grad_memory_values.astype(bf16)], axis=1
    )
    grad_cross_value_bias = jnp.sum(grad_memory_pair[:, width:].astype(f32), axis=0)
    grad_cross_memory = jnp.dot(memory_rows.T, grad_memory_pair, preferred_element_type=f32)
    memory_grad = jnp.dot(grad_memory_pair, cross_memory_full.T, preferred_element_type=f32)[None]
    grad_cross_low_queries = grad_cross_queries.astype(bf16)
    grad_cross_query_bias = jnp.sum(grad_cross_low_queries.astype(f32), axis=0)
    grad_cross_query = jnp.dot(hidden_low.T, grad_cross_low_queries, preferred_element_type=f32)
    grad_hidden_one = residual_scale * grad_second + jnp.dot(
        grad_cross_low_queries, cross_query_full.T, preferred_element_type=f32
    )
    grad_first, grad_first_gain, grad_first_shift = layer_norm_back(
        grad_hidden_one, gain_one, normed_one, inverse_one
    )
    grad_branch = grad_first.astype(bf16)
    grad_self_output_bias = jnp.sum(grad_branch.astype(f32), axis=0)
    grad_self_output = jnp.dot(attended_low.T, grad_branch, preferred_element_type=f32)
    grad_attended = jnp.dot(grad_branch, self_out_full.T, preferred_element_type=f32).astype(bf16)
    grad_attended_heads = head_split(grad_attended)
    self_delta = jnp.sum(grad_attended_heads.astype(f32) * attended, axis=-1).T
    grad_queries, key_terms, value_terms = attend_backward(
        query_heads,
        key_heads,
        value_heads,
        self_total,
        grad_attended_heads,
        self_delta,
        self_live,
        True,
    )
    grad_keys, grad_values = (
        lax.psum_scatter(
            key_terms.astype(jnp.bfloat16), "ctx", scatter_dimension=0, tiled=True
        ).astype(jnp.float32),
        lax.psum_scatter(
            value_terms.astype(jnp.bfloat16), "ctx", scatter_dimension=0, tiled=True
        ).astype(jnp.float32),
    )
    grad_projected = jnp.concatenate(
        [grad_queries.astype(bf16), grad_keys.astype(bf16), grad_values.astype(bf16)], axis=1
    )
    grad_self_query_bias = jnp.sum(grad_projected[:, :width].astype(f32), axis=0)
    grad_self_value_bias = jnp.sum(grad_projected[:, 2 * width :].astype(f32), axis=0)
    grad_self_projection = jnp.dot(rows_in.T, grad_projected, preferred_element_type=f32)
    token_grad = (
        residual_scale * grad_first
        + jnp.dot(grad_projected, projection_full.T, preferred_element_type=f32)
    )[None]
    shares = (
        lax.psum_scatter(
            grad_self_projection.astype(jnp.bfloat16), "fsdp", scatter_dimension=0, tiled=True
        ).astype(jnp.float32),
        lax.psum_scatter(
            grad_self_output.astype(jnp.bfloat16), "fsdp", scatter_dimension=0, tiled=True
        ).astype(jnp.float32),
        lax.psum_scatter(
            grad_self_query_bias.astype(jnp.bfloat16), "fsdp", scatter_dimension=0, tiled=True
        ).astype(jnp.float32),
        lax.psum_scatter(
            grad_self_value_bias.astype(jnp.bfloat16), "fsdp", scatter_dimension=0, tiled=True
        ).astype(jnp.float32),
        lax.psum_scatter(
            grad_self_output_bias.astype(jnp.bfloat16), "fsdp", scatter_dimension=0, tiled=True
        ).astype(jnp.float32),
        lax.psum_scatter(
            grad_first_gain.astype(jnp.bfloat16), "fsdp", scatter_dimension=0, tiled=True
        ).astype(jnp.float32),
        lax.psum_scatter(
            grad_first_shift.astype(jnp.bfloat16), "fsdp", scatter_dimension=0, tiled=True
        ).astype(jnp.float32),
        lax.psum_scatter(
            grad_cross_query.astype(jnp.bfloat16), "fsdp", scatter_dimension=0, tiled=True
        ).astype(jnp.float32),
        lax.psum_scatter(
            grad_cross_memory.astype(jnp.bfloat16), "fsdp", scatter_dimension=0, tiled=True
        ).astype(jnp.float32),
        lax.psum_scatter(
            grad_cross_output.astype(jnp.bfloat16), "fsdp", scatter_dimension=0, tiled=True
        ).astype(jnp.float32),
        lax.psum_scatter(
            grad_cross_query_bias.astype(jnp.bfloat16), "fsdp", scatter_dimension=0, tiled=True
        ).astype(jnp.float32),
        lax.psum_scatter(
            grad_cross_value_bias.astype(jnp.bfloat16), "fsdp", scatter_dimension=0, tiled=True
        ).astype(jnp.float32),
        lax.psum_scatter(
            grad_cross_output_bias.astype(jnp.bfloat16), "fsdp", scatter_dimension=0, tiled=True
        ).astype(jnp.float32),
        lax.psum_scatter(
            grad_second_gain.astype(jnp.bfloat16), "fsdp", scatter_dimension=0, tiled=True
        ).astype(jnp.float32),
        lax.psum_scatter(
            grad_second_shift.astype(jnp.bfloat16), "fsdp", scatter_dimension=0, tiled=True
        ).astype(jnp.float32),
        lax.psum_scatter(
            grad_expand_weight.astype(jnp.bfloat16), "fsdp", scatter_dimension=0, tiled=True
        ).astype(jnp.float32),
        lax.psum_scatter(
            grad_reduce_weight.astype(jnp.bfloat16), "fsdp", scatter_dimension=0, tiled=True
        ).astype(jnp.float32),
        lax.psum_scatter(
            grad_expand_bias.astype(jnp.bfloat16), "fsdp", scatter_dimension=0, tiled=True
        ).astype(jnp.float32),
        lax.psum_scatter(
            grad_reduce_bias.astype(jnp.bfloat16), "fsdp", scatter_dimension=0, tiled=True
        ).astype(jnp.float32),
        lax.psum_scatter(
            grad_third_gain.astype(jnp.bfloat16), "fsdp", scatter_dimension=0, tiled=True
        ).astype(jnp.float32),
        lax.psum_scatter(
            grad_third_shift.astype(jnp.bfloat16), "fsdp", scatter_dimension=0, tiled=True
        ).astype(jnp.float32),
    )
    summed = (
        lax.psum(shares[0].astype(jnp.bfloat16), "ctx").astype(jnp.float32),
        lax.psum(shares[1].astype(jnp.bfloat16), "ctx").astype(jnp.float32),
        lax.psum(shares[2].astype(jnp.bfloat16), "ctx").astype(jnp.float32),
        lax.psum(shares[3].astype(jnp.bfloat16), "ctx").astype(jnp.float32),
        lax.psum(shares[4].astype(jnp.bfloat16), "ctx").astype(jnp.float32),
        lax.psum(shares[5].astype(jnp.bfloat16), "ctx").astype(jnp.float32),
        lax.psum(shares[6].astype(jnp.bfloat16), "ctx").astype(jnp.float32),
        lax.psum(shares[7].astype(jnp.bfloat16), "ctx").astype(jnp.float32),
        lax.psum(shares[8].astype(jnp.bfloat16), "ctx").astype(jnp.float32),
        lax.psum(shares[9].astype(jnp.bfloat16), "ctx").astype(jnp.float32),
        lax.psum(shares[10].astype(jnp.bfloat16), "ctx").astype(jnp.float32),
        lax.psum(shares[11].astype(jnp.bfloat16), "ctx").astype(jnp.float32),
        lax.psum(shares[12].astype(jnp.bfloat16), "ctx").astype(jnp.float32),
        lax.psum(shares[13].astype(jnp.bfloat16), "ctx").astype(jnp.float32),
        lax.psum(shares[14].astype(jnp.bfloat16), "ctx").astype(jnp.float32),
        lax.psum(shares[15].astype(jnp.bfloat16), "ctx").astype(jnp.float32),
        lax.psum(shares[16].astype(jnp.bfloat16), "ctx").astype(jnp.float32),
        lax.psum(shares[17].astype(jnp.bfloat16), "ctx").astype(jnp.float32),
        lax.psum(shares[18].astype(jnp.bfloat16), "ctx").astype(jnp.float32),
        lax.psum(shares[19].astype(jnp.bfloat16), "ctx").astype(jnp.float32),
        lax.psum(shares[20].astype(jnp.bfloat16), "ctx").astype(jnp.float32),
    )
    return (
        output,
        token_grad,
        memory_grad,
        summed[0],
        summed[1],
        summed[2],
        summed[3],
        summed[4],
        summed[5],
        summed[6],
        summed[7],
        summed[8],
        summed[9],
        summed[10],
        summed[11],
        summed[12],
        summed[13],
        summed[14],
        summed[15],
        summed[16],
        summed[17],
        summed[18],
        summed[19],
        summed[20],
    )


def solution(mesh):
    placed = (
        P("fsdp", "ctx", None),
        P("fsdp", "ctx", None),
        P("fsdp", "ctx", None),
        P("fsdp", None, None),
        P("fsdp", None),
        P("fsdp", None),
        P("fsdp", None),
        P("fsdp"),
        P("fsdp"),
        P("fsdp"),
        P("fsdp"),
        P("fsdp"),
        P("fsdp", None),
        P("fsdp", None),
        P("fsdp", None),
        P("fsdp"),
        P("fsdp"),
        P("fsdp"),
        P("fsdp"),
        P("fsdp"),
        P("fsdp", None),
        P("fsdp", None),
        P("fsdp"),
        P("fsdp"),
        P("fsdp"),
        P("fsdp"),
    )
    sizes = (mesh.shape["ctx"], mesh.shape["fsdp"])
    return jax.shard_map(
        tiled_shards if sizes == (4, 8) else plain_shards,
        mesh=mesh,
        in_specs=placed,
        out_specs=(
            P("fsdp", "ctx", None),
            P("fsdp", "ctx", None),
            P("fsdp", "ctx", None),
            P("fsdp", None),
            P("fsdp", None),
            P("fsdp"),
            P("fsdp"),
            P("fsdp"),
            P("fsdp"),
            P("fsdp"),
            P("fsdp", None),
            P("fsdp", None),
            P("fsdp", None),
            P("fsdp"),
            P("fsdp"),
            P("fsdp"),
            P("fsdp"),
            P("fsdp"),
            P("fsdp", None),
            P("fsdp", None),
            P("fsdp"),
            P("fsdp"),
            P("fsdp"),
            P("fsdp"),
        ),
        check_vma=False,
    )
```

```python
import functools
import math

import jax
import jax.numpy as jnp
from jax import lax
from jax.experimental import pallas as pl
from jax.experimental.layout import Layout, with_layout_constraint
from jax.experimental.pallas import tpu as pltpu
from jax.sharding import PartitionSpec as P

HEADS = 16
HEAD_DIM = 64
BLK = 256


epsilon = 1e-05
residual_scale = 18.0**0.25
score_scale = 0.125
masked_score = -1e30
gelu_coeff = math.sqrt(2.0 / math.pi)


def gelu_tanh(value):
    return 0.5 * value * (1.0 + jnp.tanh(gelu_coeff * (value + 0.044715 * value * value * value)))


def gelu_slope(value):
    inner = jnp.tanh(gelu_coeff * (value + 0.044715 * value * value * value))
    return 0.5 * (1.0 + inner) + 0.5 * value * (1.0 - inner * inner) * gelu_coeff * (
        1.0 + 3.0 * 0.044715 * value * value
    )


def layer_norm(summed, gain, shift):
    centred = summed - jnp.mean(summed, axis=-1, keepdims=True)
    inverse = lax.rsqrt(jnp.mean(centred * centred, axis=-1, keepdims=True) + epsilon)
    normed = centred * inverse
    return (normed * gain + shift, normed, inverse)


def layer_norm_back(upstream, gain, normed, inverse):
    scaled = upstream * gain
    inner = (
        scaled
        - jnp.mean(scaled, axis=-1, keepdims=True)
        - normed * jnp.mean(scaled * normed, axis=-1, keepdims=True)
    )
    return (inner * inverse, jnp.sum(upstream * normed, axis=0), jnp.sum(upstream, axis=0))


score_log2 = 0.125 * math.log2(math.e)
NT = (((1,), (1,)), ((), ()))
NN = (((1,), (0,)), ((), ()))
TN = (((0,), (0,)), ((), ()))


def mxu(left, right, dims):
    return lax.dot_general(left, right, dims, preferred_element_type=jnp.float32)


def two_heads(pair):
    low = lax.broadcasted_iota(jnp.int32, pair.shape, 1) < 64
    zero = jnp.zeros_like(pair)
    return jnp.concatenate([jnp.where(low, pair, zero), jnp.where(low, zero, pair)], axis=0)


def one_pair(stacked):
    rows = stacked.shape[0] // 2
    top = stacked[:rows]
    low = lax.broadcasted_iota(jnp.int32, top.shape, 1) < 64
    return jnp.where(low, top, stacked[rows:])


def place_of(order_ref, slot_ref, index, per_group):
    return order_ref[slot_ref[0] ^ (index // per_group)] * per_group + index % per_group


def seen(scalars, query_index, key_index, per_group, count):
    if scalars is None:
        return None
    order_ref, map_ref, slot_ref = scalars
    row = place_of(order_ref, slot_ref, query_index, per_group)
    column = place_of(order_ref, slot_ref, key_index, per_group)
    return map_ref[row * count + column] > 0


def guarded(flag, work):
    if flag is None:
        work()
    else:
        pl.when(flag)(work)


def pair_lanes(unit):
    return slice(unit * 128, (unit + 1) * 128)


def forward_body(masked, units, chunks, key_rows, pieces, per_group, *refs):
    scalars = None
    if masked:
        scalars, refs = refs[:3], refs[3:]
    q_ref, refs = refs[0], refs[1:]
    k_refs, v_refs, refs = refs[:pieces], refs[pieces:2 * pieces], refs[2 * pieces:]
    o_ref, lse_ref, stacked, scores, top, shift, total, acc = refs
    rows = stacked.shape[1]
    query_index = pl.program_id(1)

    def part(ref_list, chunk, unit):
        if pieces > 1:
            return ref_list[chunk][:, pair_lanes(unit)]
        return ref_list[0][chunk * key_rows:(chunk + 1) * key_rows, pair_lanes(unit)]

    for unit in range(units):
        stacked[unit] = two_heads(q_ref[:, pair_lanes(unit)])
        top[unit] = jnp.full((rows, 128), -1e30, jnp.float32)
        total[unit] = jnp.zeros((rows, 128), jnp.float32)
        acc[unit] = jnp.zeros((rows, 128), jnp.float32)
    for chunk in range(chunks):
        flag = seen(scalars, query_index, chunk, per_group, chunks)

        def scan_max(chunk=chunk):
            for unit in range(units):
                found = mxu(stacked[unit], part(k_refs, chunk, unit), NT)
                scores[unit, chunk] = found
                best = top[unit]
                for lane in range(0, key_rows, 128):
                    best = jnp.maximum(best, found[:, lane:lane + 128])
                top[unit] = best

        guarded(flag, scan_max)
    for unit in range(units):
        peak = jnp.max(top[unit], axis=1, keepdims=True) * score_log2
        shift[unit] = jnp.broadcast_to(peak, (rows, 128))
    for chunk in range(chunks):
        flag = seen(scalars, query_index, chunk, per_group, chunks)

        def weigh(chunk=chunk):
            for unit in range(units):
                found = scores[unit, chunk]
                offset = shift[unit]
                summed = total[unit]
                parts = []
                for lane in range(0, key_rows, 128):
                    weight = jnp.exp2(found[:, lane:lane + 128] * score_log2 - offset)
                    summed = summed + weight
                    parts.append(weight.astype(jnp.bfloat16))
                total[unit] = summed
                acc[unit] = acc[unit] + mxu(jnp.concatenate(parts, axis=1), part(v_refs, chunk, unit), NN)

        guarded(flag, weigh)
    for unit in range(units):
        row_sum = jnp.sum(total[unit], axis=1, keepdims=True)
        o_ref[:, pair_lanes(unit)] = one_pair(acc[unit] / row_sum).astype(o_ref.dtype)
        lse = shift[unit] + jnp.log2(row_sum)
        lse_ref[unit] = lse.T[:8]


def backward_body(masked, units, chunks, key_rows, pieces, per_group, *refs):
    scalars = None
    if masked:
        scalars, refs = refs[:3], refs[3:]
    q_ref, do_ref, o_ref, lse_ref, refs = refs[0], refs[1], refs[2], refs[3], refs[4:]
    k_refs, v_refs, refs = refs[:pieces], refs[pieces:2 * pieces], refs[2 * pieces:]
    dq_ref, dk_refs, dv_refs, refs = refs[0], refs[1:1 + pieces], refs[1 + pieces:1 + 2 * pieces], refs[1 + 2 * pieces:]
    stacked, grads, delta, dq_acc, dk_acc, dv_acc = refs
    query_index = pl.program_id(1)

    @pl.when(query_index == 0)
    def clear():
        dk_acc[...] = jnp.zeros_like(dk_acc)
        dv_acc[...] = jnp.zeros_like(dv_acc)

    for unit in range(units):
        lanes = pair_lanes(unit)
        stacked[unit] = two_heads(q_ref[:, lanes])
        upstream = do_ref[:, lanes]
        grads[unit] = two_heads(upstream)
        product = (upstream.astype(jnp.float32) * o_ref[:, lanes].astype(jnp.float32)).T
        first = jnp.sum(product[:64], axis=0, keepdims=True)
        second = jnp.sum(product[64:], axis=0, keepdims=True)
        delta[unit] = jnp.broadcast_to(jnp.concatenate([first, second], axis=1), delta.shape[1:])
        dq_acc[unit] = jnp.zeros(dq_acc.shape[1:], jnp.float32)
    def step(first, count):
        rows = slice(first * key_rows, (first + count) * key_rows)
        for unit in range(units):
            queries, upstream = stacked[unit], grads[unit]
            keys, values = k_refs[0][rows, pair_lanes(unit)], v_refs[0][rows, pair_lanes(unit)]
            found = mxu(keys, queries, NT)
            probs = jnp.exp2(found * score_log2 - lse_ref[unit, 0:1])
            grad_probs = mxu(values, upstream, NT)
            grad_scores = (probs * (grad_probs - delta[unit, 0:1])).astype(jnp.bfloat16)
            dv_acc[unit, rows] += mxu(probs.astype(jnp.bfloat16), upstream, NN)
            dk_acc[unit, rows] += mxu(grad_scores, queries, NN)
            dq_acc[unit] += mxu(grad_scores, keys, TN)

    if masked:
        for chunk in range(0, chunks, 2):
            first = seen(scalars, query_index, chunk, per_group, chunks)
            second = seen(scalars, query_index, chunk + 1, per_group, chunks)
            pl.when(first & second)(functools.partial(step, chunk, 2))
            pl.when(first & jnp.logical_not(second))(functools.partial(step, chunk, 1))
            pl.when(second & jnp.logical_not(first))(functools.partial(step, chunk + 1, 1))
    else:
        for chunk in range(chunks):
            step(chunk, 1)
    for unit in range(units):
        dq_ref[:, pair_lanes(unit)] = (one_pair(dq_acc[unit]) * 0.125).astype(dq_ref.dtype)

    @pl.when(query_index == pl.num_programs(1) - 1)
    def finish():
        for unit in range(units):
            dk_refs[0][:, pair_lanes(unit)] = (dk_acc[unit] * 0.125).astype(jnp.bfloat16)
            dv_refs[0][:, pair_lanes(unit)] = dv_acc[unit].astype(jnp.bfloat16)


def attention_forward(q, q_col, k_list, k_col, v_list, v_col, width, scalars, key_rows, units=2, per_group=2):
    pieces = len(k_list)
    lanes = units * 128
    rows = q.shape[0]
    keys = sum(k.shape[0] for k in k_list)
    chunks = keys // key_rows
    groups, blocks = width // lanes, rows // BLK
    masked = scalars is not None
    spec_q = pl.BlockSpec((BLK, lanes), lambda h, i, *_: (i, q_col + h))
    specs_k = [pl.BlockSpec((k.shape[0], lanes), lambda h, i, *_: (0, k_col + h)) for k in k_list]
    specs_v = [pl.BlockSpec((v.shape[0], lanes), lambda h, i, *_: (0, v_col + h)) for v in v_list]
    body = functools.partial(forward_body, masked, units, chunks, key_rows, pieces, per_group)
    pairs = rows * keys * (width // 64)
    return pl.pallas_call(
        body,
        grid_spec=pltpu.PrefetchScalarGridSpec(
            num_scalar_prefetch=3 if masked else 0,
            grid=(groups, blocks),
            in_specs=[spec_q] + specs_k + specs_v,
            out_specs=[
                pl.BlockSpec((BLK, lanes), lambda h, i, *_: (i, h)),
                pl.BlockSpec((units, 8, 2 * BLK), lambda h, i, *_: (h, 0, i)),
            ],
            scratch_shapes=[
                pltpu.VMEM((units, 2 * BLK, 128), jnp.bfloat16),
                pltpu.VMEM((units, chunks, 2 * BLK, key_rows), jnp.float32),
                pltpu.VMEM((units, 2 * BLK, 128), jnp.float32),
                pltpu.VMEM((units, 2 * BLK, 128), jnp.float32),
                pltpu.VMEM((units, 2 * BLK, 128), jnp.float32),
                pltpu.VMEM((units, 2 * BLK, 128), jnp.float32),
            ],
        ),
        out_shape=[
            jax.ShapeDtypeStruct((rows, width), jnp.bfloat16),
            jax.ShapeDtypeStruct((width // 128, 8, blocks * 2 * BLK), jnp.float32),
        ],
        compiler_params=pltpu.CompilerParams(vmem_limit_bytes=48 << 20),
        cost_estimate=pl.CostEstimate(flops=pairs * 512, transcendentals=pairs, bytes_accessed=4 * (rows + keys) * width),
    )(*(scalars or ()), q, *k_list, *v_list)


def attention_backward(q, q_col, do, o, lse, k_list, k_col, v_list, v_col, width, scalars, key_rows, units=2, per_group=2, o_col=0):
    pieces = len(k_list)
    lanes = units * 128
    rows = q.shape[0]
    keys = sum(k.shape[0] for k in k_list)
    chunks = keys // key_rows
    groups, blocks = width // lanes, rows // BLK
    masked = scalars is not None
    spec_q = pl.BlockSpec((BLK, lanes), lambda h, i, *_: (i, q_col + h))
    spec_o = pl.BlockSpec((BLK, lanes), lambda h, i, *_: (i, o_col + h))
    spec_dq = pl.BlockSpec((BLK, lanes), lambda h, i, *_: (i, h))
    spec_lse = pl.BlockSpec((units, 8, 2 * BLK), lambda h, i, *_: (o_col + h, 0, i))
    specs_k = [pl.BlockSpec((k.shape[0], lanes), lambda h, i, *_: (0, k_col + h)) for k in k_list]
    specs_v = [pl.BlockSpec((v.shape[0], lanes), lambda h, i, *_: (0, v_col + h)) for v in v_list]
    outs_k = [pl.BlockSpec((k.shape[0], lanes), lambda h, i, *_: (0, h)) for k in k_list]
    body = functools.partial(backward_body, masked, units, chunks, key_rows, pieces, per_group)
    pairs = rows * keys * (width // 64)
    shape_k = [jax.ShapeDtypeStruct((k.shape[0], width), jnp.bfloat16) for k in k_list]
    return pl.pallas_call(
        body,
        grid_spec=pltpu.PrefetchScalarGridSpec(
            num_scalar_prefetch=3 if masked else 0,
            grid=(groups, blocks),
            in_specs=[spec_q, spec_o, spec_o, spec_lse] + specs_k + specs_v,
            out_specs=[spec_dq] + outs_k + outs_k,
            scratch_shapes=[
                pltpu.VMEM((units, 2 * BLK, 128), jnp.bfloat16),
                pltpu.VMEM((units, 2 * BLK, 128), jnp.bfloat16),
                pltpu.VMEM((units, 8, 2 * BLK), jnp.float32),
                pltpu.VMEM((units, 2 * BLK, 128), jnp.float32),
                pltpu.VMEM((units, keys, 128), jnp.float32),
                pltpu.VMEM((units, keys, 128), jnp.float32),
            ],
        ),
        out_shape=[jax.ShapeDtypeStruct((rows, width), jnp.bfloat16)] + shape_k + shape_k,
        compiler_params=pltpu.CompilerParams(vmem_limit_bytes=48 << 20),
        cost_estimate=pl.CostEstimate(flops=pairs * 1280, transcendentals=pairs, bytes_accessed=8 * (rows + keys) * width),
    )(*(scalars or ()), q, do, o, lse, *k_list, *v_list)


def norm_sums(summed):
    mean = jnp.mean(summed, axis=-1, keepdims=True)
    centred = summed - mean
    inverse = lax.rsqrt(jnp.mean(centred * centred, axis=-1, keepdims=True) + epsilon)
    return centred * inverse, inverse


def feed_body(
    core_ref, hidden_ref, upstream_ref, weights_ref, expand_bias_ref, vectors_ref,
    out_ref, grad_hidden_ref, send_ref, keep_ref, grad_bias_ref, sums_ref,
    low, expanded, activated, total, grad_low,
):
    step = pl.program_id(0)
    blocks = pl.num_programs(0) // 2
    block = step % blocks
    width = hidden_ref.shape[1]
    first = weights_ref[:, 0, :128].reshape(width, width)
    second = weights_ref[:, 0, 128:].reshape(width, width)

    @pl.when(step == 0)
    def begin():
        low[...] = hidden_ref[...].astype(jnp.bfloat16)
        total[...] = residual_scale * hidden_ref[...] + vectors_ref[0:1]

    @pl.when(step < blocks)
    def forward():
        wide = mxu(low[...], first, NN) + expand_bias_ref[0]
        expanded[block] = wide
        active = gelu_tanh(wide).astype(jnp.bfloat16)
        activated[block] = active
        total[...] += mxu(active, second, NN)

    @pl.when(step == blocks)
    def turn():
        normed, inverse = norm_sums(total[...])
        gain = vectors_ref[1:2]
        out_ref[...] = (normed * gain + vectors_ref[2:3]).astype(out_ref.dtype)
        upstream = upstream_ref[...].astype(jnp.float32)
        scaled = upstream * gain
        grad = inverse * (
            scaled
            - jnp.mean(scaled, axis=-1, keepdims=True)
            - normed * jnp.mean(scaled * normed, axis=-1, keepdims=True)
        )
        grad_low[...] = grad.astype(jnp.bfloat16)
        grad_hidden_ref[...] = residual_scale * grad
        sums_ref[0:1] = jnp.sum(grad_low[...].astype(jnp.float32), axis=0, keepdims=True)
        sums_ref[1:2] = jnp.sum(upstream * normed, axis=0, keepdims=True)
        sums_ref[2:3] = jnp.sum(upstream, axis=0, keepdims=True)

    @pl.when(step >= blocks)
    def backward():
        grad_active = mxu(grad_low[...], second, NT)
        grad_wide = (grad_active * gelu_slope(expanded[block])).astype(jnp.bfloat16)
        grad_second = mxu(activated[block], grad_low[...], TN).astype(jnp.bfloat16).reshape(-1, 128, width)
        grad_first = mxu(low[...], grad_wide, TN).astype(jnp.bfloat16).reshape(-1, 128, width)

        @pl.when(block < blocks // 2)
        def to_send():
            send_ref[:, 0, 128:] = grad_second
            send_ref[:, 0, :128] = grad_first

        @pl.when(block >= blocks // 2)
        def to_keep():
            keep_ref[:, 0, 128:] = grad_second
            keep_ref[:, 0, :128] = grad_first

        grad_bias_ref[0] = jnp.sum(grad_wide.astype(jnp.float32), axis=0, keepdims=True)
        grad_hidden_ref[...] += mxu(grad_wide, first, NT)


def feed_forward(core, hidden, upstream, weights, expand_bias, vectors):
    rows, width = hidden.shape
    groups, blocks = weights.shape[:2]
    half = blocks // 2

    def at(i, core_ref):
        return (i + half * (1 - core_ref[0])) % blocks

    def back(i, core_ref):
        return (jnp.maximum(i - blocks, 0) + half * (1 - core_ref[0])) % blocks

    whole = pl.BlockSpec((rows, width), lambda i, c: (0, 0))
    once = pl.BlockSpec((rows, width), lambda i, c: (0, 0), pipeline_mode=pl.Buffered(1))
    f32, bf16 = jnp.float32, jnp.bfloat16
    part = (groups, 1, 256, width)
    return pl.pallas_call(
        feed_body,
        grid_spec=pltpu.PrefetchScalarGridSpec(
            num_scalar_prefetch=1,
            grid=(2 * blocks,),
            in_specs=[
                once, once,
                pl.BlockSpec(part, lambda i, c: (0, at(i, c), 0, 0)),
                pl.BlockSpec((1, 1, width), lambda i, c: (at(i, c), 0, 0)),
                pl.BlockSpec((8, width), lambda i, c: (0, 0)),
            ],
            out_specs=[
                whole, whole,
                pl.BlockSpec(part, lambda i, c: (0, jnp.clip(i - blocks, 0, half - 1), 0, 0)),
                pl.BlockSpec(part, lambda i, c: (0, jnp.clip(i - blocks - half, 0, half - 1), 0, 0)),
                pl.BlockSpec((1, 1, width), lambda i, c: (back(i, c), 0, 0)),
                pl.BlockSpec((8, width), lambda i, c: (0, 0)),
            ],
            scratch_shapes=[
                pltpu.VMEM((rows, width), bf16),
                pltpu.VMEM((blocks, rows, width), f32),
                pltpu.VMEM((blocks, rows, width), bf16),
                pltpu.VMEM((rows, width), f32),
                pltpu.VMEM((rows, width), bf16),
            ],
        ),
        out_shape=[
            jax.ShapeDtypeStruct((rows, width), bf16),
            jax.ShapeDtypeStruct((rows, width), f32),
            jax.ShapeDtypeStruct((groups, half, 256, width), bf16),
            jax.ShapeDtypeStruct((groups, half, 256, width), bf16),
            jax.ShapeDtypeStruct((blocks, 1, width), f32),
            jax.ShapeDtypeStruct((8, width), f32),
        ],
        compiler_params=pltpu.CompilerParams(vmem_limit_bytes=60 << 20),
        cost_estimate=pl.CostEstimate(flops=12 * rows * width * width * blocks, transcendentals=2 * rows * width * blocks, bytes_accessed=52 << 20),
    )(core.reshape(1).astype(jnp.int32), hidden, upstream, weights, expand_bias, vectors)


def core_perm():
    return [(c, c ^ 1) for c in range(4)]


def y_perm():
    return [(c, c ^ 2) for c in range(4)]


def diagonal_perm():
    return [(c, c ^ 3) for c in range(4)]


def x_perm():
    return [(f, f ^ 1) for f in range(8)]


def z_perm(k):
    return [(f, f ^ (2 * k)) for f in range(8)]


def to_core(v):
    return lax.ppermute(v, "ctx", core_perm())


def to_y(v):
    return lax.ppermute(v, "ctx", y_perm())


def to_diagonal(v):
    return lax.ppermute(v, "ctx", diagonal_perm())


def to_x(v):
    return lax.ppermute(v, "fsdp", x_perm())


def to_z(v, k):
    return lax.ppermute(v, "fsdp", z_perm(k))


def fsdp_pieces(own):
    along = [own] + [to_z(own, k) for k in (1, 2, 3)]
    return along + [to_x(piece) for piece in along]


def fsdp_sources(me):
    return [me ^ (2 * k + d) for d in (0, 1) for k in range(4)]


def place_body(plan, *refs):
    offsets, refs = refs[0], refs[1:]
    outs, sems = refs[-1 - len(plan):-1], refs[-1]
    pieces = refs[:-1 - len(plan)]
    copies = []
    for i, piece in enumerate(pieces):
        for s, (lead, first, rows) in enumerate(plan):
            source = piece if lead is None else piece.at[lead]
            start = pl.multiple_of(offsets[i] * rows, rows)
            copy = pltpu.make_async_copy(source.at[pl.ds(first, rows)], outs[s].at[pl.ds(start, rows)], sems.at[i, s])
            copy.start()
            copies.append(copy)
    for copy in copies:
        copy.wait()


def place(pieces, slots, plan):
    columns = pieces[0].shape[-1]
    count = len(pieces)
    out = [jax.ShapeDtypeStruct((count * rows, columns), pieces[0].dtype) for _, _, rows in plan]
    anywhere = pl.BlockSpec(memory_space=pl.ANY)
    moved = 4 * count * columns * sum(rows for _, _, rows in plan)
    return pl.pallas_call(
        functools.partial(place_body, plan),
        in_specs=[pl.BlockSpec(memory_space=pltpu.SMEM)] + [anywhere] * count,
        out_specs=[pl.BlockSpec(memory_space=pltpu.VMEM)] * len(plan),
        out_shape=out,
        scratch_shapes=[pltpu.SemaphoreType.DMA((count, len(plan)))],
        compiler_params=pltpu.CompilerParams(vmem_limit_bytes=(moved // 2) + (4 << 20)),
        cost_estimate=pl.CostEstimate(flops=0, transcendentals=0, bytes_accessed=moved),
    )(jnp.stack(slots).astype(jnp.int32), *pieces)


def after(value, other):
    return lax.optimization_barrier((value, other))[0]


def xor_take(stack, me):
    return jnp.concatenate([lax.dynamic_index_in_dim(stack, n ^ me, 0) for n in range(stack.shape[0])])


def from_fsdp(blocks):
    got = lax.all_to_all(blocks, "fsdp", 0, 0)
    return jnp.sum(got.astype(jnp.float32), axis=0)


def part_of(parts, index, axis):
    return lax.dynamic_index_in_dim(parts, index, axis, keepdims=False)


def added(keep, got):
    return (keep.astype(jnp.float32) + got.astype(jnp.float32)).astype(jnp.bfloat16)


def halves_dot(pairs, core):
    def side(index):
        terms = []
        for left, right in pairs:
            half = right.shape[1] // 2
            chosen = lax.dynamic_slice_in_dim(right, index * half, half, axis=1)
            terms.append(jnp.dot(left.T, chosen, preferred_element_type=jnp.float32).astype(jnp.bfloat16))
        return with_layout_constraint(jnp.concatenate(terms, axis=1), Layout(major_to_minor=(0, 1)))

    return side(core), side(core ^ 1)


def over_z(parts, z):
    got = [to_z(part_of(parts, z ^ k, 1), k) for k in (1, 2, 3)]
    total = part_of(parts, z, 1).astype(jnp.float32)
    return (total + got[0].astype(jnp.float32) + got[1].astype(jnp.float32) + got[2].astype(jnp.float32)).astype(jnp.bfloat16)


def ctx_pieces(own):
    line = to_y(own)
    return [own, to_core(own), line, to_core(line)]


def spread_feed_body(core_ref, *refs):
    (own, other), (expand_ref, reduce_ref) = refs[:2], refs[2:]
    for index, source in ((core_ref[0], own), (1 - core_ref[0], other)):
        for p in range(2):
            at = pl.multiple_of(index * 256 + p * 128, 128)
            reduce_ref[pl.ds(at, 128), :] = source[p, 128:].astype(jnp.float32)
            for f in range(8):
                expand_ref[:, pl.ds(at + f * 512, 128)] = source[p, :128, f * 128:(f + 1) * 128].astype(jnp.float32)


def spread_projection_body(me_ref, *refs):
    pieces, (out_ref, vectors_ref) = refs[:4], refs[4:]
    total = jnp.zeros((8, 384), jnp.float32)
    for k in range(4):
        at = pl.multiple_of((me_ref[0] ^ k) * 256, 128)
        for part in range(3):
            for pair in range(2):
                source = pieces[k][:128, pair * 384 + part * 128:pair * 384 + (part + 1) * 128]
                out_ref[:, pl.ds(at + part * 1024 + pair * 128, 128)] = source.astype(jnp.float32)
        total = total + pieces[k][128:136, 384:].astype(jnp.float32)
    for i in range(18):
        vectors_ref[i:i + 1] = total[i // 3:i // 3 + 1, (i % 3) * 128:(i % 3 + 1) * 128]


def spread_middle_body(core_ref, *refs):
    (early, early_other, late, late_other), (memory_ref, query_ref, cross_ref, self_ref) = refs[:4], refs[4:]
    for index, first, second in ((core_ref[0], early, late), (1 - core_ref[0], early_other, late_other)):
        for half, source in ((0, first), (512, second)):
            at = pl.multiple_of(half + index * 256, 256)
            memory_ref[:, pl.ds(at, 256)] = source[:, 0:256].astype(jnp.float32)
            memory_ref[:, pl.ds(at + 1024, 256)] = source[:, 256:512].astype(jnp.float32)
            query_ref[:, pl.ds(at, 256)] = source[:, 512:768].astype(jnp.float32)
        at = pl.multiple_of(index * 512, 512)
        cross_ref[:, pl.ds(at, 512)] = first[:, 768:].astype(jnp.float32)
        self_ref[:, pl.ds(at, 512)] = second[:, 768:].astype(jnp.float32)


def spread(body, index, pieces, shapes):
    whole = pl.BlockSpec(memory_space=pltpu.VMEM)
    moved = sum(p.size * 2 for p in pieces) + sum(a * b * 4 for a, b in shapes)
    return pl.pallas_call(
        body,
        in_specs=[pl.BlockSpec(memory_space=pltpu.SMEM)] + [whole] * len(pieces),
        out_specs=[whole] * len(shapes),
        out_shape=[jax.ShapeDtypeStruct(shape, jnp.float32) for shape in shapes],
        compiler_params=pltpu.CompilerParams(vmem_limit_bytes=moved + (4 << 20)),
        cost_estimate=pl.CostEstimate(flops=0, transcendentals=0, bytes_accessed=moved),
    )(index.reshape(1).astype(jnp.int32), *pieces)


def chip_sums(terms, rows):
    pairs = terms.reshape(2, 2, rows, terms.shape[1])
    got = to_core(pairs[:, 1])
    return pairs[0, 0].astype(jnp.float32) + got[0].astype(jnp.float32), added(pairs[1, 0], got[1])


def tiled_shards(
    tokens,
    memory,
    cotangent,
    block_map,
    block_order,
    self_projection,
    self_output,
    self_query_bias,
    self_value_bias,
    self_output_bias,
    first_gain,
    first_shift,
    cross_query,
    cross_memory,
    cross_output,
    cross_query_bias,
    cross_value_bias,
    cross_output_bias,
    second_gain,
    second_shift,
    expand_weight,
    reduce_weight,
    expand_bias,
    reduce_bias,
    third_gain,
    third_shift,
):
    bf16 = jnp.bfloat16
    f32 = jnp.float32
    own_rows = tokens[0]
    rows, width = own_rows.shape
    me_c, me_f = lax.axis_index("ctx"), lax.axis_index("fsdp")
    core, line, z, x = me_c % 2, me_c // 2, me_f // 2, me_f % 2
    share = width // 4

    def dot(left, right):
        return jnp.dot(left, right, preferred_element_type=f32)

    vectors = [self_query_bias, self_value_bias, self_output_bias, first_gain, first_shift, cross_query_bias,
               cross_value_bias, cross_output_bias, second_gain, second_shift, reduce_bias, third_gain, third_shift]
    vectors += [expand_bias[i * 128:(i + 1) * 128] for i in range(4)] + [jnp.zeros((128,), bf16)]
    vector_rows = jnp.stack([jnp.concatenate(vectors[i * 6:i * 6 + 6]) for i in range(3)])
    columns = [lax.dynamic_slice(self_projection, (0, part * width + me_c * share), (128, share)) for part in range(3)]
    own_piece = jnp.concatenate([jnp.concatenate(columns, axis=1), vector_rows, jnp.zeros((13, 3 * share), bf16)])
    projection_pieces = fsdp_pieces(own_piece)
    rows_y = to_y(own_rows)
    rows_core = to_core(own_rows)
    rows_diagonal = to_core(after(rows_y, projection_pieces[1:4]))
    sequence = jnp.concatenate([own_rows, rows_core, rows_y, rows_diagonal])
    sources = fsdp_sources(me_f)
    projection, vector_blocks = place(projection_pieces, sources, ((None, 0, 128), (None, 128, 16)))
    vector_blocks = vector_blocks.reshape(8, 16, 3 * share).astype(f32)
    gathered = [vector_blocks[:, i // 6, (i % 6) * 128:(i % 6 + 1) * 128].reshape(width) for i in range(17)]
    (query_bias, value_bias, out_bias, gain_one, shift_one, cross_qbias, cross_vbias, cross_obias,
     gain_two, shift_two, reduce_bias_full, gain_three, shift_three) = gathered[:13]
    expand_bias_blocks = jnp.stack(gathered[13:]).reshape(4, 1, width)

    middle = [cross_memory[:, :width], cross_memory[:, width:], self_output, cross_query, cross_output]
    middle_own = jnp.stack([lax.dynamic_slice_in_dim(weight, me_c * 32, 32) for weight in middle])
    middle_all = lax.all_gather(middle_own, ("fsdp", "ctx"), axis=0)
    memory_key_full, memory_value_full, self_out_full, cross_query_full, cross_out_full = [
        middle_all[:, i].reshape(width, width) for i in range(5)
    ]
    expand_columns = lax.dynamic_index_in_dim(expand_weight.reshape(128, 8, 4, 128), me_c, 2, keepdims=False)
    feed_own = jnp.concatenate([expand_columns.reshape(128, width), lax.dynamic_slice_in_dim(reduce_weight, me_c * 128, 128)])

    memory_rows = memory[0]
    memory_y = to_y(after(memory_rows, projection_pieces[4:]))
    memory_core = to_core(memory_rows)

    projected = dot(sequence, projection)
    bias = jnp.concatenate([
        lax.dynamic_slice_in_dim(query_bias, me_c * share, share),
        jnp.zeros((share,), f32),
        lax.dynamic_slice_in_dim(value_bias, me_c * share, share),
    ])
    qkv = (projected + bias).astype(bf16)
    scalars = (block_order[0], block_map[0].reshape(-1), me_c.reshape(1).astype(jnp.int32))
    heads_out, self_lse = attention_forward(qkv, 0, [qkv], 1, [qkv], 2, share, scalars, BLK)
    heads_out, memory_y = lax.optimization_barrier((heads_out, memory_y))
    memory_all = jnp.concatenate([memory_rows, memory_core, memory_y, to_core(memory_y)])

    feed_weights = lax.all_gather(after(feed_own, (middle_all, heads_out)), ("fsdp", "ctx"), axis=0, tiled=True)
    memory_keys = dot(memory_all, memory_key_full).astype(bf16)
    memory_values = (dot(memory_all, memory_value_full) + cross_vbias).astype(bf16)

    pieces = [heads_out[i * rows:(i + 1) * rows] for i in range(4)]
    others = after([to_core(pieces[1]), to_y(pieces[2]), to_diagonal(pieces[3])], (memory_keys, memory_values))
    arrived = jnp.stack([pieces[0]] + others)
    attended = jnp.concatenate([part_of(arrived, n ^ me_c, 0) for n in range(4)], axis=1)
    branch = dot(attended, self_out_full) + out_bias
    hidden_one, normed_one, inverse_one = layer_norm(residual_scale * own_rows.astype(f32) + branch, gain_one, shift_one)

    hidden_low = hidden_one.astype(bf16)
    cross_queries = (dot(hidden_low, cross_query_full) + cross_qbias).astype(bf16)
    cross_low, cross_lse = attention_forward(cross_queries, 0, [memory_keys], 0, [memory_values], 0, width, None, rows)
    cross_branch = dot(cross_low, cross_out_full) + cross_obias
    hidden_two, normed_two, inverse_two = layer_norm(residual_scale * hidden_one + cross_branch, gain_two, shift_two)

    feed_vectors = jnp.concatenate([jnp.stack([reduce_bias_full, gain_three, shift_three]), jnp.zeros((5, width), f32)])
    output, grad_hidden_two, feed_send, feed_keep, grad_expand_bias, feed_sums = feed_forward(
        core, hidden_two, cotangent[0], feed_weights.reshape(8, 4, 256, width), expand_bias_blocks, feed_vectors
    )
    feed_got = to_core(feed_send)

    grad_second, grad_second_gain, grad_second_shift = layer_norm_back(grad_hidden_two, gain_two, normed_two, inverse_two)
    grad_cross_branch = grad_second.astype(bf16)
    grad_cross_output_bias = jnp.sum(grad_cross_branch.astype(f32), axis=0)
    grad_cross_low = dot(grad_cross_branch, cross_out_full.T).astype(bf16)

    def cross_half(half, queries):
        return attention_backward(
            queries, 2 * half, grad_cross_low, cross_low, cross_lse, [memory_keys], 2 * half, [memory_values], 2 * half,
            width // 2, None, rows, o_col=2 * half
        )

    def line_split(summed):
        return summed.reshape(8, 2, 64, summed.shape[1])

    feed_half = added(feed_keep, feed_got).reshape(8 * 512, width)
    feed_share = lax.psum_scatter(feed_half, "fsdp", scatter_dimension=0, tiled=True)
    early_q, early_k, early_v = cross_half(0, after(cross_queries, feed_half))
    first_q, first_k, first_v = early_q, early_k, early_v
    keep, send = halves_dot(
        [(memory_all, first_k), (memory_all, first_v), (hidden_low, first_q), (cross_low, grad_cross_branch)], core
    )
    early_got = to_core(send)
    late_q, late_k, late_v = cross_half(1, after(cross_queries, (keep, send)))
    late_q, late_k, late_v, early_got = lax.optimization_barrier((late_q, late_k, late_v, early_got))
    early = line_split(added(keep, early_got))
    early_send = part_of(early, line ^ 1, 1)
    early_got = to_y(early_send)
    late_q, early_q = after((late_q, early_q), early_send)

    grad_cross_queries = jnp.concatenate([early_q, late_q], axis=1)
    grad_cross_query_bias = jnp.sum(grad_cross_queries.astype(f32), axis=0)
    grad_hidden_one = residual_scale * grad_second + dot(grad_cross_queries, cross_query_full.T)
    grad_first, grad_first_gain, grad_first_shift = layer_norm_back(grad_hidden_one, gain_one, normed_one, inverse_one)
    grad_branch = grad_first.astype(bf16)
    grad_self_output_bias = jnp.sum(grad_branch.astype(f32), axis=0)
    grad_attended = dot(grad_branch, self_out_full.T).astype(bf16)
    by_heads = jnp.stack([grad_attended[:, i * share:(i + 1) * share] for i in range(4)])
    sends = [part_of(by_heads, k ^ me_c, 0) for k in range(4)]
    received = [to_core(sends[1]), to_y(sends[2]), to_diagonal(sends[3])]
    heads_grad = jnp.concatenate([sends[0]] + received)

    ready_q, ready_k, ready_v, ready_branch = after((late_q, late_k, late_v, grad_branch), received[0])
    grad_cross_value_bias = jnp.concatenate([jnp.sum(early_v.astype(f32), axis=0), jnp.sum(ready_v.astype(f32), axis=0)])
    memory_terms = dot(jnp.concatenate([early_k, early_v, ready_k, ready_v], axis=1), jnp.concatenate([
        memory_key_full[:, :width // 2], memory_value_full[:, :width // 2],
        memory_key_full[:, width // 2:], memory_value_full[:, width // 2:],
    ], axis=1).T).astype(bf16)
    memory_near, memory_far = chip_sums(memory_terms, rows)
    late_keep, late_send = halves_dot(
        [(memory_all, ready_k), (memory_all, ready_v), (hidden_low, ready_q), (attended, ready_branch)], core
    )
    late_got = to_core(late_send)
    early = added(part_of(early, line, 1), early_got).reshape(4, 2, 64, 5 * share)

    def heads_back(pair, upstream):
        return attention_backward(
            qkv, pair, upstream, heads_out, self_lse, [qkv], 2 + pair, [qkv], 4 + pair, share // 2, scalars, BLK,
            units=1, o_col=pair,
        )

    def own_blocks(grads):
        return dot(sequence.T, grads).astype(bf16).reshape(8, 128, grads.shape[1])

    vector_grads = jnp.concatenate([
        jnp.stack([
            grad_self_output_bias, grad_first_gain, grad_first_shift, grad_cross_query_bias, grad_cross_value_bias,
            grad_cross_output_bias, grad_second_gain, grad_second_shift,
        ]),
        feed_sums[:3],
        grad_expand_bias.reshape(4, width),
    ])
    vector_rows = vector_grads.reshape(5, 3, 8, 128).transpose(2, 0, 1, 3).reshape(8, 5, 384).astype(bf16)
    heads_grad = after(heads_grad, (early, late_keep, late_send, memory_far, vector_rows))
    memory_got = to_y(memory_far)
    early_got = to_x(part_of(early, x ^ 1, 1))
    first_heads = jnp.concatenate(heads_back(0, heads_grad), axis=1)
    first_heads, early_got, late_got, feed_share = lax.optimization_barrier((first_heads, early_got, late_got, feed_share))
    feed_far = to_y(feed_share)
    first_blocks = own_blocks(first_heads)
    late = added(late_keep, late_got).reshape(4, 2, 128, 5 * share)
    late_got = to_x(part_of(late, x ^ 1, 1))
    early = added(part_of(early, x, 1), early_got)
    early_sends = [part_of(early, z ^ k, 0) for k in (1, 2, 3)]
    first_total = lax.all_to_all(first_blocks, "fsdp", 0, 0)
    second_heads = jnp.concatenate(heads_back(1, after(heads_grad, (first_blocks, late, early_sends))), axis=1)
    early_pieces = [to_z(piece, k) for piece, k in zip(early_sends, (1, 2, 3))]
    second_heads, early_pieces, late_got, memory_got, feed_far, first_total = lax.optimization_barrier(
        (second_heads, early_pieces, late_got, memory_got, feed_far, first_total)
    )
    first_total = jnp.sum(first_total.astype(f32), axis=0)
    second_blocks = own_blocks(second_heads)
    ready_first, ready_second = after((first_heads, second_heads), second_blocks)
    token_terms = (
        dot(ready_first, jnp.concatenate([projection[:, i * share:i * share + 128] for i in range(3)], axis=1).T)
        + dot(ready_second, jnp.concatenate([projection[:, i * share + 128:(i + 1) * share] for i in range(3)], axis=1).T)
    ).astype(bf16)
    token_near, token_far = chip_sums(token_terms, rows)
    feed_near = feed_share
    token_got = to_y(token_far)
    token_grad = (residual_scale * grad_first + token_near + token_got.astype(f32))[None]
    memory_grad = (memory_near + memory_got.astype(f32))[None]

    both_heads = [first_heads.astype(f32), second_heads.astype(f32)]
    head_sums = jnp.stack([
        jnp.concatenate([jnp.sum(half[:, at:at + 128], axis=0) for half in both_heads]) for at in (0, 256)
    ])
    head_sums = lax.dynamic_update_slice(jnp.zeros((2, width), f32), head_sums, (0, me_c * share))
    head_rows = jnp.concatenate([head_sums, jnp.zeros((1, width), f32)])
    head_rows = head_rows.reshape(3, 8, 128).transpose(1, 0, 2).reshape(8, 1, 384).astype(bf16)
    blocks = jnp.concatenate([second_blocks, vector_rows, head_rows, jnp.zeros((8, 10, 384), bf16)], axis=1)
    second_total = from_fsdp(blocks)
    padded = jnp.concatenate([first_total, jnp.zeros((16, 384), f32)])
    total = after(jnp.concatenate([padded, second_total], axis=1).astype(bf16), token_got)

    early = part_of(early, z, 0).astype(f32)
    for piece in early_pieces:
        early = early + piece.astype(f32)
    early = early.astype(bf16)
    late = over_z(added(after(part_of(late, x, 1), (blocks, token_far)), late_got)[None], z)[0]
    early_got = to_y(early)
    early = jnp.concatenate([jnp.where(line == 0, early, early_got), jnp.where(line == 0, early_got, early)])
    late = added(late, to_y(late))
    grad_cross_memory, grad_cross_query, grad_cross_output, grad_self_output = spread(
        spread_middle_body, core, [early, to_core(early), late, to_core(late)],
        [(128, 2 * width), (128, width), (128, width), (128, width)],
    )

    grad_self_projection, sums = spread(
        spread_projection_body, me_c, ctx_pieces(total), [(128, 3 * width), (18, 128)]
    )

    feed_own = added(feed_near, feed_far).reshape(2, 256, width)
    grad_expand, grad_reduce = spread(spread_feed_body, core, [feed_own, to_core(feed_own)], [(128, 4 * width), (512, width)])

    return (
        output[None],
        token_grad,
        memory_grad,
        grad_self_projection,
        grad_self_output,
        sums[15],
        sums[16],
        sums[0],
        sums[1],
        sums[2],
        grad_cross_query,
        grad_cross_memory,
        grad_cross_output,
        sums[3],
        sums[4],
        sums[5],
        sums[6],
        sums[7],
        grad_expand,
        grad_reduce,
        sums[11:15].reshape(512),
        sums[8],
        sums[9],
        sums[10],
    )


def head_split(matrix):
    return matrix.reshape(matrix.shape[0], HEADS, HEAD_DIM)


def piece_size(length):
    return min(512, length)


def piece_masks(key_blocks, allowed_rows):
    length = key_blocks.shape[0]
    piece = piece_size(length)
    count = length // piece
    if allowed_rows is None:
        return jnp.ones((count, 1, 1), jnp.bool_)
    nblocks = allowed_rows.shape[1]
    onehot = (key_blocks[:, None] == jnp.arange(nblocks, dtype=jnp.int32)[None, :]).astype(
        jnp.float32
    )
    live = jnp.dot(allowed_rows, onehot.T) > 0.5
    return jnp.moveaxis(live.reshape(live.shape[0], count, piece), 1, 0)


def masked_scores(query_heads, key_piece, live):
    scores = (
        jnp.einsum("qhd,khd->hqk", query_heads, key_piece, preferred_element_type=jnp.float32)
        * score_scale
    )
    return jnp.where(live[None], scores, masked_score)


def run_guarded(guarded, live, work, fallback):
    if guarded:
        return lax.cond(jnp.any(live), work, lambda unused: fallback, live)
    return work(live)


def attend_forward(query_heads, key_heads, value_heads, live_pieces, guarded):
    count = live_pieces.shape[0]
    piece = key_heads.shape[0] // count
    key_pieces = key_heads.reshape((count, piece) + key_heads.shape[1:])
    value_pieces = value_heads.reshape((count, piece) + value_heads.shape[1:])
    rows = query_heads.shape[0]

    def first_step(carry, inputs):
        run_max, run_sum = carry
        key_piece, live = inputs

        def work(live_now):
            scores = masked_scores(query_heads, key_piece, live_now)
            new_max = jnp.maximum(run_max, jnp.max(scores, axis=-1))
            shifted = jnp.where(live_now[None], jnp.exp(scores - new_max[:, :, None]), 0.0)
            return (new_max, run_sum * jnp.exp(run_max - new_max) + jnp.sum(shifted, axis=-1))

        return (run_guarded(guarded, live, work, (run_max, run_sum)), None)

    start = (
        jnp.full((HEADS, rows), masked_score, jnp.float32),
        jnp.zeros((HEADS, rows), jnp.float32),
    )
    (final_max, final_sum), unused = lax.scan(first_step, start, (key_pieces, live_pieces))
    log_total = final_max + jnp.log(final_sum)

    def second_step(total, inputs):
        key_piece, value_piece, live = inputs

        def work(live_now):
            scores = masked_scores(query_heads, key_piece, live_now)
            probs = jnp.exp(scores - log_total[:, :, None]).astype(jnp.bfloat16)
            return total + jnp.einsum(
                "hqk,khd->qhd", probs, value_piece, preferred_element_type=jnp.float32
            )

        return (run_guarded(guarded, live, work, total), None)

    empty = jnp.zeros((rows, HEADS, HEAD_DIM), jnp.float32)
    attended, unused = lax.scan(second_step, empty, (key_pieces, value_pieces, live_pieces))
    return (attended, log_total)


def attend_backward(
    query_heads, key_heads, value_heads, log_total, grad_heads, delta, live_pieces, guarded
):
    count = live_pieces.shape[0]
    piece = key_heads.shape[0] // count
    key_pieces = key_heads.reshape((count, piece) + key_heads.shape[1:])
    value_pieces = value_heads.reshape((count, piece) + value_heads.shape[1:])
    rows = query_heads.shape[0]
    blank = jnp.zeros((piece, HEADS, HEAD_DIM), jnp.float32)

    def back_step(grad_query, inputs):
        key_piece, value_piece, live = inputs

        def work(live_now):
            scores = masked_scores(query_heads, key_piece, live_now)
            probs = jnp.exp(scores - log_total[:, :, None])
            grad_probs = jnp.einsum(
                "qhd,khd->hqk", grad_heads, value_piece, preferred_element_type=jnp.float32
            )
            grad_scores = (probs * (grad_probs - delta[:, :, None])).astype(jnp.bfloat16)
            new_query = (
                grad_query
                + jnp.einsum(
                    "hqk,khd->qhd", grad_scores, key_piece, preferred_element_type=jnp.float32
                )
                * score_scale
            )
            grad_key = (
                jnp.einsum(
                    "hqk,qhd->khd", grad_scores, query_heads, preferred_element_type=jnp.float32
                )
                * score_scale
            )
            grad_value = jnp.einsum(
                "hqk,qhd->khd",
                probs.astype(jnp.bfloat16),
                grad_heads,
                preferred_element_type=jnp.float32,
            )
            return (new_query, (grad_key, grad_value))

        return run_guarded(guarded, live, work, (grad_query, (blank, blank)))

    empty = jnp.zeros((rows, HEADS, HEAD_DIM), jnp.float32)
    grad_query, (key_grads, value_grads) = lax.scan(
        back_step, empty, (key_pieces, value_pieces, live_pieces)
    )
    width = HEADS * HEAD_DIM
    return (
        grad_query.reshape(rows, width),
        key_grads.reshape(-1, width),
        value_grads.reshape(-1, width),
    )


def plain_shards(
    tokens,
    memory,
    cotangent,
    block_map,
    block_order,
    self_projection,
    self_output,
    self_query_bias,
    self_value_bias,
    self_output_bias,
    first_gain,
    first_shift,
    cross_query,
    cross_memory,
    cross_output,
    cross_query_bias,
    cross_value_bias,
    cross_output_bias,
    second_gain,
    second_shift,
    expand_weight,
    reduce_weight,
    expand_bias,
    reduce_bias,
    third_gain,
    third_shift,
):
    bf16 = jnp.bfloat16
    f32 = jnp.float32
    rows_in = tokens[0]
    rows = rows_in.shape[0]
    width = rows_in.shape[1]
    ctx_count = lax.axis_size("ctx")
    slot = lax.axis_index("ctx")
    positions = jnp.arange(rows * ctx_count, dtype=jnp.int32)
    group_index = positions // rows
    group_match = group_index[:, None] == jnp.arange(ctx_count, dtype=jnp.int32)[None, :]
    group_place = jnp.sum(jnp.where(group_match, block_order[0][None, :], 0), axis=1)
    key_blocks = (group_place * rows + positions % rows) // BLK
    own_blocks = lax.dynamic_slice_in_dim(key_blocks, slot * rows, rows)
    nblocks = block_map.shape[1]
    own_onehot = (own_blocks[:, None] == jnp.arange(nblocks, dtype=jnp.int32)[None, :]).astype(f32)
    allowed_rows = jnp.dot(own_onehot, block_map[0].astype(f32))
    self_live = piece_masks(key_blocks, allowed_rows)
    (
        projection_full,
        self_out_full,
        query_bias_full,
        value_bias_full,
        out_bias_full,
        gain_one,
        shift_one,
    ) = (
        lax.all_gather(self_projection, "fsdp", axis=0, tiled=True),
        lax.all_gather(self_output, "fsdp", axis=0, tiled=True),
        lax.all_gather(self_query_bias, "fsdp", axis=0, tiled=True),
        lax.all_gather(self_value_bias, "fsdp", axis=0, tiled=True),
        lax.all_gather(self_output_bias, "fsdp", axis=0, tiled=True),
        lax.all_gather(first_gain, "fsdp", axis=0, tiled=True),
        lax.all_gather(first_shift, "fsdp", axis=0, tiled=True),
    )
    projected = jnp.dot(rows_in, projection_full, preferred_element_type=f32)
    queries = (projected[:, :width] + query_bias_full).astype(bf16)
    keys_own = projected[:, width : 2 * width].astype(bf16)
    values_own = (projected[:, 2 * width :] + value_bias_full).astype(bf16)
    keys_all, values_all = (
        lax.all_gather(keys_own, "ctx", axis=0, tiled=True),
        lax.all_gather(values_own, "ctx", axis=0, tiled=True),
    )
    query_heads = head_split(queries)
    key_heads = head_split(keys_all)
    value_heads = head_split(values_all)
    attended, self_total = attend_forward(query_heads, key_heads, value_heads, self_live, True)
    attended_low = attended.reshape(rows, width).astype(bf16)
    branch = jnp.dot(attended_low, self_out_full, preferred_element_type=f32) + out_bias_full
    hidden_one, normed_one, inverse_one = layer_norm(
        residual_scale * rows_in.astype(f32) + branch, gain_one, shift_one
    )
    (
        cross_query_full,
        cross_memory_full,
        cross_out_full,
        cross_qbias_full,
        cross_vbias_full,
        cross_obias_full,
        gain_two,
        shift_two,
    ) = (
        lax.all_gather(cross_query, "fsdp", axis=0, tiled=True),
        lax.all_gather(cross_memory, "fsdp", axis=0, tiled=True),
        lax.all_gather(cross_output, "fsdp", axis=0, tiled=True),
        lax.all_gather(cross_query_bias, "fsdp", axis=0, tiled=True),
        lax.all_gather(cross_value_bias, "fsdp", axis=0, tiled=True),
        lax.all_gather(cross_output_bias, "fsdp", axis=0, tiled=True),
        lax.all_gather(second_gain, "fsdp", axis=0, tiled=True),
        lax.all_gather(second_shift, "fsdp", axis=0, tiled=True),
    )
    hidden_low = hidden_one.astype(bf16)
    cross_queries = (
        jnp.dot(hidden_low, cross_query_full, preferred_element_type=f32) + cross_qbias_full
    ).astype(bf16)
    memory_rows = memory[0]
    memory_proj = jnp.dot(memory_rows, cross_memory_full, preferred_element_type=f32)
    memory_keys = memory_proj[:, :width].astype(bf16)
    memory_values = (memory_proj[:, width:] + cross_vbias_full).astype(bf16)
    memory_keys_all, memory_values_all = (
        lax.all_gather(memory_keys, "ctx", axis=0, tiled=True),
        lax.all_gather(memory_values, "ctx", axis=0, tiled=True),
    )
    cross_heads = head_split(cross_queries)
    memory_key_heads = head_split(memory_keys_all)
    memory_value_heads = head_split(memory_values_all)
    cross_live = piece_masks(jnp.zeros((memory_keys_all.shape[0],), jnp.int32), None)
    cross_attended, cross_total = attend_forward(
        cross_heads, memory_key_heads, memory_value_heads, cross_live, False
    )
    cross_low = cross_attended.reshape(rows, width).astype(bf16)
    cross_branch = jnp.dot(cross_low, cross_out_full, preferred_element_type=f32) + cross_obias_full
    hidden_two, normed_two, inverse_two = layer_norm(
        residual_scale * hidden_one + cross_branch, gain_two, shift_two
    )
    expand_full, reduce_full, expand_bias_full, reduce_bias_full, gain_three, shift_three = (
        lax.all_gather(expand_weight, "fsdp", axis=0, tiled=True),
        lax.all_gather(reduce_weight, "fsdp", axis=0, tiled=True),
        lax.all_gather(expand_bias, "fsdp", axis=0, tiled=True),
        lax.all_gather(reduce_bias, "fsdp", axis=0, tiled=True),
        lax.all_gather(third_gain, "fsdp", axis=0, tiled=True),
        lax.all_gather(third_shift, "fsdp", axis=0, tiled=True),
    )
    hidden_two_low = hidden_two.astype(bf16)
    expanded = jnp.dot(hidden_two_low, expand_full, preferred_element_type=f32) + expand_bias_full
    activated = gelu_tanh(expanded).astype(bf16)
    reduced = jnp.dot(activated, reduce_full, preferred_element_type=f32) + reduce_bias_full
    result, normed_three, inverse_three = layer_norm(
        residual_scale * hidden_two + reduced, gain_three, shift_three
    )
    output = result.astype(bf16)[None]
    upstream = cotangent[0].astype(f32)
    grad_third, grad_third_gain, grad_third_shift = layer_norm_back(
        upstream, gain_three, normed_three, inverse_three
    )
    grad_reduced = grad_third.astype(bf16)
    grad_reduce_bias = jnp.sum(grad_reduced.astype(f32), axis=0)
    grad_reduce_weight = jnp.dot(activated.T, grad_reduced, preferred_element_type=f32)
    grad_activated = jnp.dot(grad_reduced, reduce_full.T, preferred_element_type=f32)
    grad_expanded = (grad_activated * gelu_slope(expanded)).astype(bf16)
    grad_expand_bias = jnp.sum(grad_expanded.astype(f32), axis=0)
    grad_expand_weight = jnp.dot(hidden_two_low.T, grad_expanded, preferred_element_type=f32)
    grad_hidden_two = residual_scale * grad_third + jnp.dot(
        grad_expanded, expand_full.T, preferred_element_type=f32
    )
    grad_second, grad_second_gain, grad_second_shift = layer_norm_back(
        grad_hidden_two, gain_two, normed_two, inverse_two
    )
    grad_cross_branch = grad_second.astype(bf16)
    grad_cross_output_bias = jnp.sum(grad_cross_branch.astype(f32), axis=0)
    grad_cross_output = jnp.dot(cross_low.T, grad_cross_branch, preferred_element_type=f32)
    grad_cross_low = jnp.dot(
        grad_cross_branch, cross_out_full.T, preferred_element_type=f32
    ).astype(bf16)
    grad_cross_heads = head_split(grad_cross_low)
    cross_delta = jnp.sum(grad_cross_heads.astype(f32) * cross_attended, axis=-1).T
    grad_cross_queries, memory_key_terms, memory_value_terms = attend_backward(
        cross_heads,
        memory_key_heads,
        memory_value_heads,
        cross_total,
        grad_cross_heads,
        cross_delta,
        cross_live,
        False,
    )
    grad_memory_keys, grad_memory_values = (
        lax.psum_scatter(
            memory_key_terms.astype(jnp.bfloat16), "ctx", scatter_dimension=0, tiled=True
        ).astype(jnp.float32),
        lax.psum_scatter(
            memory_value_terms.astype(jnp.bfloat16), "ctx", scatter_dimension=0, tiled=True
        ).astype(jnp.float32),
    )
    grad_memory_pair = jnp.concatenate(
        [grad_memory_keys.astype(bf16), grad_memory_values.astype(bf16)], axis=1
    )
    grad_cross_value_bias = jnp.sum(grad_memory_pair[:, width:].astype(f32), axis=0)
    grad_cross_memory = jnp.dot(memory_rows.T, grad_memory_pair, preferred_element_type=f32)
    memory_grad = jnp.dot(grad_memory_pair, cross_memory_full.T, preferred_element_type=f32)[None]
    grad_cross_low_queries = grad_cross_queries.astype(bf16)
    grad_cross_query_bias = jnp.sum(grad_cross_low_queries.astype(f32), axis=0)
    grad_cross_query = jnp.dot(hidden_low.T, grad_cross_low_queries, preferred_element_type=f32)
    grad_hidden_one = residual_scale * grad_second + jnp.dot(
        grad_cross_low_queries, cross_query_full.T, preferred_element_type=f32
    )
    grad_first, grad_first_gain, grad_first_shift = layer_norm_back(
        grad_hidden_one, gain_one, normed_one, inverse_one
    )
    grad_branch = grad_first.astype(bf16)
    grad_self_output_bias = jnp.sum(grad_branch.astype(f32), axis=0)
    grad_self_output = jnp.dot(attended_low.T, grad_branch, preferred_element_type=f32)
    grad_attended = jnp.dot(grad_branch, self_out_full.T, preferred_element_type=f32).astype(bf16)
    grad_attended_heads = head_split(grad_attended)
    self_delta = jnp.sum(grad_attended_heads.astype(f32) * attended, axis=-1).T
    grad_queries, key_terms, value_terms = attend_backward(
        query_heads,
        key_heads,
        value_heads,
        self_total,
        grad_attended_heads,
        self_delta,
        self_live,
        True,
    )
    grad_keys, grad_values = (
        lax.psum_scatter(
            key_terms.astype(jnp.bfloat16), "ctx", scatter_dimension=0, tiled=True
        ).astype(jnp.float32),
        lax.psum_scatter(
            value_terms.astype(jnp.bfloat16), "ctx", scatter_dimension=0, tiled=True
        ).astype(jnp.float32),
    )
    grad_projected = jnp.concatenate(
        [grad_queries.astype(bf16), grad_keys.astype(bf16), grad_values.astype(bf16)], axis=1
    )
    grad_self_query_bias = jnp.sum(grad_projected[:, :width].astype(f32), axis=0)
    grad_self_value_bias = jnp.sum(grad_projected[:, 2 * width :].astype(f32), axis=0)
    grad_self_projection = jnp.dot(rows_in.T, grad_projected, preferred_element_type=f32)
    token_grad = (
        residual_scale * grad_first
        + jnp.dot(grad_projected, projection_full.T, preferred_element_type=f32)
    )[None]
    shares = (
        lax.psum_scatter(
            grad_self_projection.astype(jnp.bfloat16), "fsdp", scatter_dimension=0, tiled=True
        ).astype(jnp.float32),
        lax.psum_scatter(
            grad_self_output.astype(jnp.bfloat16), "fsdp", scatter_dimension=0, tiled=True
        ).astype(jnp.float32),
        lax.psum_scatter(
            grad_self_query_bias.astype(jnp.bfloat16), "fsdp", scatter_dimension=0, tiled=True
        ).astype(jnp.float32),
        lax.psum_scatter(
            grad_self_value_bias.astype(jnp.bfloat16), "fsdp", scatter_dimension=0, tiled=True
        ).astype(jnp.float32),
        lax.psum_scatter(
            grad_self_output_bias.astype(jnp.bfloat16), "fsdp", scatter_dimension=0, tiled=True
        ).astype(jnp.float32),
        lax.psum_scatter(
            grad_first_gain.astype(jnp.bfloat16), "fsdp", scatter_dimension=0, tiled=True
        ).astype(jnp.float32),
        lax.psum_scatter(
            grad_first_shift.astype(jnp.bfloat16), "fsdp", scatter_dimension=0, tiled=True
        ).astype(jnp.float32),
        lax.psum_scatter(
            grad_cross_query.astype(jnp.bfloat16), "fsdp", scatter_dimension=0, tiled=True
        ).astype(jnp.float32),
        lax.psum_scatter(
            grad_cross_memory.astype(jnp.bfloat16), "fsdp", scatter_dimension=0, tiled=True
        ).astype(jnp.float32),
        lax.psum_scatter(
            grad_cross_output.astype(jnp.bfloat16), "fsdp", scatter_dimension=0, tiled=True
        ).astype(jnp.float32),
        lax.psum_scatter(
            grad_cross_query_bias.astype(jnp.bfloat16), "fsdp", scatter_dimension=0, tiled=True
        ).astype(jnp.float32),
        lax.psum_scatter(
            grad_cross_value_bias.astype(jnp.bfloat16), "fsdp", scatter_dimension=0, tiled=True
        ).astype(jnp.float32),
        lax.psum_scatter(
            grad_cross_output_bias.astype(jnp.bfloat16), "fsdp", scatter_dimension=0, tiled=True
        ).astype(jnp.float32),
        lax.psum_scatter(
            grad_second_gain.astype(jnp.bfloat16), "fsdp", scatter_dimension=0, tiled=True
        ).astype(jnp.float32),
        lax.psum_scatter(
            grad_second_shift.astype(jnp.bfloat16), "fsdp", scatter_dimension=0, tiled=True
        ).astype(jnp.float32),
        lax.psum_scatter(
            grad_expand_weight.astype(jnp.bfloat16), "fsdp", scatter_dimension=0, tiled=True
        ).astype(jnp.float32),
        lax.psum_scatter(
            grad_reduce_weight.astype(jnp.bfloat16), "fsdp", scatter_dimension=0, tiled=True
        ).astype(jnp.float32),
        lax.psum_scatter(
            grad_expand_bias.astype(jnp.bfloat16), "fsdp", scatter_dimension=0, tiled=True
        ).astype(jnp.float32),
        lax.psum_scatter(
            grad_reduce_bias.astype(jnp.bfloat16), "fsdp", scatter_dimension=0, tiled=True
        ).astype(jnp.float32),
        lax.psum_scatter(
            grad_third_gain.astype(jnp.bfloat16), "fsdp", scatter_dimension=0, tiled=True
        ).astype(jnp.float32),
        lax.psum_scatter(
            grad_third_shift.astype(jnp.bfloat16), "fsdp", scatter_dimension=0, tiled=True
        ).astype(jnp.float32),
    )
    summed = (
        lax.psum(shares[0].astype(jnp.bfloat16), "ctx").astype(jnp.float32),
        lax.psum(shares[1].astype(jnp.bfloat16), "ctx").astype(jnp.float32),
        lax.psum(shares[2].astype(jnp.bfloat16), "ctx").astype(jnp.float32),
        lax.psum(shares[3].astype(jnp.bfloat16), "ctx").astype(jnp.float32),
        lax.psum(shares[4].astype(jnp.bfloat16), "ctx").astype(jnp.float32),
        lax.psum(shares[5].astype(jnp.bfloat16), "ctx").astype(jnp.float32),
        lax.psum(shares[6].astype(jnp.bfloat16), "ctx").astype(jnp.float32),
        lax.psum(shares[7].astype(jnp.bfloat16), "ctx").astype(jnp.float32),
        lax.psum(shares[8].astype(jnp.bfloat16), "ctx").astype(jnp.float32),
        lax.psum(shares[9].astype(jnp.bfloat16), "ctx").astype(jnp.float32),
        lax.psum(shares[10].astype(jnp.bfloat16), "ctx").astype(jnp.float32),
        lax.psum(shares[11].astype(jnp.bfloat16), "ctx").astype(jnp.float32),
        lax.psum(shares[12].astype(jnp.bfloat16), "ctx").astype(jnp.float32),
        lax.psum(shares[13].astype(jnp.bfloat16), "ctx").astype(jnp.float32),
        lax.psum(shares[14].astype(jnp.bfloat16), "ctx").astype(jnp.float32),
        lax.psum(shares[15].astype(jnp.bfloat16), "ctx").astype(jnp.float32),
        lax.psum(shares[16].astype(jnp.bfloat16), "ctx").astype(jnp.float32),
        lax.psum(shares[17].astype(jnp.bfloat16), "ctx").astype(jnp.float32),
        lax.psum(shares[18].astype(jnp.bfloat16), "ctx").astype(jnp.float32),
        lax.psum(shares[19].astype(jnp.bfloat16), "ctx").astype(jnp.float32),
        lax.psum(shares[20].astype(jnp.bfloat16), "ctx").astype(jnp.float32),
    )
    return (
        output,
        token_grad,
        memory_grad,
        summed[0],
        summed[1],
        summed[2],
        summed[3],
        summed[4],
        summed[5],
        summed[6],
        summed[7],
        summed[8],
        summed[9],
        summed[10],
        summed[11],
        summed[12],
        summed[13],
        summed[14],
        summed[15],
        summed[16],
        summed[17],
        summed[18],
        summed[19],
        summed[20],
    )


def solution(mesh):
    placed = (
        P("fsdp", "ctx", None),
        P("fsdp", "ctx", None),
        P("fsdp", "ctx", None),
        P("fsdp", None, None),
        P("fsdp", None),
        P("fsdp", None),
        P("fsdp", None),
        P("fsdp"),
        P("fsdp"),
        P("fsdp"),
        P("fsdp"),
        P("fsdp"),
        P("fsdp", None),
        P("fsdp", None),
        P("fsdp", None),
        P("fsdp"),
        P("fsdp"),
        P("fsdp"),
        P("fsdp"),
        P("fsdp"),
        P("fsdp", None),
        P("fsdp", None),
        P("fsdp"),
        P("fsdp"),
        P("fsdp"),
        P("fsdp"),
    )
    sizes = (mesh.shape["ctx"], mesh.shape["fsdp"])
    return jax.shard_map(
        tiled_shards if sizes == (4, 8) else plain_shards,
        mesh=mesh,
        in_specs=placed,
        out_specs=(
            P("fsdp", "ctx", None),
            P("fsdp", "ctx", None),
            P("fsdp", "ctx", None),
            P("fsdp", None),
            P("fsdp", None),
            P("fsdp"),
            P("fsdp"),
            P("fsdp"),
            P("fsdp"),
            P("fsdp"),
            P("fsdp", None),
            P("fsdp", None),
            P("fsdp", None),
            P("fsdp"),
            P("fsdp"),
            P("fsdp"),
            P("fsdp"),
            P("fsdp"),
            P("fsdp", None),
            P("fsdp", None),
            P("fsdp"),
            P("fsdp"),
            P("fsdp"),
            P("fsdp"),
        ),
        check_vma=False,
    )
```
